32 devices in a mesh: ctx: 8 (over z, y), head: 4 (over x, core).
Axes of the slice: x: 2, y: 2, z: 4, core: 2. Of those that a mesh axis runs over, the one named last changes fastest.
Arguments:
- x_in: bfloat16 [4096, 8192], P('ctx', 'head'), may hold values from -6 to 6
- z_in: bfloat16 [4096, 8192], P('ctx', 'head'), may hold values from -6 to 6
- bc_in: bfloat16 [4096, 256], P('ctx', 'head'), may hold values from -6 to 6
- dt: float32 [4096, 128], P('ctx', 'head'), may hold values from 4.8828125e-05 to 0.25146484, as said below
- decay_scale: float32 [128], P('head'), may hold values from 0.5 to 2
- conv_x: bfloat16 [4, 8192], P(None, 'head'), may hold values from -3 to 3
- conv_bc: bfloat16 [4, 256], P(None, 'head'), may hold values from -3 to 3
- norm_gain: bfloat16 [8192], P('head'), may hold values from 0.25 to 1.75
- doc_start: int32 [4096], P('ctx'), may hold values from 0 to 1, as said below
Outputs:
- out: bfloat16 [4096, 8192], P('ctx', 'head')
The draws below stay inside these ranges and needn't reach their ends.
Inputs may be any that keep to these rules, and one draw needn't show every extreme that they name: doc_start[0] = 0; going round the loop, two consecutive ones are at most 512 apart; the document that holds position 0 is exactly 512 long and begins 3 (4 - 1) or more positions before the end. `dt`: positive step sizes.
All inputs are finite; a program needn't handle non-finite values.
Results may differ from the reference program's by a relative error of at most 0.0034.
Values may be sent and summed in bfloat16 or wider, within the bound.
No kernel may reach another device: no remote copies, remote signals or barrier semaphores. Data moves between devices by JAX's collectives and lax.ppermute only.
A program may use at most 64 MiB of HBM per device.

```python
import math
import jax
import jax.numpy as jnp
from jax import lax

HEADS = 128
HDIM = 64
DSTATE = 128
BLOCK = 256
CONV = 4
DINNER = 8192
PACKED_LENGTH = 4096
LONGEST_DOC = 512


def draw_doc_start(key, part):
    gaps = jax.random.randint(key, (PACKED_LENGTH,), 1, LONGEST_DOC + 1).astype(jnp.int32)
    gaps = gaps.at[0].set(LONGEST_DOC)
    ends = jnp.cumsum(gaps).astype(jnp.int32)
    starts = jnp.concatenate([jnp.zeros((1,), jnp.int32), ends[:-1]])
    places = jnp.where(starts < PACKED_LENGTH, starts, PACKED_LENGTH)
    linear = jnp.zeros((PACKED_LENGTH,), jnp.int32).at[places].set(1, mode='drop')
    offset = jax.random.randint(jax.random.fold_in(key, 5), (), CONV - 1, LONGEST_DOC).astype(jnp.int32)
    return jnp.roll(linear, -offset, axis=0)


def draw_dt(key, part):
    variety_key, gradual_key, quick_key, jagged_key, spike_key = jax.random.split(jax.random.fold_in(key, 17), 5)
    share = 0.5
    gradual_draw = jax.random.uniform(variety_key, (HEADS,)) < share
    gradual_baseline = jnp.exp(jax.random.uniform(gradual_key, (HEADS,), jnp.float32, jnp.log(0.05), jnp.log(0.5))) / LONGEST_DOC
    quick_baseline = jnp.exp(jax.random.uniform(quick_key, (HEADS,), jnp.float32, jnp.log(0.02), jnp.log(0.06)))
    jagged_draw = jax.random.uniform(jagged_key, (PACKED_LENGTH, HEADS), jnp.float32, 0.5, 1.5)
    spike_draw = jnp.where(jax.random.uniform(spike_key, (PACKED_LENGTH, 1)) < 2.0 / LONGEST_DOC, 0.25, 0.0)
    value_entry = jnp.where(gradual_draw[None, :], gradual_baseline[None, :] * jagged_draw + spike_draw, quick_baseline[None, :] * jagged_draw)
    return value_entry.astype(jnp.float32)


def block_scale(key, dims, pieces, least, top_value):
    factor_of, own = 1.0, jax.random.fold_in(key, 6)
    for axis_at, parts in pieces:
        heights = jnp.exp(jax.random.uniform(jax.random.fold_in(own, axis_at), (parts,), jnp.float32, least / len(pieces), top_value / len(pieces)))
        factor_of = factor_of * jnp.repeat(heights, dims[axis_at] // parts).reshape([-1 if axis == axis_at else 1 for axis in range(len(dims))])
    return factor_of


def scatter_about(rng, dims, scale, reach, cuts=(), kind=jnp.bfloat16):
    drawn = jax.random.normal(rng, dims, jnp.float32) * scale
    if len(cuts) > 0:
        drawn = block_scale(rng, dims, cuts, -0.22, 0.18) * drawn
    return jnp.clip(drawn, min=-reach, max=reach).astype(kind)


def setup_inputs(seed: int = 0) -> dict:
    keys = jax.random.split(jax.random.key(seed), 10)
    x_in = scatter_about(keys[0], (PACKED_LENGTH, DINNER), 1.0, 6.0, ((0, 8), (1, 4)))
    z_in = scatter_about(keys[1], (PACKED_LENGTH, DINNER), 1.0, 6.0, ((0, 8), (1, 4)))
    bc_in = scatter_about(keys[2], (PACKED_LENGTH, 2 * DSTATE), 1.0, 6.0, ((0, 8), (1, 4)))
    dt = draw_dt(jax.random.fold_in(keys[9], 71), 0)
    decay_scale = jnp.clip(jnp.exp(math.log(2.0) - 1.3862944 * jax.random.uniform(keys[4], (HEADS,), jnp.float32) ** block_scale(keys[4], (HEADS,), ((0, 4),), -0.2, 0.2)), 0.5, 2.0)
    conv_x = scatter_about(keys[5], (CONV, DINNER), CONV ** -0.5, 3.0, ((1, 4),))
    conv_bc = scatter_about(keys[6], (CONV, 2 * DSTATE), CONV ** -0.5, 3.0, ((1, 4),))
    norm_gain = jnp.clip(1.0 + 0.15 * jax.random.normal(keys[7], (DINNER,), jnp.float32), 0.25, 1.75).astype(jnp.bfloat16)
    doc_start = draw_doc_start(jax.random.fold_in(keys[9], 71), 0)
    return {"x_in": x_in, "z_in": z_in, "bc_in": bc_in, "dt": dt, "decay_scale": decay_scale, "conv_x": conv_x, "conv_bc": conv_bc, "norm_gain": norm_gain, "doc_start": doc_start}


def causal_conv(padded, taps, same):
    rows = same.shape[1]
    total = jnp.zeros((rows, taps.shape[1]), jnp.float32)
    for offset in range(taps.shape[0]):
        piece = padded[offset:offset + rows].astype(jnp.float32) * taps[offset].astype(jnp.float32)
        total = total + jnp.where(same[offset][:, None], piece, 0.0)
    return jax.nn.silu(total)

def block_pass(state, values, bmat, cmat, steps, scale, doc_ids, doc_before):
    high = lax.Precision.HIGHEST
    log_decay = jnp.cumsum(-steps * scale[None, :], axis=0)
    scores = jnp.dot(cmat, bmat.T, precision=high)
    rows = doc_ids.shape[0]
    lower = jnp.arange(rows)[:, None] >= jnp.arange(rows)[None, :]
    keep = lower & (doc_ids[:, None] == doc_ids[None, :])
    decay_t = log_decay.T
    spread = decay_t[:, :, None] - decay_t[:, None, :]
    weights = jnp.where(keep[None, :, :], jnp.exp(jnp.minimum(spread, 0.0)), 0.0) * scores[None, :, :]
    output = jnp.einsum('hts,shp->thp', weights, values, precision=high)
    live = doc_ids == doc_before
    carried = jnp.einsum('tn,hpn->thp', cmat, state, precision=high)
    output = output + jnp.where(live[:, None, None], jnp.exp(log_decay)[:, :, None] * carried, 0.0)
    tail = doc_ids == doc_ids[-1]
    to_end = jnp.where(tail[:, None], jnp.exp(log_decay[-1][None, :] - log_decay), 0.0)
    fresh = jnp.einsum('sh,shp,sn->hpn', to_end, values, bmat, precision=high)
    keep_state = jnp.where(doc_ids[-1] == doc_before, jnp.exp(log_decay[-1]), 0.0)
    return (keep_state[:, None, None] * state + fresh, output)

def gated_norm(output, gate, gain):
    rows, heads, width = output.shape
    mixed = output * jax.nn.silu(gate.astype(jnp.float32)).reshape(rows, heads, width)
    factor = lax.rsqrt(lax.optimization_barrier(jnp.mean(mixed * mixed, axis=-1, keepdims=True)) + 1e-05)
    normed = mixed * factor * gain.astype(jnp.float32).reshape(heads, width)
    return normed.reshape(rows, heads * width).astype(jnp.bfloat16)

def reference(x_in, z_in, bc_in, dt, decay_scale, conv_x, conv_bc, norm_gain, doc_start):
    first = jnp.argmax(doc_start).astype(jnp.int32)
    x_in = jnp.roll(x_in, -first, axis=0)
    z_in = jnp.roll(z_in, -first, axis=0)
    bc_in = jnp.roll(bc_in, -first, axis=0)
    dt = jnp.roll(dt, -first, axis=0)
    rolled_start = jnp.roll(doc_start, -first, axis=0)
    doc_ids = jnp.cumsum(rolled_start).astype(jnp.int32)
    lead = CONV - 1
    x_pad = jnp.concatenate([jnp.zeros((lead, DINNER), jnp.bfloat16), x_in], axis=0)
    bc_pad = jnp.concatenate([jnp.zeros((lead, 2 * DSTATE), jnp.bfloat16), bc_in], axis=0)
    ids_pad = jnp.concatenate([jnp.full((lead,), -1, jnp.int32), doc_ids], axis=0)

    def block_turn(state, index):
        start = (index * BLOCK).astype(jnp.int32)
        x_part = lax.dynamic_slice_in_dim(x_pad, start, BLOCK + lead, 0)
        bc_part = lax.dynamic_slice_in_dim(bc_pad, start, BLOCK + lead, 0)
        ids_part = lax.dynamic_slice_in_dim(ids_pad, start, BLOCK + lead, 0)
        own_ids = ids_part[lead:]
        same = jnp.stack([ids_part[offset:offset + BLOCK] == own_ids for offset in range(CONV)])
        x_conv = causal_conv(x_part, conv_x, same)
        bc_conv = lax.optimization_barrier(causal_conv(bc_part, conv_bc, same).astype(jnp.bfloat16))
        bc_wide = bc_conv.astype(jnp.float32)
        steps = lax.dynamic_slice_in_dim(dt, start, BLOCK, 0)
        values = x_conv.reshape(BLOCK, HEADS, HDIM)
        new_state, output = block_pass(state, values, bc_wide[:, :DSTATE], bc_wide[:, DSTATE:], steps, decay_scale, own_ids, ids_part[lead - 1])
        gate = lax.dynamic_slice_in_dim(z_in, start, BLOCK, 0)
        return (new_state, gated_norm(output, gate, norm_gain))
    _, outputs = lax.scan(block_turn, jnp.zeros((HEADS, HDIM, DSTATE), jnp.float32), jnp.arange(PACKED_LENGTH // BLOCK).astype(jnp.int32))
    return jnp.roll(outputs.reshape(PACKED_LENGTH, DINNER), first, axis=0)
```

```python
import functools

import jax
import jax.numpy as jnp
from jax import lax
from jax.experimental import pallas as pl
from jax.experimental.pallas import tpu as pltpu
from jax.sharding import PartitionSpec as P

HDIM = 64
DSTATE = 128
CONV = 4
CHUNK = 256
WIDE = 256
GROUPS = 2
F32 = jnp.float32
BF16 = jnp.bfloat16


def shifted(value, axis, steps):
    count = lax.axis_size(axis)
    pairs = [(source, (source + steps) % count) for source in range(count)]
    return lax.ppermute(value, axis, pairs)


def crossed(value, axis, mask):
    count = lax.axis_size(axis)
    return lax.ppermute(value, axis, [(source, source ^ mask) for source in range(count)])


def iota(shape, dim):
    return lax.broadcasted_iota(jnp.int32, shape, dim)


def mm(a, b):
    return jnp.dot(a, b, preferred_element_type=F32)


def parts(value, count):
    pieces = []
    for _ in range(count):
        piece = value.astype(BF16)
        pieces.append(piece)
        value = value - piece.astype(F32)
    return jnp.concatenate(pieces, axis=1)


def spread_matrix(copies, heads, low, width):
    shape = (copies * heads, width)
    head = lax.rem(iota(shape, 0), heads)
    return jnp.where(head == (iota(shape, 1) + low) // HDIM, 1.0, 0.0).astype(BF16)


def vmem_call(kernel, outs, scratch=(), limit=24):
    spec = pl.BlockSpec(memory_space=pltpu.VMEM)
    many = isinstance(outs, (list, tuple))
    return pl.pallas_call(
        kernel,
        out_shape=outs,
        out_specs=[spec] * len(outs) if many else spec,
        scratch_shapes=list(scratch),
        compiler_params=pltpu.CompilerParams(vmem_limit_bytes=limit << 20),
    )


def tail_kernel(start_ref, x_ref, bc_ref, out_ref):
    rows = start_ref.shape[1]
    last = start_ref[0, rows - 1]
    before = start_ref[0, rows - 2]
    width = x_ref.shape[1]

    def masked(value):
        row = iota(value.shape, 0)
        low = jnp.where(last == 1, 7, jnp.where(before == 1, 6, 5))
        return jnp.where(row >= low, value.astype(F32), 0.0).astype(BF16)

    out_ref[:, :width] = masked(x_ref[...])
    bc = masked(bc_ref[...])
    out_ref[:, width:] = jnp.concatenate([bc] * (128 // bc.shape[1]), axis=1)


def prep_kernel(dt_ref, scale_ref, start_ref, fac_ref, eps_ref, rows_ref, idc_ref, idr_ref):
    heads = dt_ref.shape[1]
    square = (CHUNK, CHUNK)
    lower = jnp.where(iota(square, 0) >= iota(square, 1), 1.0, 0.0).astype(BF16)
    upper = jnp.where(iota(square, 0) <= iota(square, 1), 1.0, 0.0).astype(BF16)
    mids = []
    offset = jnp.zeros((8, 1), F32)
    for j in range(2):
        span = slice(j * CHUNK, (j + 1) * CHUNK)
        steps = parts(-dt_ref[span, :] * scale_ref[...], 3)
        sums = mm(lower, steps)
        log_decay = sums[:, :heads] + sums[:, heads : 2 * heads] + sums[:, 2 * heads :]
        mid = 0.5 * log_decay[CHUNK - 1 : CHUNK, :]
        mids.append(mid)
        fac_ref[span, :] = parts(jnp.exp(mid - log_decay), 2)
        eps_ref[span, :] = parts(jnp.exp(log_decay - mid), 2)
        starts = start_ref[:, span].astype(F32).astype(BF16)
        by_row = mm(jnp.broadcast_to(starts, (8, CHUNK)), upper) + offset
        by_col = lax.dot_general(
            lower,
            jnp.broadcast_to(starts, (128, CHUNK)),
            (((1,), (1,)), ((), ())),
            preferred_element_type=F32,
        )
        idr_ref[:, span] = by_row
        idc_ref[span, :] = by_col + offset[:1, :]
        offset = by_row[:, CHUNK - 1 : CHUNK]
    middle = idr_ref[:1, CHUNK - 1 : CHUNK]
    final = idr_ref[:1, 2 * CHUNK - 1 : 2 * CHUNK]
    keep = jnp.where(middle == final, 1.0, 0.0)
    whole = jnp.where(final == 0.0, 1.0, 0.0)
    first, second = mids
    table = jnp.concatenate(
        [
            jnp.exp(first + second),
            jnp.exp(first + 2.0 * second) * keep,
            jnp.exp(second),
            jnp.exp(first),
            jnp.exp(2.0 * first + second),
            jnp.exp(2.0 * (first + second)) * whole,
            first,
            second,
        ],
        axis=0,
    )
    rows_ref[...] = mm(parts(table, 3), spread_matrix(3, heads, 0, rows_ref.shape[1]))


def bc_kernel(bc_ref, tail_ref, taps_ref, idc_ref, out_ref, pad_ref, ids_ref):
    rows, width = bc_ref.shape
    low = tail_ref.shape[1] - 128
    pad_ref[:8, :] = tail_ref[:, low : low + width].astype(F32)
    pad_ref[8:, :] = bc_ref[...].astype(F32)
    ids_ref[:8, :] = jnp.zeros((8, 128), F32)
    ids_ref[8:, :] = idc_ref[...]
    ids = idc_ref[:, :width]
    taps = taps_ref[...].astype(F32)
    total = pad_ref[8:, :] * taps[CONV - 1 : CONV, :]
    for back in range(1, CONV):
        same = ids_ref[pl.ds(8 - back, rows), :width] == ids
        piece = pad_ref[pl.ds(8 - back, rows), :] * taps[CONV - 1 - back : CONV - back, :]
        total = total + jnp.where(same, piece, 0.0)
    value = total / (1.0 + jnp.exp(-total))
    out_ref[...] = value.T.astype(BF16)


def conv_kernel(x_ref, tail_ref, taps_ref, fac_ref, idc_ref, out_ref, pad_ref, ids_ref, mask_ref):
    rows, columns = x_ref.shape
    heads = fac_ref.shape[1] // 2
    ids_ref[:8, :] = jnp.zeros((8, 128), F32)
    ids_ref[8:, :] = idc_ref[...]
    for back in range(1, CONV):
        same = ids_ref[pl.ds(8 - back, rows), :] == idc_ref[...]
        mask_ref[back - 1] = jnp.where(same, 1.0, 0.0)

    def column_block(block, _):
        low = pl.multiple_of(block * WIDE, WIDE)
        cols = pl.ds(low, WIDE)
        spread = spread_matrix(2, heads, low, WIDE)
        taps = 0.5 * taps_ref[:, cols].astype(F32)
        pad_ref[:8, :] = tail_ref[:, cols].astype(F32)
        pad_ref[8:, :] = x_ref[:, cols].astype(F32)
        size = 128
        for low_row in range(0, rows, size):
            span = slice(low_row, low_row + size)
            half = pad_ref[pl.ds(8 + low_row, size), :] * taps[CONV - 1 : CONV, :]
            for back in range(1, CONV):
                mask = mask_ref[back - 1, span, :]
                mask = jnp.concatenate([mask] * (WIDE // 128), axis=1)
                piece = pad_ref[pl.ds(8 + low_row - back, size), :] * mask
                half = half + piece * taps[CONV - 1 - back : CONV - back, :]
            value = half + half * jnp.tanh(half)
            out_ref[span, cols] = (value * mm(fac_ref[span, :], spread)).astype(BF16)
        return 0

    lax.fori_loop(0, columns // WIDE, column_block, 0)


def pick(flag, refs):
    half = len(refs) // 2
    near = jnp.concatenate([ref[...] for ref in refs[:half]], axis=0).astype(F32)
    far = jnp.concatenate([ref[...] for ref in refs[half:]], axis=0).astype(F32)
    first = flag == 1
    return jnp.where(first, near, far), jnp.where(first, far, near)


def state_kernel(split, flag_ref, *refs):
    b_rows, _ = pick(flag_ref[0, 0], refs[:split])
    xs_ref, rows_ref, idr_ref, mid_ref, *outs = refs[split:]
    groups = len(outs)
    group_width = outs[0].shape[1]
    pieces = []
    for j in range(2):
        span = slice(j * CHUNK, (j + 1) * CHUNK)
        ids = idr_ref[:1, span]
        end = idr_ref[:1, (j + 1) * CHUNK - 1 : (j + 1) * CHUNK]
        pieces.append(jnp.where(ids == end, b_rows[:, span], 0.0).astype(BF16))
    for group in range(groups):

        def column_block(block, _):
            low = pl.multiple_of(group * group_width + block * WIDE, WIDE)
            cols = pl.ds(low, WIDE)
            first = mm(pieces[0], xs_ref[:CHUNK, cols])
            second = mm(pieces[1], xs_ref[CHUNK:, cols])
            mid_ref[:, cols] = (first * rows_ref[0:1, cols]).astype(BF16)
            end = first * rows_ref[1:2, cols] + second * rows_ref[2:3, cols]
            here = pl.ds(pl.multiple_of(block * WIDE, WIDE), WIDE)
            outs[group][:, here] = end.astype(outs[group].dtype)
            return 0

        lax.fori_loop(0, group_width // WIDE, column_block, 0)


def local_kernel(split, flag_ref, *refs):
    b_rows, c_rows = pick(flag_ref[0, 0], refs[:split])
    xs_ref, mid_ref, idc_ref, idr_ref, y_ref, live_ref, g_ref = refs[split:]
    columns = xs_ref.shape[1]
    b_rows = b_rows.astype(BF16)
    c_cols = c_rows.T
    for j in range(2):
        span = slice(j * CHUNK, (j + 1) * CHUNK)
        ids = idc_ref[span, :]
        live_ref[span, :] = jnp.where(ids == 0.0, c_cols[span, :], 0.0).astype(BF16)
        scores = mm(c_cols[span, :].astype(BF16), b_rows[:, span])
        square = (CHUNK, CHUNK)
        wide = jnp.concatenate([ids] * (CHUNK // 128), axis=1)
        keep = (iota(square, 0) >= iota(square, 1)) & (wide == idr_ref[:1, span])
        g_ref[j] = jnp.where(keep, scores, 0.0).astype(BF16)
    ids = idc_ref[CHUNK:, :]
    before = idr_ref[:1, CHUNK - 1 : CHUNK]
    carried = jnp.where(ids == before, c_cols[CHUNK:, :], 0.0).astype(BF16)

    def column_block(block, _):
        cols = pl.ds(pl.multiple_of(block * WIDE, WIDE), WIDE)
        y_ref[:CHUNK, cols] = mm(g_ref[0], xs_ref[:CHUNK, cols])
        y_ref[CHUNK:, cols] = mm(g_ref[1], xs_ref[CHUNK:, cols]) + mm(carried, mid_ref[:, cols])
        return 0

    lax.fori_loop(0, columns // WIDE, column_block, 0)


def final_kernel(group, width, *refs):
    state_ref, y_ref, live_ref, eps_ref, rows_ref, z_ref, gain_ref = refs[:7]
    out_ref = refs[-1]
    heads = eps_ref.shape[1] // 2
    square = (WIDE, WIDE)
    mean_matrix = jnp.where(
        iota(square, 0) // HDIM == iota(square, 1) // HDIM, 1.0 / HDIM, 0.0
    ).astype(BF16)

    def column_block(block, _):
        here = pl.ds(pl.multiple_of(block * WIDE, WIDE), WIDE)
        low = pl.multiple_of(group * width + block * WIDE, WIDE)
        cols = pl.ds(low, WIDE)
        spread = spread_matrix(2, heads, low, WIDE)
        gain = gain_ref[:, cols].astype(F32)
        state = state_ref[:, here]
        size = 128
        for low_row in range(0, y_ref.shape[0], size):
            span = slice(low_row, low_row + size)
            scale = rows_ref[3:4, cols] if low_row < CHUNK else rows_ref[4:5, cols]
            total = y_ref[span, cols] + mm(live_ref[span, :], state) * scale
            half = 0.5 * z_ref[span, cols].astype(F32)
            gate = half + half * jnp.tanh(half)
            mixed = total * mm(eps_ref[span, :], spread) * gate
            mean = mm((mixed * mixed).astype(BF16), mean_matrix)
            out_ref[span, cols] = (mixed * lax.rsqrt(mean + 1e-05) * gain).astype(BF16)
        return 0

    lax.fori_loop(0, width // WIDE, column_block, 0)


def on_device(x_in, z_in, bc_in, dt, decay_scale, conv_x, conv_bc, norm_gain, doc_start):
    rows, columns = x_in.shape
    heads = dt.shape[1]
    bc_width = bc_in.shape[1]
    turns = lax.axis_size("ctx") // 8
    starts = doc_start.reshape(1, rows)
    whole = lambda *_: (0, 0)
    tail = pl.pallas_call(
        tail_kernel,
        grid=(1,),
        in_specs=[
            pl.BlockSpec((1, rows), whole, memory_space=pltpu.SMEM),
            pl.BlockSpec((8, columns), lambda i: (rows // 8 - 1, 0)),
            pl.BlockSpec((8, bc_width), lambda i: (rows // 8 - 1, 0)),
        ],
        out_specs=pl.BlockSpec((8, columns + 128), whole),
        out_shape=jax.ShapeDtypeStruct((8, columns + 128), BF16),
        compiler_params=pltpu.CompilerParams(vmem_limit_bytes=4 << 20),
    )(starts, x_in, bc_in)
    rim = shifted(tail, "ctx", 1)
    fac, eps, row_table, ids_col, ids_row = vmem_call(
        prep_kernel,
        [
            jax.ShapeDtypeStruct((rows, 2 * heads), BF16),
            jax.ShapeDtypeStruct((rows, 2 * heads), BF16),
            jax.ShapeDtypeStruct((8, columns), F32),
            jax.ShapeDtypeStruct((rows, 128), F32),
            jax.ShapeDtypeStruct((8, rows), F32),
        ],
    )(dt, decay_scale.reshape(1, heads), starts)
    own = vmem_call(
        bc_kernel,
        jax.ShapeDtypeStruct((bc_width, rows), BF16),
        [pltpu.VMEM((rows + 8, bc_width), F32), pltpu.VMEM((rows + 8, 128), F32)],
    )(bc_in, rim, conv_bc, ids_col)
    split = lax.axis_size("head")
    shares = [own] + [crossed(own, "head", mask) for mask in range(1, split)]
    values = vmem_call(
        conv_kernel,
        jax.ShapeDtypeStruct((rows, columns), BF16),
        [
            pltpu.VMEM((rows + 8, WIDE), F32),
            pltpu.VMEM((rows + 8, 128), F32),
            pltpu.VMEM((CONV - 1, rows, 128), F32),
        ],
    )(x_in, rim, conv_x, fac, ids_col)
    flag = (lax.axis_index("head") < split // 2).astype(jnp.int32).reshape(1, 1)
    spec = pl.BlockSpec(memory_space=pltpu.VMEM)
    smem = pl.BlockSpec(memory_space=pltpu.SMEM)
    width = columns // GROUPS
    state_type = BF16 if turns == 1 else F32
    out_shapes = [jax.ShapeDtypeStruct((DSTATE, columns), BF16)]
    out_shapes += [jax.ShapeDtypeStruct((DSTATE, width), state_type)] * GROUPS
    middle, *ends = pl.pallas_call(
        functools.partial(state_kernel, split),
        out_shape=out_shapes,
        in_specs=[smem] + [spec] * (split + 3),
        out_specs=[spec] * (1 + GROUPS),
        compiler_params=pltpu.CompilerParams(vmem_limit_bytes=16 << 20),
    )(flag, *shares, values, row_table, ids_row)

    def relay(group, end):
        if turns == 1:
            return shifted(end, "ctx", 1)
        through = row_table[5:6, group * width : (group + 1) * width]
        turn = lambda _, incoming: shifted(through * incoming + end, "ctx", 1)
        return lax.fori_loop(0, turns, turn, jnp.zeros_like(end)).astype(BF16)

    incoming = [relay(group, end) for group, end in enumerate(ends)]
    local, live = pl.pallas_call(
        functools.partial(local_kernel, split),
        out_shape=[
            jax.ShapeDtypeStruct((rows, columns), F32),
            jax.ShapeDtypeStruct((rows, DSTATE), BF16),
        ],
        in_specs=[smem] + [spec] * (split + 4),
        out_specs=[spec] * 2,
        scratch_shapes=[pltpu.VMEM((2, CHUNK, CHUNK), BF16)],
        compiler_params=pltpu.CompilerParams(vmem_limit_bytes=16 << 20),
    )(flag, *shares, values, middle, ids_col, ids_row)
    gain = norm_gain.reshape(1, columns)
    outs = []
    for group in range(GROUPS):
        kernel = lambda *refs, g=group: final_kernel(g, width, *refs)
        args = [incoming[group], local, live, eps, row_table, z_in, gain]
        in_specs = [spec] * 7
        alias = {}
        if group > 0:
            args.append(out)
            in_specs.append(pl.BlockSpec(memory_space=pl.ANY))
            alias = {7: 0}
        out = pl.pallas_call(
            kernel,
            out_shape=jax.ShapeDtypeStruct((rows, columns), BF16),
            in_specs=in_specs,
            out_specs=spec,
            input_output_aliases=alias,
            compiler_params=pltpu.CompilerParams(vmem_limit_bytes=16 << 20),
        )(*args)
    return out


def solution(mesh):
    in_specs = (
        P("ctx", "head"),
        P("ctx", "head"),
        P("ctx", "head"),
        P("ctx", "head"),
        P("head"),
        P(None, "head"),
        P(None, "head"),
        P("head"),
        P("ctx"),
    )
    out_specs = P("ctx", "head")
    return jax.shard_map(
        on_device, mesh=mesh, in_specs=in_specs, out_specs=out_specs, check_vma=False
    )
```

```python
import functools

import jax
import jax.numpy as jnp
from jax import lax
from jax.experimental import pallas as pl
from jax.experimental.pallas import tpu as pltpu
from jax.sharding import PartitionSpec as P

HDIM = 64
DSTATE = 128
CONV = 4
CHUNK = 256
WIDE = 256
SHARES = (4, 2, 2)
F32 = jnp.float32
BF16 = jnp.bfloat16


def shifted(value, axis, steps):
    count = lax.axis_size(axis)
    pairs = [(source, (source + steps) % count) for source in range(count)]
    return lax.ppermute(value, axis, pairs)


def crossed(value, axis, mask):
    count = lax.axis_size(axis)
    return lax.ppermute(value, axis, [(source, source ^ mask) for source in range(count)])


def iota(shape, dim):
    return lax.broadcasted_iota(jnp.int32, shape, dim)


def mm(a, b):
    return jnp.dot(a, b, preferred_element_type=F32)


def mm_t(a, b):
    return lax.dot_general(a, b, (((1,), (1,)), ((), ())), preferred_element_type=F32)


def parts(value, count, axis=1):
    pieces = []
    for _ in range(count):
        piece = value.astype(BF16)
        pieces.append(piece)
        value = value - piece.astype(F32)
    return jnp.concatenate(pieces, axis=axis)


def spread_matrix(copies, heads, low, width):
    shape = (copies * heads, width)
    head = lax.rem(iota(shape, 0), heads)
    return jnp.where(head == (iota(shape, 1) + low) // HDIM, 1.0, 0.0).astype(BF16)


def call(kernel, in_specs, outs, scratch, name, out_spec=None, alias=None, limit=12):
    spec = out_spec or pl.BlockSpec(memory_space=pltpu.VMEM)
    return pl.pallas_call(
        kernel,
        out_shape=outs,
        in_specs=in_specs,
        out_specs=[spec] * len(outs) if isinstance(outs, list) else spec,
        scratch_shapes=list(scratch),
        input_output_aliases=alias or {},
        compiler_params=pltpu.CompilerParams(vmem_limit_bytes=limit << 20),
        name=name,
    )


def tail_kernel(start_ref, x_ref, bc_ref, out_ref, buffer, sem):
    rows, width = x_ref.shape
    copy = pltpu.make_async_copy(x_ref.at[pl.ds(rows - 8, 8), :], buffer, sem)
    copy.start()
    starts = start_ref[:, rows - 128 :].astype(F32)
    last = starts[:, 127:128]
    before = jnp.maximum(last, starts[:, 126:127])
    row = iota((8, 128), 0)
    kept = jnp.where(row == 5, 1.0 - before, jnp.where(row == 6, 1.0 - last, 1.0))
    kept = jnp.where(row >= 5, kept, 0.0)
    bc = bc_ref[:, rows - 128 :].astype(F32).T[120:, :]
    bc = jnp.concatenate([bc] * (128 // bc.shape[1]), axis=1)
    out_ref[:, width:] = (bc * kept).astype(BF16)
    copy.wait()
    kept = jnp.concatenate([kept] * (width // 128), axis=1)
    out_ref[:, :width] = (buffer[...].astype(F32) * kept).astype(BF16)


def prep_kernel(dt_ref, scale_ref, start_ref, fac_ref, eps_ref, rows_ref, idc_ref, idr_ref):
    heads = dt_ref.shape[0]
    square = (CHUNK, CHUNK)
    lower = jnp.where(iota(square, 0) >= iota(square, 1), 1.0, 0.0).astype(BF16)
    upper = jnp.where(iota(square, 0) <= iota(square, 1), 1.0, 0.0).astype(BF16)
    mids = []
    offset = jnp.zeros((8, 1), F32)
    for j in range(2):
        span = slice(j * CHUNK, (j + 1) * CHUNK)
        sums = mm_t(lower, parts(dt_ref[:, span], 3, 0))
        sums = sums[:, :heads] + sums[:, heads : 2 * heads] + sums[:, 2 * heads :]
        log_decay = -(sums * scale_ref[...])
        mid = 0.5 * log_decay[CHUNK - 1 : CHUNK, :]
        mids.append(mid)
        fac_ref[span, :] = parts(jnp.exp(mid - log_decay), 2)
        eps_ref[span, :] = parts(jnp.exp(log_decay - mid), 2)
        starts = start_ref[:, span].astype(F32).astype(BF16)
        by_row = mm(jnp.broadcast_to(starts, (8, CHUNK)), upper) + offset
        by_col = mm_t(lower, jnp.broadcast_to(starts, (128, CHUNK)))
        idr_ref[:, span] = by_row
        idc_ref[span, :] = by_col + offset[:1, :]
        offset = by_row[:, CHUNK - 1 : CHUNK]
    middle = idr_ref[:1, CHUNK - 1 : CHUNK]
    final = idr_ref[:1, 2 * CHUNK - 1 : 2 * CHUNK]
    keep = jnp.where(middle == final, 1.0, 0.0)
    whole = jnp.where(final == 0.0, 1.0, 0.0)
    first, second = mids
    table = jnp.concatenate(
        [
            jnp.exp(first + second),
            jnp.exp(first + 2.0 * second) * keep,
            jnp.exp(second),
            jnp.exp(first),
            jnp.exp(2.0 * first + second),
            jnp.exp(2.0 * (first + second)) * whole,
            first,
            second,
        ],
        axis=0,
    )
    rows_ref[...] = mm(parts(table, 3), spread_matrix(3, heads, 0, rows_ref.shape[1]))


def bc_kernel(bc_ref, tail_ref, taps_ref, idr_ref, out_ref):
    width, rows = bc_ref.shape
    low = tail_ref.shape[1] - 128
    tail = tail_ref[:, low : low + width].astype(F32)
    tail = jnp.concatenate([jnp.zeros((120, width), F32), tail], axis=0).T
    values = jnp.concatenate([tail, bc_ref[...].astype(F32)], axis=1)
    ids = jnp.concatenate([jnp.zeros((8, 128), F32), idr_ref[...]], axis=1)
    taps = jnp.concatenate([taps_ref[...].astype(F32)] * 2, axis=0).T
    total = values[:, 128:] * taps[:, CONV - 1 : CONV]
    for back in range(1, CONV):
        same = pltpu.roll(ids, back, 1)[:1, 128:] == ids[:1, 128:]
        kept = jnp.where(same, 1.0, 0.0)
        piece = pltpu.roll(values, back, 1)[:, 128:] * kept
        total = total + piece * taps[:, CONV - 1 - back : CONV - back]
    out_ref[...] = (total / (1.0 + jnp.exp(-total))).astype(BF16)


def conv_kernel(low, x_ref, tail_ref, taps_ref, fac_ref, idc_ref, out_ref, ids_ref, mask_ref):
    rows = x_ref.shape[0]
    heads = fac_ref.shape[1] // 2
    ids_ref[:8, :] = jnp.zeros((8, 128), F32)
    ids_ref[8:, :] = idc_ref[...]
    for back in range(1, CONV):
        same = ids_ref[pl.ds(8 - back, rows), :] == idc_ref[...]
        mask_ref[back - 1] = jnp.where(same, 1.0, 0.0)
    for block in range(out_ref.shape[1] // WIDE):
        start = low + block * WIDE
        cols = slice(start, start + WIDE)
        spread = spread_matrix(2, heads, start, WIDE)
        taps = 0.5 * taps_ref[:, cols].astype(F32)
        factor = mm(fac_ref[...], spread)
        size = 128
        for row in range(0, rows, size):
            span = slice(row, row + size)
            above = tail_ref[:, cols] if row == 0 else x_ref[row - 8 : row, cols]
            here = x_ref[span, cols].astype(F32)
            padded = jnp.concatenate([above.astype(F32), here], axis=0)
            half = here * taps[CONV - 1 : CONV, :]
            for back in range(1, CONV):
                mask = jnp.concatenate([mask_ref[back - 1, span, :]] * (WIDE // 128), axis=1)
                piece = pltpu.roll(padded, back, 0)[8:] * mask
                half = half + piece * taps[CONV - 1 - back : CONV - back, :]
            value = half + half * jnp.tanh(half)
            out_ref[span, block * WIDE : (block + 1) * WIDE] = (value * factor[span]).astype(BF16)


def pick(flag, refs):
    half = len(refs) // 2
    near = jnp.concatenate([ref[...] for ref in refs[:half]], axis=0).astype(F32)
    far = jnp.concatenate([ref[...] for ref in refs[half:]], axis=0).astype(F32)
    first = flag == 1
    return jnp.where(first, near, far), jnp.where(first, far, near)


def state_kernel(low, split, flag_ref, *refs):
    b_rows, _ = pick(flag_ref[0, 0], refs[:split])
    xs_ref, rows_ref, idr_ref, mid_ref, end_ref = refs[split:]
    pieces = []
    for j in range(2):
        span = slice(j * CHUNK, (j + 1) * CHUNK)
        ids = idr_ref[:1, span]
        end = idr_ref[:1, (j + 1) * CHUNK - 1 : (j + 1) * CHUNK]
        pieces.append(jnp.where(ids == end, b_rows[:, span], 0.0).astype(BF16))
    for block in range(xs_ref.shape[1] // WIDE):
        here = slice(block * WIDE, (block + 1) * WIDE)
        cols = slice(low + block * WIDE, low + (block + 1) * WIDE)
        first = mm(pieces[0], xs_ref[:CHUNK, here])
        second = mm(pieces[1], xs_ref[CHUNK:, here])
        mid_ref[:, here] = (first * rows_ref[0:1, cols]).astype(BF16)
        end = first * rows_ref[1:2, cols] + second * rows_ref[2:3, cols]
        end_ref[:, here] = end.astype(end_ref.dtype)


def score_kernel(split, flag_ref, *refs):
    b_rows, c_rows = pick(flag_ref[0, 0], refs[:split])
    idc_ref, idr_ref, g_ref, live_ref, carried_ref = refs[split:]
    b_rows = b_rows.astype(BF16)
    c_cols = c_rows.T
    for j in range(2):
        span = slice(j * CHUNK, (j + 1) * CHUNK)
        ids = idc_ref[span, :]
        live_ref[span, :] = jnp.where(ids == 0.0, c_cols[span, :], 0.0).astype(BF16)
        scores = mm(c_cols[span, :].astype(BF16), b_rows[:, span])
        square = (CHUNK, CHUNK)
        wide = jnp.concatenate([ids] * (CHUNK // 128), axis=1)
        keep = (iota(square, 0) >= iota(square, 1)) & (wide == idr_ref[:1, span])
        g_ref[j] = jnp.where(keep, scores, 0.0).astype(BF16)
    before = idr_ref[:1, CHUNK - 1 : CHUNK]
    ids = idc_ref[CHUNK:, :]
    carried_ref[...] = jnp.where(ids == before, c_cols[CHUNK:, :], 0.0).astype(BF16)


def local_kernel(low, xs_ref, mid_ref, g_ref, carried_ref, eps_ref, rows_ref, z_ref, y_ref, dec_ref):
    heads = eps_ref.shape[1] // 2
    for block in range(xs_ref.shape[1] // WIDE):
        start = low + block * WIDE
        here = slice(block * WIDE, (block + 1) * WIDE)
        cols = slice(start, start + WIDE)
        spread = spread_matrix(2, heads, start, WIDE)
        for j in range(2):
            span = slice(j * CHUNK, (j + 1) * CHUNK)
            y = mm(g_ref[j], xs_ref[span, here])
            if j == 1:
                y = y + mm(carried_ref[...], mid_ref[:, here])
            half = 0.5 * z_ref[span, cols].astype(F32)
            gate = (half + half * jnp.tanh(half)) * mm(eps_ref[span, :], spread)
            y_ref[span, here] = y * gate
            dec_ref[span, here] = rows_ref[3 + j : 4 + j, cols] * gate


def final_kernel(low, state_ref, y_ref, dec_ref, live_ref, gain_ref, *refs):
    out_ref, buffer, sem = refs[-3:]
    square = (WIDE, WIDE)
    same = iota(square, 0) // HDIM == iota(square, 1) // HDIM
    mean_matrix = jnp.where(same, 1.0 / HDIM, 0.0).astype(BF16)
    copies = []
    for block in range(y_ref.shape[1] // WIDE):
        here = slice(block * WIDE, (block + 1) * WIDE)
        cols = slice(low + block * WIDE, low + (block + 1) * WIDE)
        gain = gain_ref[:, cols].astype(F32)
        for j in range(2):
            span = slice(j * CHUNK, (j + 1) * CHUNK)
            mixed = y_ref[span, here] + mm(live_ref[span, :], state_ref[:, here]) * dec_ref[span, here]
            mean = mm((mixed * mixed).astype(BF16), mean_matrix)
            buffer[block, span, :] = (mixed * lax.rsqrt(mean + 1e-05) * gain).astype(BF16)
        copy = pltpu.make_async_copy(buffer.at[block], out_ref.at[:, cols], sem.at[block])
        copy.start()
        copies.append(copy)
    for copy in copies:
        copy.wait()


def on_device(x_in, z_in, bc_in, dt, decay_scale, conv_x, conv_bc, norm_gain, doc_start):
    rows, columns = x_in.shape
    heads = dt.shape[1]
    bc_width = bc_in.shape[1]
    turns = lax.axis_size("ctx") // 8
    split = lax.axis_size("head")
    starts = doc_start.reshape(1, rows)
    spec = pl.BlockSpec(memory_space=pltpu.VMEM)
    smem = pl.BlockSpec(memory_space=pltpu.SMEM)
    hbm = pl.BlockSpec(memory_space=pltpu.HBM)
    shape = jax.ShapeDtypeStruct
    bc_rows = bc_in.T
    tail = call(
        tail_kernel,
        [spec, hbm, spec],
        shape((8, columns + 128), BF16),
        [pltpu.VMEM((8, columns), BF16), pltpu.SemaphoreType.DMA],
        "tail",
    )(starts, x_in, bc_rows)
    rim = shifted(tail, "ctx", 1)
    fac, eps, table, ids_col, ids_row = call(
        prep_kernel,
        [spec] * 3,
        [
            shape((rows, 2 * heads), BF16),
            shape((rows, 2 * heads), BF16),
            shape((8, columns), F32),
            shape((rows, 128), F32),
            shape((8, rows), F32),
        ],
        (),
        "prep",
    )(dt.T, decay_scale.reshape(1, heads), starts)
    own = call(bc_kernel, [spec] * 4, shape((bc_width, rows), BF16), (), "bc")(
        bc_rows, rim, conv_bc, ids_row
    )
    shares = [own] + [crossed(own, "head", mask) for mask in range(1, split)]
    flag = (lax.axis_index("head") < split // 2).astype(jnp.int32).reshape(1, 1)
    total = sum(SHARES)
    widths = [columns * share // total for share in SHARES]
    lows = [sum(widths[:group]) for group in range(len(widths))]
    state_type = BF16 if turns == 1 else F32
    gain = norm_gain.reshape(1, columns)

    def relay(low, width, end):
        if turns == 1:
            return shifted(end, "ctx", 1)
        through = table[5:6, low : low + width]
        turn = lambda _, incoming: shifted(through * incoming + end, "ctx", 1)
        return lax.fori_loop(0, turns, turn, jnp.zeros_like(end)).astype(BF16)

    values, middles, incoming = [], [], []
    for low, width in zip(lows, widths):
        part = call(
            functools.partial(conv_kernel, low),
            [spec] * 5,
            shape((rows, width), BF16),
            [pltpu.VMEM((rows + 8, 128), F32), pltpu.VMEM((CONV - 1, rows, 128), F32)],
            f"conv{low}",
        )(x_in, rim, conv_x, fac, ids_col)
        middle, end = call(
            functools.partial(state_kernel, low, split),
            [smem] + [spec] * (split + 3),
            [shape((DSTATE, width), BF16), shape((DSTATE, width), state_type)],
            (),
            f"state{low}",
        )(flag, *shares, part, table, ids_row)
        values.append(part)
        middles.append(middle)
        incoming.append(relay(low, width, end))
    scores, live, carried = call(
        functools.partial(score_kernel, split),
        [smem] + [spec] * (split + 2),
        [shape((2, CHUNK, CHUNK), BF16), shape((rows, DSTATE), BF16), shape((CHUNK, DSTATE), BF16)],
        (),
        "score",
    )(flag, *shares, ids_col, ids_row)
    out = None
    for group, (low, width) in enumerate(zip(lows, widths)):
        mixed, decay = call(
            functools.partial(local_kernel, low),
            [spec] * 7,
            [shape((rows, width), F32)] * 2,
            (),
            f"local{low}",
        )(values[group], middles[group], scores, carried, eps, table, z_in)
        blocks = width // WIDE
        args = [incoming[group], mixed, decay, live, gain]
        in_specs = [spec] * 5
        if group > 0:
            args.append(out)
            in_specs.append(hbm)
        out = call(
            functools.partial(final_kernel, low),
            in_specs,
            shape((rows, columns), BF16),
            [pltpu.VMEM((blocks, rows, WIDE), BF16), pltpu.SemaphoreType.DMA((blocks,))],
            f"final{low}",
            hbm,
            {5: 0} if group > 0 else {},
        )(*args)
    return out


def solution(mesh):
    in_specs = (
        P("ctx", "head"),
        P("ctx", "head"),
        P("ctx", "head"),
        P("ctx", "head"),
        P("head"),
        P(None, "head"),
        P(None, "head"),
        P("head"),
        P("ctx"),
    )
    out_specs = P("ctx", "head")
    return jax.shard_map(
        on_device, mesh=mesh, in_specs=in_specs, out_specs=out_specs, check_vma=False
    )
```

```python
import functools

import jax
import jax.numpy as jnp
from jax import lax
from jax.experimental import pallas as pl
from jax.experimental.pallas import tpu as pltpu
from jax.sharding import PartitionSpec as P

HDIM = 64
DSTATE = 128
CONV = 4
CHUNK = 256
WIDE = 256
SHARES = (2, 4, 2)
EDGE = 16
F32 = jnp.float32
BF16 = jnp.bfloat16


def shifted(value, axis, steps):
    count = lax.axis_size(axis)
    pairs = [(source, (source + steps) % count) for source in range(count)]
    return lax.ppermute(value, axis, pairs)


def crossed(value, axis, mask):
    count = lax.axis_size(axis)
    return lax.ppermute(value, axis, [(source, source ^ mask) for source in range(count)])


def iota(shape, dim):
    return lax.broadcasted_iota(jnp.int32, shape, dim)


def mm(a, b):
    return jnp.dot(a, b, preferred_element_type=F32)


def mm_t(a, b):
    return lax.dot_general(a, b, (((1,), (1,)), ((), ())), preferred_element_type=F32)


def parts(value, count, axis=1):
    pieces = []
    for _ in range(count):
        piece = value.astype(BF16)
        pieces.append(piece)
        value = value - piece.astype(F32)
    return jnp.concatenate(pieces, axis=axis)


def spread_matrix(copies, heads, low, width):
    shape = (copies * heads, width)
    head = lax.rem(iota(shape, 0), heads)
    return jnp.where(head == (iota(shape, 1) + low) // HDIM, 1.0, 0.0).astype(BF16)


def call(kernel, in_specs, outs, scratch, name, out_spec=None, alias=None, limit=12):
    spec = out_spec or pl.BlockSpec(memory_space=pltpu.VMEM)
    return pl.pallas_call(
        kernel,
        out_shape=outs,
        in_specs=in_specs,
        out_specs=[spec] * len(outs) if isinstance(outs, list) else spec,
        scratch_shapes=list(scratch),
        input_output_aliases=alias or {},
        compiler_params=pltpu.CompilerParams(vmem_limit_bytes=limit << 20),
        name=name,
    )


def rim_rows(columns, split, width):
    return -(-3 * (columns + 128 * split) // width // 16) * 16


def rim_block(x_ref, start_ref, shares, width):
    rows, columns = x_ref.shape
    total = rim_rows(columns, len(shares), width)
    starts = start_ref[:, rows - 128 :].astype(F32)
    last = starts[:, 127:128]
    before = jnp.maximum(last, starts[:, 126:127])
    row = iota((8, 128), 0)
    kept = jnp.where(row == 5, 1.0 - before, jnp.where(row == 6, 1.0 - last, 1.0))
    kept = jnp.where(row >= 5, kept, 0.0)
    kept = jnp.concatenate([kept] * (width // 128), axis=1)
    row = iota((8, width), 0)
    block = jnp.zeros((total, width), F32)
    below = jnp.zeros((total - 8, width), F32)
    slot = 0
    for low in range(0, columns, width):
        piece = x_ref[rows - 8 :, low : low + width].astype(F32) * kept
        piece = jnp.concatenate([piece, below], axis=0)
        block = block + pltpu.roll(piece, (slot - 5) % total, 0)
        slot += 3
    count = width // 128
    for index in range(0, len(shares), count):
        piece = [share[share.shape[0] - 8 :, :128] for share in shares[index : index + count]]
        piece = jnp.concatenate(piece, axis=1).astype(F32)
        piece = jnp.where((row >= 3) & (row < 6), piece, 0.0)
        piece = jnp.concatenate([piece, below], axis=0)
        block = block + pltpu.roll(piece, (slot - 3) % total, 0)
        slot += 3
    return block.astype(BF16)


def tail_kernel(x_ref, start_ref, *refs):
    refs[-1][...] = rim_block(x_ref, start_ref, refs[:-1], refs[-1].shape[1])


def prep_kernel(dt_ref, scale_ref, start_ref, x_hbm, *refs):
    fac_ref, eps_ref, rows_ref, idc_ref, idr_ref, x_ref, sem = refs
    copy = pltpu.make_async_copy(x_hbm, x_ref, sem)
    copy.start()
    heads = dt_ref.shape[0]
    square = (CHUNK, CHUNK)
    lower = jnp.where(iota(square, 0) >= iota(square, 1), 1.0, 0.0).astype(BF16)
    upper = jnp.where(iota(square, 0) <= iota(square, 1), 1.0, 0.0).astype(BF16)
    mids = []
    offset = jnp.zeros((8, 1), F32)
    for j in range(2):
        span = slice(j * CHUNK, (j + 1) * CHUNK)
        sums = mm_t(lower, parts(dt_ref[:, span], 3, 0))
        sums = sums[:, :heads] + sums[:, heads : 2 * heads] + sums[:, 2 * heads :]
        log_decay = -(sums * scale_ref[...])
        mid = 0.5 * log_decay[CHUNK - 1 : CHUNK, :]
        mids.append(mid)
        fac_ref[span, :] = parts(jnp.exp(mid - log_decay), 2)
        eps_ref[span, :] = parts(jnp.exp(log_decay - mid), 2)
        starts = start_ref[:, span].astype(F32).astype(BF16)
        by_row = mm(jnp.broadcast_to(starts, (8, CHUNK)), upper) + offset
        by_col = mm_t(lower, jnp.broadcast_to(starts, (128, CHUNK)))
        idr_ref[:, span] = by_row
        idc_ref[span, :] = by_col + offset[:1, :]
        offset = by_row[:, CHUNK - 1 : CHUNK]
    middle = idr_ref[:1, CHUNK - 1 : CHUNK]
    final = idr_ref[:1, 2 * CHUNK - 1 : 2 * CHUNK]
    keep = jnp.where(middle == final, 1.0, 0.0)
    whole = jnp.where(final == 0.0, 1.0, 0.0)
    first, second = mids
    table = jnp.concatenate(
        [
            jnp.exp(first + second),
            jnp.exp(first + 2.0 * second) * keep,
            jnp.exp(second),
            jnp.exp(first),
            jnp.exp(2.0 * first + second),
            jnp.exp(2.0 * (first + second)) * whole,
            first,
            second,
        ],
        axis=0,
    )
    rows_ref[...] = mm(parts(table, 3), spread_matrix(3, heads, 0, rows_ref.shape[1]))
    copy.wait()


def bc_kernel(*refs):
    sources, (out_ref, *copied), (bc_ref, taps_ref, sems) = refs[:6], refs[6:11], refs[11:]
    width, rows = bc_ref.shape
    start_ref = copied[0]
    copies = [
        pltpu.make_async_copy(source, target, sems.at[index])
        for index, (source, target) in enumerate(zip(sources, [bc_ref, taps_ref, *copied]))
    ]
    for copy in copies:
        copy.start()
    for copy in copies[:3]:
        copy.wait()
    values = jnp.concatenate([jnp.zeros((width, 128), F32), bc_ref[...].astype(F32)], axis=1)
    starts = jnp.broadcast_to(start_ref[...].astype(F32), (8, rows))
    open_ = jnp.concatenate([jnp.ones((8, 128), F32), 1.0 - starts], axis=1)
    taps = jnp.concatenate([taps_ref[...].astype(F32)] * 2, axis=0).T
    total = values[:, 128:] * taps[:, CONV - 1 : CONV]
    kept = open_
    for back in range(1, CONV):
        if back > 1:
            kept = kept * pltpu.roll(open_, back - 1, 1)
        piece = pltpu.roll(values, back, 1)[:, 128:] * kept[:1, 128:]
        total = total + piece * taps[:, CONV - 1 - back : CONV - back]
    out_ref[:width, :] = (total / (1.0 + jnp.exp(-total))).astype(BF16)
    lane = iota((1, 128), 1)
    last = open_[:1, rows:]
    near, far = last[:, 127:128], last[:, 126:127]
    kept = jnp.where(lane == 125, near * far, jnp.where(lane == 126, near, 1.0))
    ends = jnp.where(lane >= 125, kept, 0.0) * values[:, rows:]
    after = jnp.zeros((width, 128), F32)
    for back in range(1, CONV):
        after = after + pltpu.roll(ends, back, 1) * taps[:, CONV - 1 - back : CONV - back]
    table = jnp.where(lane < 3, total[:, :128], pltpu.roll(after, 3, 1))
    table = jnp.where(lane < 6, table, 0.0).T[:8, :]
    high = table.astype(BF16)
    low = (table - high.astype(F32)).astype(BF16)
    gap = [jnp.zeros((8, 64 - width), BF16)] if width < 64 else []
    out_ref[width:, :128] = jnp.concatenate([high, *gap, low, *gap], axis=1)
    out_ref[width:, 128:] = jnp.zeros((8, rows - 128), BF16)
    for copy in copies[3:]:
        copy.wait()


def fix_kernel(x_ref, rim_ref, taps_ref, fac_ref, idc_ref, *refs):
    shares, bc_ref, xs_ref = refs[:-2], refs[-2], refs[-1]
    columns = x_ref.shape[1]
    depth = rim_rows(columns, len(shares), rim_ref.shape[1])
    base = rim_ref.shape[0] - depth

    def rim(low, size, row):
        slot, lane = low // rim_ref.shape[1], low % rim_ref.shape[1]
        block = rim_ref[base:, lane : lane + size].astype(F32)
        return pltpu.roll(block, (row - 3 * slot) % depth, 0)[:8]

    heads = fac_ref.shape[1] // 2
    width = shares[0].shape[0] - 8
    live = idc_ref[:8, :] == 0.0
    lane = iota((width, 128), 1)
    for index, share in enumerate(shares):
        low = columns + index * 128
        own = share[width:, :128].astype(F32)
        after = jnp.where(live, rim(low, 128, 0), 0.0)
        total = own + after
        total = total + pltpu.roll(total, 64, 1)
        value = total / (1.0 + jnp.exp(-total))
        value = jnp.concatenate([value, jnp.zeros((120, 128), F32)], axis=0).T[:width, :]
        first = jnp.where(lane < 3, value, share[:width, :128].astype(F32))
        bc_ref[index * width : (index + 1) * width, :] = first.astype(BF16)
    ids = jnp.concatenate([jnp.zeros((8, 128), F32), idc_ref[:EDGE, :]], axis=0)
    masks = []
    for back in range(1, CONV):
        same = pltpu.roll(ids, back, 0)[8:] == ids[8:]
        masks.append(jnp.concatenate([jnp.where(same, 1.0, 0.0)] * (WIDE // 128), axis=1))
    for low in range(0, columns, WIDE):
        cols = slice(low, low + WIDE)
        taps = 0.5 * taps_ref[:, cols].astype(F32)
        above = rim(low, WIDE, 5)
        padded = jnp.concatenate([above, x_ref[:EDGE, cols].astype(F32)], axis=0)
        half = padded[8:] * taps[CONV - 1 : CONV, :]
        for back in range(1, CONV):
            piece = pltpu.roll(padded, back, 0)[8:] * masks[back - 1]
            half = half + piece * taps[CONV - 1 - back : CONV - back, :]
        value = half + half * jnp.tanh(half)
        factor = mm(fac_ref[:EDGE, :], spread_matrix(2, heads, low, WIDE))
        xs_ref[:, cols] = (value * factor).astype(BF16)


def conv_kernel(low, x_ref, taps_ref, fac_ref, idc_ref, out_ref, ids_ref, mask_ref):
    rows = x_ref.shape[0]
    heads = fac_ref.shape[1] // 2
    ids_ref[:8, :] = jnp.zeros((8, 128), F32)
    ids_ref[8:, :] = idc_ref[...]
    for back in range(1, CONV):
        same = ids_ref[pl.ds(8 - back, rows), :] == idc_ref[...]
        mask_ref[back - 1] = jnp.where(same, 1.0, 0.0)
    for block in range(out_ref.shape[1] // WIDE):
        start = low + block * WIDE
        cols = slice(start, start + WIDE)
        spread = spread_matrix(2, heads, start, WIDE)
        taps = 0.5 * taps_ref[:, cols].astype(F32)
        factor = mm(fac_ref[...], spread)
        size = 128
        for row in range(0, rows, size):
            span = slice(row, row + size)
            here = x_ref[span, cols].astype(F32)
            if row == 0:
                above = jnp.zeros((8, WIDE), F32)
            else:
                above = x_ref[row - 8 : row, cols].astype(F32)
            padded = jnp.concatenate([above, here], axis=0)
            half = here * taps[CONV - 1 : CONV, :]
            for back in range(1, CONV):
                mask = jnp.concatenate([mask_ref[back - 1, span, :]] * (WIDE // 128), axis=1)
                piece = pltpu.roll(padded, back, 0)[8:] * mask
                half = half + piece * taps[CONV - 1 - back : CONV - back, :]
            value = half + half * jnp.tanh(half)
            out_ref[span, block * WIDE : (block + 1) * WIDE] = (value * factor[span]).astype(BF16)


def pick(flag, refs, first=None):
    half = len(refs) // 2
    width = refs[0].shape[0] - 8
    near = jnp.concatenate([ref[:width, :] for ref in refs[:half]], axis=0).astype(F32)
    far = jnp.concatenate([ref[:width, :] for ref in refs[half:]], axis=0).astype(F32)
    if first is not None:
        edge = first[...].astype(F32)
        near = jnp.concatenate([edge[:DSTATE], near[:, 128:]], axis=1)
        far = jnp.concatenate([edge[DSTATE:], far[:, 128:]], axis=1)
    own = flag == 1
    return jnp.where(own, near, far), jnp.where(own, far, near)


def ending(b_rows, idr_ref, j):
    span = slice(j * CHUNK, (j + 1) * CHUNK)
    end = idr_ref[:1, (j + 1) * CHUNK - 1 : (j + 1) * CHUNK]
    return jnp.where(idr_ref[:1, span] == end, b_rows[:, span], 0.0).astype(BF16)


def opening(xs_ref, edge_ref, here, cols):
    return jnp.concatenate([edge_ref[:, cols], xs_ref[EDGE:CHUNK, here]], axis=0)


def state_kernel(low, split, carries, flag_ref, *refs):
    xs_ref, rows_ref, idr_ref, *edges, end_ref = refs[split:]
    if carries:
        x_ref, start_ref = edges
        edges = []
        end_ref[DSTATE:, :] = rim_block(x_ref, start_ref, refs[:split], end_ref.shape[1])
    b_rows, _ = pick(flag_ref[0, 0], refs[:split], edges[0] if edges else None)
    pieces = [ending(b_rows, idr_ref, j) for j in range(2)]
    for block in range(xs_ref.shape[1] // WIDE):
        here = slice(block * WIDE, (block + 1) * WIDE)
        cols = slice(low + block * WIDE, low + (block + 1) * WIDE)
        values = opening(xs_ref, edges[1], here, cols) if edges else xs_ref[:CHUNK, here]
        first = mm(pieces[0], values)
        second = mm(pieces[1], xs_ref[CHUNK:, here])
        end = first * rows_ref[1:2, cols] + second * rows_ref[2:3, cols]
        end_ref[:DSTATE, here] = end.astype(end_ref.dtype)


def score_kernel(split, flag_ref, *refs):
    edge_ref, idc_ref, idr_ref, g_ref, live_ref, carried_ref, ending_ref = refs[split:]
    b_rows, c_rows = pick(flag_ref[0, 0], refs[:split], edge_ref)
    ending_ref[...] = ending(b_rows, idr_ref, 0)
    b_rows = b_rows.astype(BF16)
    c_cols = c_rows.T
    for j in range(2):
        span = slice(j * CHUNK, (j + 1) * CHUNK)
        ids = idc_ref[span, :]
        live_ref[span, :] = jnp.where(ids == 0.0, c_cols[span, :], 0.0).astype(BF16)
        scores = mm(c_cols[span, :].astype(BF16), b_rows[:, span])
        square = (CHUNK, CHUNK)
        wide = jnp.concatenate([ids] * (CHUNK // 128), axis=1)
        keep = (iota(square, 0) >= iota(square, 1)) & (wide == idr_ref[:1, span])
        g_ref[j] = jnp.where(keep, scores, 0.0).astype(BF16)
    before = idr_ref[:1, CHUNK - 1 : CHUNK]
    ids = idc_ref[CHUNK:, :]
    carried_ref[...] = jnp.where(ids == before, c_cols[CHUNK:, :], 0.0).astype(BF16)


def local_kernel(low, xs_ref, edge_ref, g_ref, carried_ref, ending_ref, eps_ref, rows_ref, z_ref, y_ref, dec_ref):
    heads = eps_ref.shape[1] // 2
    for block in range(xs_ref.shape[1] // WIDE):
        start = low + block * WIDE
        here = slice(block * WIDE, (block + 1) * WIDE)
        cols = slice(start, start + WIDE)
        spread = spread_matrix(2, heads, start, WIDE)
        values = opening(xs_ref, edge_ref, here, cols)
        middle = (mm(ending_ref[...], values) * rows_ref[0:1, cols]).astype(BF16)
        for j in range(2):
            span = slice(j * CHUNK, (j + 1) * CHUNK)
            if j == 0:
                y = mm(g_ref[0], values)
            else:
                y = mm(g_ref[1], xs_ref[span, here]) + mm(carried_ref[...], middle)
            half = 0.5 * z_ref[span, cols].astype(F32)
            gate = (half + half * jnp.tanh(half)) * mm(eps_ref[span, :], spread)
            y_ref[span, here] = y * gate
            dec_ref[span, here] = rows_ref[3 + j : 4 + j, cols] * gate


def final_kernel(low, state_ref, y_ref, dec_ref, live_ref, gain_ref, *refs):
    out_ref, buffer, sem = refs[-3:]
    square = (WIDE, WIDE)
    same = iota(square, 0) // HDIM == iota(square, 1) // HDIM
    mean_matrix = jnp.where(same, 1.0 / HDIM, 0.0).astype(BF16)
    copies = []
    for block in range(y_ref.shape[1] // WIDE):
        here = slice(block * WIDE, (block + 1) * WIDE)
        cols = slice(low + block * WIDE, low + (block + 1) * WIDE)
        gain = gain_ref[:, cols].astype(F32)
        for j in range(2):
            span = slice(j * CHUNK, (j + 1) * CHUNK)
            mixed = y_ref[span, here] + mm(live_ref[span, :], state_ref[:DSTATE, here]) * dec_ref[span, here]
            mean = mm((mixed * mixed).astype(BF16), mean_matrix)
            buffer[block, span, :] = (mixed * lax.rsqrt(mean + 1e-05) * gain).astype(BF16)
        copy = pltpu.make_async_copy(buffer.at[block], out_ref.at[:, cols], sem.at[block])
        copy.start()
        copies.append(copy)
    for copy in copies:
        copy.wait()


def on_device(x_in, z_in, bc_in, dt, decay_scale, conv_x, conv_bc, norm_gain, doc_start):
    rows, columns = x_in.shape
    heads = dt.shape[1]
    bc_width = bc_in.shape[1]
    turns = lax.axis_size("ctx") // 8
    split = lax.axis_size("head")
    starts = doc_start.reshape(1, rows)
    spec = pl.BlockSpec(memory_space=pltpu.VMEM)
    smem = pl.BlockSpec(memory_space=pltpu.SMEM)
    hbm = pl.BlockSpec(memory_space=pltpu.HBM)
    shape = jax.ShapeDtypeStruct
    in_hbm = lambda value: pltpu.with_memory_space_constraint(value, pltpu.HBM)
    own, starts, steps, scale, taps = call(
        bc_kernel,
        [hbm] * 6,
        [
            shape((bc_width + 8, rows), BF16),
            shape((1, rows), jnp.int32),
            shape((heads, rows), F32),
            shape((1, heads), F32),
            shape((CONV, columns), BF16),
        ],
        [
            pltpu.VMEM((bc_width, rows), BF16),
            pltpu.VMEM((CONV, bc_width), BF16),
            pltpu.SemaphoreType.DMA((6,)),
        ],
        "bc",
    )(
        in_hbm(bc_in.T),
        in_hbm(conv_bc),
        in_hbm(starts),
        in_hbm(dt.T),
        in_hbm(decay_scale.reshape(1, heads)),
        in_hbm(conv_x),
    )
    shares = [own] + [crossed(own, "head", mask) for mask in range(1, split)]
    fac, eps, table, ids_col, ids_row, x_near = call(
        prep_kernel,
        [spec] * 3 + [hbm],
        [
            shape((rows, 2 * heads), BF16),
            shape((rows, 2 * heads), BF16),
            shape((8, columns), F32),
            shape((rows, 128), F32),
            shape((8, rows), F32),
            shape((rows, columns), BF16),
        ],
        [pltpu.SemaphoreType.DMA],
        "prep",
    )(steps, scale, starts, in_hbm(x_in))
    flag = (lax.axis_index("head") < split // 2).astype(jnp.int32).reshape(1, 1)
    total = sum(SHARES)
    widths = [columns * share // total for share in SHARES]
    lows = [sum(widths[:group]) for group in range(len(widths))]
    state_type = BF16 if turns == 1 else F32
    gain = norm_gain.reshape(1, columns)
    extra = rim_rows(columns, split, widths[0])

    def fixed(rim):
        return call(
            fix_kernel,
            [spec] * (5 + split),
            [shape((2 * DSTATE, 128), BF16), shape((EDGE, columns), BF16)],
            (),
            "fix",
        )(x_near, rim, taps, fac, ids_col, *shares)

    edges = []
    if turns > 1:
        tail = call(tail_kernel, [spec] * (2 + split), shape((extra, widths[0]), BF16), (), "tail")
        edges = fixed(shifted(tail(x_near, starts, *shares), "ctx", 1))

    def relay(low, width, end):
        if turns == 1:
            return shifted(end, "ctx", 1)
        through = table[5:6, low : low + width]
        turn = lambda _, incoming: shifted(through * incoming + end, "ctx", 1)
        return lax.fori_loop(0, turns, turn, jnp.zeros_like(end)).astype(BF16)

    values, incoming = [], []
    for low, width in zip(lows, widths):
        part = call(
            functools.partial(conv_kernel, low),
            [spec] * 4,
            shape((rows, width), BF16),
            [pltpu.VMEM((rows + 8, 128), F32), pltpu.VMEM((CONV - 1, rows, 128), F32)],
            f"conv{low}",
        )(x_near, taps, fac, ids_col)
        carries = turns == 1 and low == 0
        others = [x_near, starts] if carries else edges
        end = call(
            functools.partial(state_kernel, low, split, carries),
            [smem] + [spec] * (split + 3 + len(others)),
            shape((DSTATE + extra if carries else DSTATE, width), state_type),
            (),
            f"state{low}",
        )(flag, *shares, part, table, ids_row, *others)
        values.append(part)
        incoming.append(relay(low, width, end))
    edge_bc, edge_x = edges or fixed(incoming[0])
    scores, live, carried, ended = call(
        functools.partial(score_kernel, split),
        [smem] + [spec] * (split + 3),
        [
            shape((2, CHUNK, CHUNK), BF16),
            shape((rows, DSTATE), BF16),
            shape((CHUNK, DSTATE), BF16),
            shape((DSTATE, CHUNK), BF16),
        ],
        (),
        "score",
    )(flag, *shares, edge_bc, ids_col, ids_row)
    out = None
    for group, (low, width) in enumerate(zip(lows, widths)):
        mixed, decay = call(
            functools.partial(local_kernel, low),
            [spec] * 8,
            [shape((rows, width), F32)] * 2,
            (),
            f"local{low}",
        )(values[group], edge_x, scores, carried, ended, eps, table, z_in)
        blocks = width // WIDE
        args = [incoming[group], mixed, decay, live, gain]
        in_specs = [spec] * 5
        if group > 0:
            args.append(out)
            in_specs.append(hbm)
        out = call(
            functools.partial(final_kernel, low),
            in_specs,
            shape((rows, columns), BF16),
            [pltpu.VMEM((blocks, rows, WIDE), BF16), pltpu.SemaphoreType.DMA((blocks,))],
            f"final{low}",
            hbm,
            {5: 0} if group > 0 else {},
        )(*args)
    return out


def solution(mesh):
    in_specs = (
        P("ctx", "head"),
        P("ctx", "head"),
        P("ctx", "head"),
        P("ctx", "head"),
        P("head"),
        P(None, "head"),
        P(None, "head"),
        P("head"),
        P("ctx"),
    )
    out_specs = P("ctx", "head")
    return jax.shard_map(
        on_device, mesh=mesh, in_specs=in_specs, out_specs=out_specs, check_vma=False
    )
```

```python
import functools

import jax
import jax.numpy as jnp
from jax import lax
from jax.experimental import pallas as pl
from jax.experimental.pallas import tpu as pltpu
from jax.sharding import PartitionSpec as P

HDIM = 64
DSTATE = 128
CONV = 4
CHUNK = 256
WIDE = 256
SHARES = (4, 2, 2)
EDGE = 16
F32 = jnp.float32
BF16 = jnp.bfloat16


def shifted(value, axis, steps):
    count = lax.axis_size(axis)
    pairs = [(source, (source + steps) % count) for source in range(count)]
    return lax.ppermute(value, axis, pairs)


def crossed(value, axis, mask):
    count = lax.axis_size(axis)
    return lax.ppermute(value, axis, [(source, source ^ mask) for source in range(count)])


def iota(shape, dim):
    return lax.broadcasted_iota(jnp.int32, shape, dim)


def mm(a, b):
    return jnp.dot(a, b, preferred_element_type=F32)


def mm_t(a, b):
    return lax.dot_general(a, b, (((1,), (1,)), ((), ())), preferred_element_type=F32)


def parts(value, count, axis=1):
    pieces = []
    for _ in range(count):
        piece = value.astype(BF16)
        pieces.append(piece)
        value = value - piece.astype(F32)
    return jnp.concatenate(pieces, axis=axis)


def spread_matrix(copies, heads, low, width):
    shape = (copies * heads, width)
    head = lax.rem(iota(shape, 0), heads)
    return jnp.where(head == (iota(shape, 1) + low) // HDIM, 1.0, 0.0).astype(BF16)


def call(kernel, in_specs, outs, scratch, name, out_spec=None, alias=None, limit=12):
    spec = out_spec or pl.BlockSpec(memory_space=pltpu.VMEM)
    return pl.pallas_call(
        kernel,
        out_shape=outs,
        in_specs=in_specs,
        out_specs=[spec] * len(outs) if isinstance(outs, list) else spec,
        scratch_shapes=list(scratch),
        input_output_aliases=alias or {},
        compiler_params=pltpu.CompilerParams(vmem_limit_bytes=limit << 20),
        name=name,
    )


def rim_rows(columns, split, width):
    slots = columns // width + -(-128 * split // width)
    return -(-3 * slots // 16) * 16


def rim_block(x_ref, start_ref, shares, width):
    rows, columns = x_ref.shape
    total = rim_rows(columns, len(shares), width)
    starts = start_ref[:, rows - 128 :].astype(F32)
    last = starts[:, 127:128]
    before = jnp.maximum(last, starts[:, 126:127])
    row = iota((8, 128), 0)
    kept = jnp.where(row == 5, 1.0 - before, jnp.where(row == 6, 1.0 - last, 1.0))
    kept = jnp.where(row >= 5, kept, 0.0)
    kept = jnp.concatenate([kept] * (width // 128), axis=1)
    row = iota((8, width), 0)
    block = jnp.zeros((total, width), F32)
    below = jnp.zeros((total - 8, width), F32)
    slot = 0
    for low in range(0, columns, width):
        piece = x_ref[rows - 8 :, low : low + width].astype(F32) * kept
        piece = jnp.concatenate([piece, below], axis=0)
        block = block + pltpu.roll(piece, (slot - 5) % total, 0)
        slot += 3
    count = width // 128
    for index in range(0, len(shares), count):
        piece = [share[share.shape[0] - 8 :, :128] for share in shares[index : index + count]]
        gap = width - 128 * len(piece)
        piece += [jnp.zeros((8, gap), BF16)] if gap else []
        piece = jnp.concatenate(piece, axis=1).astype(F32)
        piece = jnp.where((row >= 3) & (row < 6), piece, 0.0)
        piece = jnp.concatenate([piece, below], axis=0)
        block = block + pltpu.roll(piece, (slot - 3) % total, 0)
        slot += 3
    return block.astype(BF16)


def tail_kernel(x_ref, start_ref, *refs):
    refs[-1][...] = rim_block(x_ref, start_ref, refs[:-1], refs[-1].shape[1])


def prep_kernel(dt_ref, scale_ref, start_ref, x_hbm, *refs):
    fac_ref, eps_ref, rows_ref, idc_ref, idr_ref, x_ref, sem = refs
    copy = pltpu.make_async_copy(x_hbm, x_ref, sem)
    copy.start()
    heads = dt_ref.shape[0]
    square = (CHUNK, CHUNK)
    lower = jnp.where(iota(square, 0) >= iota(square, 1), 1.0, 0.0).astype(BF16)
    upper = jnp.where(iota(square, 0) <= iota(square, 1), 1.0, 0.0).astype(BF16)
    mids = []
    offset = jnp.zeros((8, 1), F32)
    for j in range(2):
        span = slice(j * CHUNK, (j + 1) * CHUNK)
        sums = mm_t(lower, parts(dt_ref[:, span], 3, 0))
        sums = sums[:, :heads] + sums[:, heads : 2 * heads] + sums[:, 2 * heads :]
        log_decay = -(sums * scale_ref[...])
        mid = 0.5 * log_decay[CHUNK - 1 : CHUNK, :]
        mids.append(mid)
        fac_ref[span, :] = parts(jnp.exp(mid - log_decay), 2)
        eps_ref[span, :] = parts(jnp.exp(log_decay - mid), 2)
        starts = start_ref[:, span].astype(F32).astype(BF16)
        by_row = mm(jnp.broadcast_to(starts, (8, CHUNK)), upper) + offset
        by_col = mm_t(lower, jnp.broadcast_to(starts, (128, CHUNK)))
        idr_ref[:, span] = by_row
        idc_ref[span, :] = by_col + offset[:1, :]
        offset = by_row[:, CHUNK - 1 : CHUNK]
    middle = idr_ref[:1, CHUNK - 1 : CHUNK]
    final = idr_ref[:1, 2 * CHUNK - 1 : 2 * CHUNK]
    keep = jnp.where(middle == final, 1.0, 0.0)
    whole = jnp.where(final == 0.0, 1.0, 0.0)
    first, second = mids
    table = jnp.concatenate(
        [
            jnp.exp(first + second),
            jnp.exp(first + 2.0 * second) * keep,
            jnp.exp(second),
            jnp.exp(first),
            jnp.exp(2.0 * first + second),
            jnp.exp(2.0 * (first + second)) * whole,
            first,
            second,
        ],
        axis=0,
    )
    rows_ref[...] = mm(parts(table, 3), spread_matrix(3, heads, 0, rows_ref.shape[1]))
    copy.wait()


def bc_kernel(*refs):
    sources, (out_ref, *copied), (bc_ref, taps_ref, sems) = refs[:6], refs[6:11], refs[11:]
    width, rows = bc_ref.shape
    start_ref = copied[0]
    copies = [
        pltpu.make_async_copy(source, target, sems.at[index])
        for index, (source, target) in enumerate(zip(sources, [bc_ref, taps_ref, *copied]))
    ]
    for copy in copies:
        copy.start()
    for copy in copies[:3]:
        copy.wait()
    values = jnp.concatenate([jnp.zeros((width, 128), F32), bc_ref[...].astype(F32)], axis=1)
    starts = jnp.broadcast_to(start_ref[...].astype(F32), (8, rows))
    open_ = jnp.concatenate([jnp.ones((8, 128), F32), 1.0 - starts], axis=1)
    taps = jnp.concatenate([taps_ref[...].astype(F32)] * 2, axis=0).T
    total = values[:, 128:] * taps[:, CONV - 1 : CONV]
    kept = open_
    for back in range(1, CONV):
        if back > 1:
            kept = kept * pltpu.roll(open_, back - 1, 1)
        piece = pltpu.roll(values, back, 1)[:, 128:] * kept[:1, 128:]
        total = total + piece * taps[:, CONV - 1 - back : CONV - back]
    out_ref[:width, :] = (total / (1.0 + jnp.exp(-total))).astype(BF16)
    lane = iota((1, 128), 1)
    last = open_[:1, rows:]
    near, far = last[:, 127:128], last[:, 126:127]
    kept = jnp.where(lane == 125, near * far, jnp.where(lane == 126, near, 1.0))
    ends = jnp.where(lane >= 125, kept, 0.0) * values[:, rows:]
    after = jnp.zeros((width, 128), F32)
    for back in range(1, CONV):
        after = after + pltpu.roll(ends, back, 1) * taps[:, CONV - 1 - back : CONV - back]
    table = jnp.where(lane < 3, total[:, :128], pltpu.roll(after, 3, 1))
    table = jnp.where(lane < 6, table, 0.0).T[:8, :]
    high = table.astype(BF16)
    low = (table - high.astype(F32)).astype(BF16)
    gap = [jnp.zeros((8, 64 - width), BF16)] if width < 64 else []
    out_ref[width:, :128] = jnp.concatenate([high, *gap, low, *gap], axis=1)
    out_ref[width:, 128:] = jnp.zeros((8, rows - 128), BF16)
    for copy in copies[3:]:
        copy.wait()


def fix_kernel(x_ref, rim_ref, taps_ref, fac_ref, idc_ref, *refs):
    shares, bc_ref, xs_ref = refs[:-2], refs[-2], refs[-1]
    columns = x_ref.shape[1]
    depth = rim_rows(columns, len(shares), rim_ref.shape[1])
    base = rim_ref.shape[0] - depth

    def rim(low, size, row):
        slot, lane = low // rim_ref.shape[1], low % rim_ref.shape[1]
        block = rim_ref[base:, lane : lane + size].astype(F32)
        return pltpu.roll(block, (row - 3 * slot) % depth, 0)[:8]

    heads = fac_ref.shape[1] // 2
    width = shares[0].shape[0] - 8
    live = idc_ref[:8, :] == 0.0
    lane = iota((width, 128), 1)
    for index, share in enumerate(shares):
        low = columns + index * 128
        own = share[width:, :128].astype(F32)
        after = jnp.where(live, rim(low, 128, 0), 0.0)
        total = own + after
        total = total + pltpu.roll(total, 64, 1)
        value = total / (1.0 + jnp.exp(-total))
        value = jnp.concatenate([value, jnp.zeros((120, 128), F32)], axis=0).T[:width, :]
        first = jnp.where(lane < 3, value, share[:width, :128].astype(F32))
        bc_ref[index * width : (index + 1) * width, :] = first.astype(BF16)
    ids = jnp.concatenate([jnp.zeros((8, 128), F32), idc_ref[:EDGE, :]], axis=0)
    masks = []
    for back in range(1, CONV):
        same = pltpu.roll(ids, back, 0)[8:] == ids[8:]
        masks.append(jnp.concatenate([jnp.where(same, 1.0, 0.0)] * (WIDE // 128), axis=1))
    for low in range(0, columns, WIDE):
        cols = slice(low, low + WIDE)
        taps = 0.5 * taps_ref[:, cols].astype(F32)
        above = rim(low, WIDE, 5)
        padded = jnp.concatenate([above, x_ref[:EDGE, cols].astype(F32)], axis=0)
        half = padded[8:] * taps[CONV - 1 : CONV, :]
        for back in range(1, CONV):
            piece = pltpu.roll(padded, back, 0)[8:] * masks[back - 1]
            half = half + piece * taps[CONV - 1 - back : CONV - back, :]
        value = half + half * jnp.tanh(half)
        factor = mm(fac_ref[:EDGE, :], spread_matrix(2, heads, low, WIDE))
        xs_ref[:, cols] = (value * factor).astype(BF16)


def conv_kernel(low, x_ref, taps_ref, fac_ref, idc_ref, out_ref, ids_ref, mask_ref):
    rows = x_ref.shape[0]
    heads = fac_ref.shape[1] // 2
    ids_ref[:8, :] = jnp.zeros((8, 128), F32)
    ids_ref[8:, :] = idc_ref[...]
    for back in range(1, CONV):
        same = ids_ref[pl.ds(8 - back, rows), :] == idc_ref[...]
        mask_ref[back - 1] = jnp.where(same, 1.0, 0.0)
    for block in range(out_ref.shape[1] // WIDE):
        start = low + block * WIDE
        cols = slice(start, start + WIDE)
        spread = spread_matrix(2, heads, start, WIDE)
        taps = 0.5 * taps_ref[:, cols].astype(F32)
        factor = mm(fac_ref[...], spread)
        size = 128
        for row in range(0, rows, size):
            span = slice(row, row + size)
            here = x_ref[span, cols].astype(F32)
            if row == 0:
                above = jnp.zeros((8, WIDE), F32)
            else:
                above = x_ref[row - 8 : row, cols].astype(F32)
            padded = jnp.concatenate([above, here], axis=0)
            half = here * taps[CONV - 1 : CONV, :]
            for back in range(1, CONV):
                mask = jnp.concatenate([mask_ref[back - 1, span, :]] * (WIDE // 128), axis=1)
                piece = pltpu.roll(padded, back, 0)[8:] * mask
                half = half + piece * taps[CONV - 1 - back : CONV - back, :]
            value = half + half * jnp.tanh(half)
            out_ref[span, block * WIDE : (block + 1) * WIDE] = (value * factor[span]).astype(BF16)


def pick(flag, refs, first=None):
    half = len(refs) // 2
    width = refs[0].shape[0] - 8
    near = jnp.concatenate([ref[:width, :] for ref in refs[:half]], axis=0).astype(F32)
    far = jnp.concatenate([ref[:width, :] for ref in refs[half:]], axis=0).astype(F32)
    if first is not None:
        edge = first[...].astype(F32)
        near = jnp.concatenate([edge[:DSTATE], near[:, 128:]], axis=1)
        far = jnp.concatenate([edge[DSTATE:], far[:, 128:]], axis=1)
    own = flag == 1
    return jnp.where(own, near, far), jnp.where(own, far, near)


def ending(b_rows, idr_ref, j):
    span = slice(j * CHUNK, (j + 1) * CHUNK)
    end = idr_ref[:1, (j + 1) * CHUNK - 1 : (j + 1) * CHUNK]
    return jnp.where(idr_ref[:1, span] == end, b_rows[:, span], 0.0).astype(BF16)


def opening(xs_ref, edge_ref, here, cols):
    return jnp.concatenate([edge_ref[:, cols], xs_ref[EDGE:CHUNK, here]], axis=0)


def state_kernel(low, split, carries, flag_ref, *refs):
    xs_ref, rows_ref, idr_ref, *edges, end_ref = refs[split:]
    if carries:
        x_ref, start_ref = edges
        edges = []
        end_ref[DSTATE:, :] = rim_block(x_ref, start_ref, refs[:split], end_ref.shape[1])
    b_rows, _ = pick(flag_ref[0, 0], refs[:split], edges[0] if edges else None)
    pieces = [ending(b_rows, idr_ref, j) for j in range(2)]
    for block in range(xs_ref.shape[1] // WIDE):
        here = slice(block * WIDE, (block + 1) * WIDE)
        cols = slice(low + block * WIDE, low + (block + 1) * WIDE)
        values = opening(xs_ref, edges[1], here, cols) if edges else xs_ref[:CHUNK, here]
        first = mm(pieces[0], values)
        second = mm(pieces[1], xs_ref[CHUNK:, here])
        end = first * rows_ref[1:2, cols] + second * rows_ref[2:3, cols]
        end_ref[:DSTATE, here] = end.astype(end_ref.dtype)


def score_kernel(split, flag_ref, *refs):
    edge_ref, idc_ref, idr_ref, g_ref, live_ref, carried_ref, ending_ref = refs[split:]
    b_rows, c_rows = pick(flag_ref[0, 0], refs[:split], edge_ref)
    ending_ref[...] = ending(b_rows, idr_ref, 0)
    b_rows = b_rows.astype(BF16)
    c_cols = c_rows.T
    for j in range(2):
        span = slice(j * CHUNK, (j + 1) * CHUNK)
        ids = idc_ref[span, :]
        live_ref[span, :] = jnp.where(ids == 0.0, c_cols[span, :], 0.0).astype(BF16)
        scores = mm(c_cols[span, :].astype(BF16), b_rows[:, span])
        square = (CHUNK, CHUNK)
        wide = jnp.concatenate([ids] * (CHUNK // 128), axis=1)
        keep = (iota(square, 0) >= iota(square, 1)) & (wide == idr_ref[:1, span])
        g_ref[j] = jnp.where(keep, scores, 0.0).astype(BF16)
    before = idr_ref[:1, CHUNK - 1 : CHUNK]
    ids = idc_ref[CHUNK:, :]
    carried_ref[...] = jnp.where(ids == before, c_cols[CHUNK:, :], 0.0).astype(BF16)


def local_kernel(low, xs_ref, edge_ref, g_ref, carried_ref, ending_ref, eps_ref, rows_ref, z_ref, y_ref, dec_ref):
    heads = eps_ref.shape[1] // 2
    for block in range(xs_ref.shape[1] // WIDE):
        start = low + block * WIDE
        here = slice(block * WIDE, (block + 1) * WIDE)
        cols = slice(start, start + WIDE)
        spread = spread_matrix(2, heads, start, WIDE)
        values = opening(xs_ref, edge_ref, here, cols)
        middle = (mm(ending_ref[...], values) * rows_ref[0:1, cols]).astype(BF16)
        for j in range(2):
            span = slice(j * CHUNK, (j + 1) * CHUNK)
            if j == 0:
                y = mm(g_ref[0], values)
            else:
                y = mm(g_ref[1], xs_ref[span, here]) + mm(carried_ref[...], middle)
            half = 0.5 * z_ref[span, cols].astype(F32)
            gate = (half + half * jnp.tanh(half)) * mm(eps_ref[span, :], spread)
            y_ref[span, here] = y * gate
            dec_ref[span, here] = rows_ref[3 + j : 4 + j, cols] * gate


def final_kernel(low, state_ref, y_ref, dec_ref, live_ref, gain_ref, *refs):
    out_ref, buffer, sem = refs[-3:]
    square = (WIDE, WIDE)
    same = iota(square, 0) // HDIM == iota(square, 1) // HDIM
    mean_matrix = jnp.where(same, 1.0 / HDIM, 0.0).astype(BF16)
    copies = []
    for block in range(y_ref.shape[1] // WIDE):
        here = slice(block * WIDE, (block + 1) * WIDE)
        cols = slice(low + block * WIDE, low + (block + 1) * WIDE)
        gain = gain_ref[:, cols].astype(F32)
        for j in range(2):
            span = slice(j * CHUNK, (j + 1) * CHUNK)
            mixed = y_ref[span, here] + mm(live_ref[span, :], state_ref[:DSTATE, here]) * dec_ref[span, here]
            mean = mm((mixed * mixed).astype(BF16), mean_matrix)
            buffer[block, span, :] = (mixed * lax.rsqrt(mean + 1e-05) * gain).astype(BF16)
        copy = pltpu.make_async_copy(buffer.at[block], out_ref.at[:, cols], sem.at[block])
        copy.start()
        copies.append(copy)
    for copy in copies:
        copy.wait()


def on_device(x_in, z_in, bc_in, dt, decay_scale, conv_x, conv_bc, norm_gain, doc_start):
    rows, columns = x_in.shape
    heads = dt.shape[1]
    bc_width = bc_in.shape[1]
    turns = lax.axis_size("ctx") // 8
    split = lax.axis_size("head")
    starts = doc_start.reshape(1, rows)
    spec = pl.BlockSpec(memory_space=pltpu.VMEM)
    smem = pl.BlockSpec(memory_space=pltpu.SMEM)
    hbm = pl.BlockSpec(memory_space=pltpu.HBM)
    shape = jax.ShapeDtypeStruct
    in_hbm = lambda value: pltpu.with_memory_space_constraint(value, pltpu.HBM)
    own, starts, steps, scale, taps = call(
        bc_kernel,
        [hbm] * 6,
        [
            shape((bc_width + 8, rows), BF16),
            shape((1, rows), jnp.int32),
            shape((heads, rows), F32),
            shape((1, heads), F32),
            shape((CONV, columns), BF16),
        ],
        [
            pltpu.VMEM((bc_width, rows), BF16),
            pltpu.VMEM((CONV, bc_width), BF16),
            pltpu.SemaphoreType.DMA((6,)),
        ],
        "bc",
    )(
        in_hbm(bc_in.T),
        in_hbm(conv_bc),
        in_hbm(starts),
        in_hbm(dt.T),
        in_hbm(decay_scale.reshape(1, heads)),
        in_hbm(conv_x),
    )
    shares = [own] + [crossed(own, "head", mask) for mask in range(1, split)]
    fac, eps, table, ids_col, ids_row, x_near = call(
        prep_kernel,
        [spec] * 3 + [hbm],
        [
            shape((rows, 2 * heads), BF16),
            shape((rows, 2 * heads), BF16),
            shape((8, columns), F32),
            shape((rows, 128), F32),
            shape((8, rows), F32),
            shape((rows, columns), BF16),
        ],
        [pltpu.SemaphoreType.DMA],
        "prep",
    )(steps, scale, starts, in_hbm(x_in))
    flag = (lax.axis_index("head") < split // 2).astype(jnp.int32).reshape(1, 1)
    total = sum(SHARES)
    widths = [columns * share // total for share in SHARES]
    lows = [sum(widths[:group]) for group in range(len(widths))]
    state_type = BF16 if turns == 1 else F32
    gain = norm_gain.reshape(1, columns)
    extra = rim_rows(columns, split, widths[0])

    def fixed(rim):
        return call(
            fix_kernel,
            [spec] * (5 + split),
            [shape((2 * DSTATE, 128), BF16), shape((EDGE, columns), BF16)],
            (),
            "fix",
        )(x_near, rim, taps, fac, ids_col, *shares)

    edges = []
    if turns > 1:
        tail = call(tail_kernel, [spec] * (2 + split), shape((extra, widths[0]), BF16), (), "tail")
        edges = fixed(shifted(tail(x_near, starts, *shares), "ctx", 1))

    def relay(low, width, end):
        if turns == 1:
            return shifted(end, "ctx", 1)
        through = table[5:6, low : low + width]
        turn = lambda _, incoming: shifted(through * incoming + end, "ctx", 1)
        return lax.fori_loop(0, turns, turn, jnp.zeros_like(end)).astype(BF16)

    values, incoming = [], []
    for low, width in zip(lows, widths):
        part = call(
            functools.partial(conv_kernel, low),
            [spec] * 4,
            shape((rows, width), BF16),
            [pltpu.VMEM((rows + 8, 128), F32), pltpu.VMEM((CONV - 1, rows, 128), F32)],
            f"conv{low}",
        )(x_near, taps, fac, ids_col)
        carries = turns == 1 and low == 0
        others = [x_near, starts] if carries else edges
        end = call(
            functools.partial(state_kernel, low, split, carries),
            [smem] + [spec] * (split + 3 + len(others)),
            shape((DSTATE + extra if carries else DSTATE, width), state_type),
            (),
            f"state{low}",
        )(flag, *shares, part, table, ids_row, *others)
        values.append(part)
        incoming.append(relay(low, width, end))
    edge_bc, edge_x = edges or fixed(incoming[0])
    scores, live, carried, ended = call(
        functools.partial(score_kernel, split),
        [smem] + [spec] * (split + 3),
        [
            shape((2, CHUNK, CHUNK), BF16),
            shape((rows, DSTATE), BF16),
            shape((CHUNK, DSTATE), BF16),
            shape((DSTATE, CHUNK), BF16),
        ],
        (),
        "score",
    )(flag, *shares, edge_bc, ids_col, ids_row)
    out = None
    for group, (low, width) in enumerate(zip(lows, widths)):
        mixed, decay = call(
            functools.partial(local_kernel, low),
            [spec] * 8,
            [shape((rows, width), F32)] * 2,
            (),
            f"local{low}",
        )(values[group], edge_x, scores, carried, ended, eps, table, z_in)
        blocks = width // WIDE
        args = [incoming[group], mixed, decay, live, gain]
        in_specs = [spec] * 5
        if group > 0:
            args.append(out)
            in_specs.append(hbm)
        out = call(
            functools.partial(final_kernel, low),
            in_specs,
            shape((rows, columns), BF16),
            [pltpu.VMEM((blocks, rows, WIDE), BF16), pltpu.SemaphoreType.DMA((blocks,))],
            f"final{low}",
            hbm,
            {5: 0} if group > 0 else {},
        )(*args)
    return out


def solution(mesh):
    in_specs = (
        P("ctx", "head"),
        P("ctx", "head"),
        P("ctx", "head"),
        P("ctx", "head"),
        P("head"),
        P(None, "head"),
        P(None, "head"),
        P("head"),
        P("ctx"),
    )
    out_specs = P("ctx", "head")
    return jax.shard_map(
        on_device, mesh=mesh, in_specs=in_specs, out_specs=out_specs, check_vma=False
    )
```

```python
import functools

import jax
import jax.numpy as jnp
from jax import lax
from jax.experimental import pallas as pl
from jax.experimental.pallas import tpu as pltpu
from jax.sharding import PartitionSpec as P

HDIM = 64
HDIM_BITS = 6
DSTATE = 128
CONV = 4
CHUNK = 256
WIDE = 256
SHARES = (4, 2, 2)
EDGE = 16
F32 = jnp.float32
BF16 = jnp.bfloat16


def shifted(value, axis, steps):
    count = lax.axis_size(axis)
    pairs = [(source, (source + steps) % count) for source in range(count)]
    return lax.ppermute(value, axis, pairs)


def crossed(value, axis, mask):
    count = lax.axis_size(axis)
    return lax.ppermute(value, axis, [(source, source ^ mask) for source in range(count)])


def iota(shape, dim):
    return lax.broadcasted_iota(jnp.int32, shape, dim)


def mm(a, b):
    return jnp.dot(a, b, preferred_element_type=F32)


def mm_t(a, b):
    return lax.dot_general(a, b, (((1,), (1,)), ((), ())), preferred_element_type=F32)


def parts(value, count, axis=1):
    pieces = []
    for _ in range(count):
        piece = value.astype(BF16)
        pieces.append(piece)
        value = value - piece.astype(F32)
    return jnp.concatenate(pieces, axis=axis)


def spread_matrix(copies, heads, low, width):
    shape = (copies * heads, width)
    head = iota(shape, 0) & (heads - 1)
    return jnp.where(head == (iota(shape, 1) + low) >> HDIM_BITS, 1.0, 0.0).astype(BF16)


def call(kernel, in_specs, outs, scratch, name, out_spec=None, alias=None, limit=12):
    spec = out_spec or pl.BlockSpec(memory_space=pltpu.VMEM)
    return pl.pallas_call(
        kernel,
        out_shape=outs,
        in_specs=in_specs,
        out_specs=[spec] * len(outs) if isinstance(outs, list) else spec,
        scratch_shapes=list(scratch),
        input_output_aliases=alias or {},
        compiler_params=pltpu.CompilerParams(vmem_limit_bytes=limit << 20),
        name=name,
    )


def rim_rows(columns, split, width):
    slots = columns // width + -(-128 * split // width)
    return -(-3 * slots // 16) * 16


def rim_block(x_ref, start_ref, shares, width):
    rows, columns = x_ref.shape
    total = rim_rows(columns, len(shares), width)
    starts = start_ref[:, rows - 128 :].astype(F32)
    last = starts[:, 127:128]
    before = jnp.maximum(last, starts[:, 126:127])
    row = iota((8, 128), 0)
    kept = jnp.where(row == 5, 1.0 - before, jnp.where(row == 6, 1.0 - last, 1.0))
    kept = jnp.where(row >= 5, kept, 0.0)
    kept = jnp.concatenate([kept] * (width // 128), axis=1)
    row = iota((8, width), 0)
    block = jnp.zeros((total, width), F32)
    below = jnp.zeros((total - 8, width), F32)
    slot = 0
    for low in range(0, columns, width):
        piece = x_ref[rows - 8 :, low : low + width].astype(F32) * kept
        piece = jnp.concatenate([piece, below], axis=0)
        block = block + pltpu.roll(piece, (slot - 5) % total, 0)
        slot += 3
    count = width // 128
    for index in range(0, len(shares), count):
        piece = [share[share.shape[0] - 8 :, :128] for share in shares[index : index + count]]
        gap = width - 128 * len(piece)
        piece += [jnp.zeros((8, gap), BF16)] if gap else []
        piece = jnp.concatenate(piece, axis=1).astype(F32)
        piece = jnp.where((row >= 3) & (row < 6), piece, 0.0)
        piece = jnp.concatenate([piece, below], axis=0)
        block = block + pltpu.roll(piece, (slot - 3) % total, 0)
        slot += 3
    return block.astype(BF16)


def tail_kernel(x_ref, start_ref, *refs):
    refs[-1][...] = rim_block(x_ref, start_ref, refs[:-1], refs[-1].shape[1])


def prep_kernel(dt_ref, scale_ref, start_ref, x_hbm, *refs):
    fac_ref, eps_ref, inv_ref, rows_ref, idc_ref, idr_ref, x_ref, sem = refs
    copy = pltpu.make_async_copy(x_hbm, x_ref, sem)
    copy.start()
    heads = dt_ref.shape[0]
    square = (CHUNK, CHUNK)
    lower = jnp.where(iota(square, 0) >= iota(square, 1), 1.0, 0.0).astype(BF16)
    upper = jnp.where(iota(square, 0) <= iota(square, 1), 1.0, 0.0).astype(BF16)
    mids = []
    offset = jnp.zeros((8, 1), F32)
    for j in range(2):
        span = slice(j * CHUNK, (j + 1) * CHUNK)
        sums = mm_t(lower, parts(dt_ref[:, span], 3, 0))
        sums = sums[:, :heads] + sums[:, heads : 2 * heads] + sums[:, 2 * heads :]
        log_decay = -(sums * scale_ref[...])
        mid = 0.5 * log_decay[CHUNK - 1 : CHUNK, :]
        mids.append(mid)
        fac_ref[span, :] = parts(jnp.exp(mid - log_decay), 2)
        eps_ref[span, :] = parts(jnp.exp(log_decay - mid), 2)
        if j == 0:
            inv_ref[...] = parts(jnp.exp(-log_decay[:EDGE, :]), 2)
        starts = start_ref[:, span].astype(F32).astype(BF16)
        by_row = mm(jnp.broadcast_to(starts, (8, CHUNK)), upper) + offset
        by_col = mm_t(lower, jnp.broadcast_to(starts, (128, CHUNK)))
        idr_ref[:, span] = by_row
        idc_ref[span, :] = by_col + offset[:1, :]
        offset = by_row[:, CHUNK - 1 : CHUNK]
    middle = idr_ref[:1, CHUNK - 1 : CHUNK]
    final = idr_ref[:1, 2 * CHUNK - 1 : 2 * CHUNK]
    keep = jnp.where(middle == final, 1.0, 0.0)
    whole = jnp.where(final == 0.0, 1.0, 0.0)
    first, second = mids
    table = jnp.concatenate(
        [
            jnp.exp(first + second),
            jnp.exp(first + 2.0 * second) * keep,
            jnp.exp(second),
            jnp.exp(first),
            jnp.exp(2.0 * first + second),
            jnp.exp(2.0 * (first + second)) * whole,
            first,
            second,
        ],
        axis=0,
    )
    rows_ref[...] = mm(parts(table, 3), spread_matrix(3, heads, 0, rows_ref.shape[1]))
    copy.wait()


def bc_kernel(*refs):
    sources, (out_ref, *copied), (bc_ref, taps_ref, sems) = refs[:6], refs[6:11], refs[11:]
    width, rows = bc_ref.shape
    start_ref = copied[0]
    copies = [
        pltpu.make_async_copy(source, target, sems.at[index])
        for index, (source, target) in enumerate(zip(sources, [bc_ref, taps_ref, *copied]))
    ]
    for copy in copies:
        copy.start()
    for copy in copies[:3]:
        copy.wait()
    values = jnp.concatenate([jnp.zeros((width, 128), F32), bc_ref[...].astype(F32)], axis=1)
    starts = jnp.broadcast_to(start_ref[...].astype(F32), (8, rows))
    open_ = jnp.concatenate([jnp.ones((8, 128), F32), 1.0 - starts], axis=1)
    taps = jnp.concatenate([taps_ref[...].astype(F32)] * 2, axis=0).T
    total = values[:, 128:] * taps[:, CONV - 1 : CONV]
    kept = open_
    for back in range(1, CONV):
        if back > 1:
            kept = kept * pltpu.roll(open_, back - 1, 1)
        piece = pltpu.roll(values, back, 1)[:, 128:] * kept[:1, 128:]
        total = total + piece * taps[:, CONV - 1 - back : CONV - back]
    out_ref[:width, :] = (total / (1.0 + jnp.exp(-total))).astype(BF16)
    lane = iota((1, 128), 1)
    last = open_[:1, rows:]
    near, far = last[:, 127:128], last[:, 126:127]
    kept = jnp.where(lane == 125, near * far, jnp.where(lane == 126, near, 1.0))
    ends = jnp.where(lane >= 125, kept, 0.0) * values[:, rows:]
    after = jnp.zeros((width, 128), F32)
    for back in range(1, CONV):
        after = after + pltpu.roll(ends, back, 1) * taps[:, CONV - 1 - back : CONV - back]
    table = jnp.where(lane < 3, total[:, :128], pltpu.roll(after, 3, 1))
    table = jnp.where(lane < 6, table, 0.0).T[:8, :]
    high = table.astype(BF16)
    low = (table - high.astype(F32)).astype(BF16)
    gap = [jnp.zeros((8, 64 - width), BF16)] if width < 64 else []
    out_ref[width:, :128] = jnp.concatenate([high, *gap, low, *gap], axis=1)
    out_ref[width:, 128:] = jnp.zeros((8, rows - 128), BF16)
    for copy in copies[3:]:
        copy.wait()


def fix_kernel(split, flag_ref, x_ref, rim_ref, taps_ref, fac_ref, inv_ref, idc_ref, old_ref, *refs):
    shares, (live_ref, xe_ref, *exact) = refs[:split], refs[split:]
    rows, columns = x_ref.shape
    heads = fac_ref.shape[1] // 2
    width = shares[0].shape[0] - 8
    depth = rim_rows(columns, split, rim_ref.shape[1])
    base = rim_ref.shape[0] - depth

    def rim(low, size, row):
        slot, lane = low // rim_ref.shape[1], low % rim_ref.shape[1]
        block = rim_ref[base:, lane : lane + size].astype(F32)
        return pltpu.roll(block, (row - 3 * slot) % depth, 0)[:8]

    live = idc_ref[:8, :] == 0.0
    row, lane = iota((8, 128), 0), iota((width, 128), 1)
    firsts = []
    for index, share in enumerate(shares):
        own = share[width:, :128].astype(F32)
        total = own + jnp.where(live, rim(columns + index * 128, 128, 0), 0.0)
        total = total + pltpu.roll(total, 64, 1)
        value = total / (1.0 + jnp.exp(-total))
        firsts.append(value[:, :width])
        if exact:
            value = jnp.concatenate([value, jnp.zeros((120, 128), F32)], axis=0).T[:width, :]
            first = jnp.where(lane < 3, value, share[:width, :128].astype(F32))
            exact[0][index * width : (index + 1) * width, :] = first.astype(BF16)
    near = jnp.concatenate(firsts[: split // 2], axis=1)
    far = jnp.concatenate(firsts[split // 2 :], axis=1)
    own = flag_ref[0, 0] == 1
    b_edge, c_edge = jnp.where(own, near, far), jnp.where(own, far, near)
    b_edge = jnp.where((row < 3) & live, b_edge, 0.0)
    b_edge = jnp.concatenate([b_edge, jnp.zeros((120, DSTATE), F32)], axis=0).astype(BF16)
    old = old_ref[:EDGE, :].astype(F32)
    c_edge = jnp.where(row < 3, jnp.where(live, c_edge, 0.0), old[:8])
    c_edge = jnp.concatenate([c_edge, old[8:]], axis=0).astype(BF16)
    c_all = jnp.concatenate([c_edge, old_ref[EDGE:, :]], axis=0)
    live_ref[:, :DSTATE] = c_all
    ahead = (iota((rows, 128), 0) >= iota((rows, 128), 1)) & (iota((rows, 128), 1) < 3)
    live_ref[:, DSTATE:] = jnp.where(ahead, mm_t(c_all, b_edge), 0.0).astype(BF16)
    ids = jnp.concatenate([jnp.zeros((8, 128), F32), idc_ref[:EDGE, :]], axis=0)
    masks = []
    for back in range(1, CONV):
        same = pltpu.roll(ids, back, 0)[8:] == ids[8:]
        masks.append(jnp.concatenate([jnp.where(same, 1.0, 0.0)] * (WIDE // 128), axis=1))
    for low in range(0, columns, WIDE):
        cols = slice(low, low + WIDE)
        taps = 0.5 * taps_ref[:, cols].astype(F32)
        padded = jnp.concatenate([rim(low, WIDE, 5), x_ref[:EDGE, cols].astype(F32)], axis=0)
        half = padded[8:] * taps[CONV - 1 : CONV, :]
        for back in range(1, CONV):
            piece = pltpu.roll(padded, back, 0)[8:] * masks[back - 1]
            half = half + piece * taps[CONV - 1 - back : CONV - back, :]
        value = half + half * jnp.tanh(half)
        spread = spread_matrix(2, heads, low, WIDE)
        edge = jnp.where(iota(value.shape, 0) < 3, value * mm(inv_ref[...], spread), 0.0)
        xe_ref[:, cols] = edge.astype(BF16)
        if exact:
            exact[1][:, cols] = (value * mm(fac_ref[:EDGE, :], spread)).astype(BF16)


def conv_kernel(low, x_ref, taps_ref, fac_ref, idc_ref, out_ref, ids_ref, mask_ref):
    rows = x_ref.shape[0]
    heads = fac_ref.shape[1] // 2
    ids_ref[:8, :] = jnp.zeros((8, 128), F32)
    ids_ref[8:, :] = idc_ref[...]
    for back in range(1, CONV):
        same = ids_ref[pl.ds(8 - back, rows), :] == idc_ref[...]
        mask_ref[back - 1] = jnp.where(same, 1.0, 0.0)
    for block in range(out_ref.shape[1] // WIDE):
        start = low + block * WIDE
        cols = slice(start, start + WIDE)
        spread = spread_matrix(2, heads, start, WIDE)
        taps = 0.5 * taps_ref[:, cols].astype(F32)
        factor = mm(fac_ref[...], spread)
        size = 128
        for row in range(0, rows, size):
            span = slice(row, row + size)
            here = x_ref[span, cols].astype(F32)
            if row == 0:
                above = jnp.zeros((8, WIDE), F32)
            else:
                above = x_ref[row - 8 : row, cols].astype(F32)
            padded = jnp.concatenate([above, here], axis=0)
            half = here * taps[CONV - 1 : CONV, :]
            for back in range(1, CONV):
                mask = jnp.concatenate([mask_ref[back - 1, span, :]] * (WIDE // 128), axis=1)
                piece = pltpu.roll(padded, back, 0)[8:] * mask
                half = half + piece * taps[CONV - 1 - back : CONV - back, :]
            value = half + half * jnp.tanh(half)
            out_ref[span, block * WIDE : (block + 1) * WIDE] = (value * factor[span]).astype(BF16)


def pick(flag, refs, first=None):
    half = len(refs) // 2
    width = refs[0].shape[0] - 8
    near = jnp.concatenate([ref[:width, :] for ref in refs[:half]], axis=0).astype(F32)
    far = jnp.concatenate([ref[:width, :] for ref in refs[half:]], axis=0).astype(F32)
    if first is not None:
        edge = first[...].astype(F32)
        near = jnp.concatenate([edge[:DSTATE], near[:, 128:]], axis=1)
        far = jnp.concatenate([edge[DSTATE:], far[:, 128:]], axis=1)
    own = flag == 1
    return jnp.where(own, near, far), jnp.where(own, far, near)


def ending(b_rows, idr_ref, j):
    span = slice(j * CHUNK, (j + 1) * CHUNK)
    end = idr_ref[:1, (j + 1) * CHUNK - 1 : (j + 1) * CHUNK]
    return jnp.where(idr_ref[:1, span] == end, b_rows[:, span], 0.0).astype(BF16)


def state_kernel(low, split, carries, flag_ref, *refs):
    xs_ref, rows_ref, idr_ref, *edges, end_ref = refs[split:]
    if carries:
        x_ref, start_ref = edges
        edges = []
        end_ref[DSTATE:, :] = rim_block(x_ref, start_ref, refs[:split], end_ref.shape[1])
    b_rows, _ = pick(flag_ref[0, 0], refs[:split], edges[0] if edges else None)
    pieces = [ending(b_rows, idr_ref, j) for j in range(2)]
    for block in range(xs_ref.shape[1] // WIDE):
        here = slice(block * WIDE, (block + 1) * WIDE)
        cols = slice(low + block * WIDE, low + (block + 1) * WIDE)
        values = xs_ref[:CHUNK, here]
        if edges:
            values = jnp.concatenate([edges[1][:, cols], values[EDGE:]], axis=0)
        first = mm(pieces[0], values)
        second = mm(pieces[1], xs_ref[CHUNK:, here])
        end = first * rows_ref[1:2, cols] + second * rows_ref[2:3, cols]
        end_ref[:DSTATE, here] = end.astype(end_ref.dtype)


def score_kernel(split, flag_ref, *refs):
    idc_ref, idr_ref, g_ref, live_ref, carried_ref, ending_ref = refs[split:]
    b_rows, c_rows = pick(flag_ref[0, 0], refs[:split])
    rim = (iota((1, b_rows.shape[1]), 1) < 3) & (idr_ref[:1, :] == 0.0)
    b_rows = jnp.where(rim, 0.0, b_rows)
    ending_ref[...] = ending(b_rows, idr_ref, 0)
    b_rows = b_rows.astype(BF16)
    c_cols = c_rows.T
    for j in range(2):
        span = slice(j * CHUNK, (j + 1) * CHUNK)
        ids = idc_ref[span, :]
        live_ref[span, :] = jnp.where(ids == 0.0, c_cols[span, :], 0.0).astype(BF16)
        scores = mm(c_cols[span, :].astype(BF16), b_rows[:, span])
        square = (CHUNK, CHUNK)
        wide = jnp.concatenate([ids] * (CHUNK // 128), axis=1)
        keep = (iota(square, 0) >= iota(square, 1)) & (wide == idr_ref[:1, span])
        g_ref[j] = jnp.where(keep, scores, 0.0).astype(BF16)
    before = idr_ref[:1, CHUNK - 1 : CHUNK]
    ids = idc_ref[CHUNK:, :]
    carried_ref[...] = jnp.where(ids == before, c_cols[CHUNK:, :], 0.0).astype(BF16)


def local_kernel(low, xs_ref, g_ref, carried_ref, ending_ref, eps_ref, rows_ref, z_ref, y_ref, dec_ref):
    heads = eps_ref.shape[1] // 2
    for block in range(xs_ref.shape[1] // WIDE):
        start = low + block * WIDE
        here = slice(block * WIDE, (block + 1) * WIDE)
        cols = slice(start, start + WIDE)
        spread = spread_matrix(2, heads, start, WIDE)
        values = xs_ref[:CHUNK, here]
        middle = (mm(ending_ref[...], values) * rows_ref[0:1, cols]).astype(BF16)
        for j in range(2):
            span = slice(j * CHUNK, (j + 1) * CHUNK)
            if j == 0:
                y = mm(g_ref[0], values)
            else:
                y = mm(g_ref[1], xs_ref[span, here]) + mm(carried_ref[...], middle)
            half = 0.5 * z_ref[span, cols].astype(F32)
            gate = (half + half * jnp.tanh(half)) * mm(eps_ref[span, :], spread)
            y_ref[span, here] = y * gate
            dec_ref[span, here] = rows_ref[3 + j : 4 + j, cols] * gate


def final_kernel(low, state_ref, edge_ref, y_ref, dec_ref, live_ref, gain_ref, *refs):
    out_ref, buffer, sem = refs[-3:]
    square = (WIDE, WIDE)
    same = iota(square, 0) >> HDIM_BITS == iota(square, 1) >> HDIM_BITS
    mean_matrix = jnp.where(same, 1.0 / HDIM, 0.0).astype(BF16)
    empty = jnp.zeros((DSTATE - EDGE, WIDE), BF16)
    copies = []
    for block in range(y_ref.shape[1] // WIDE):
        here = slice(block * WIDE, (block + 1) * WIDE)
        cols = slice(low + block * WIDE, low + (block + 1) * WIDE)
        gain = gain_ref[:, cols].astype(F32)
        state = jnp.concatenate([state_ref[:DSTATE, here], edge_ref[:, cols], empty], axis=0)
        for j in range(2):
            span = slice(j * CHUNK, (j + 1) * CHUNK)
            mixed = y_ref[span, here] + mm(live_ref[span, :], state) * dec_ref[span, here]
            mean = mm((mixed * mixed).astype(BF16), mean_matrix)
            buffer[block, span, :] = (mixed * lax.rsqrt(mean + 1e-05) * gain).astype(BF16)
            copy = pltpu.make_async_copy(
                buffer.at[block, span], out_ref.at[span, cols], sem.at[block, j]
            )
            copy.start()
            copies.append(copy)
    for copy in copies:
        copy.wait()


def on_device(x_in, z_in, bc_in, dt, decay_scale, conv_x, conv_bc, norm_gain, doc_start):
    rows, columns = x_in.shape
    heads = dt.shape[1]
    bc_width = bc_in.shape[1]
    turns = lax.axis_size("ctx") // 8
    split = lax.axis_size("head")
    starts = doc_start.reshape(1, rows)
    spec = pl.BlockSpec(memory_space=pltpu.VMEM)
    smem = pl.BlockSpec(memory_space=pltpu.SMEM)
    hbm = pl.BlockSpec(memory_space=pltpu.HBM)
    shape = jax.ShapeDtypeStruct
    in_hbm = lambda value: pltpu.with_memory_space_constraint(value, pltpu.HBM)
    own, starts, steps, scale, taps = call(
        bc_kernel,
        [hbm] * 6,
        [
            shape((bc_width + 8, rows), BF16),
            shape((1, rows), jnp.int32),
            shape((heads, rows), F32),
            shape((1, heads), F32),
            shape((CONV, columns), BF16),
        ],
        [
            pltpu.VMEM((bc_width, rows), BF16),
            pltpu.VMEM((CONV, bc_width), BF16),
            pltpu.SemaphoreType.DMA((6,)),
        ],
        "bc",
    )(
        in_hbm(bc_in.T),
        in_hbm(conv_bc),
        in_hbm(starts),
        in_hbm(dt.T),
        in_hbm(decay_scale.reshape(1, heads)),
        in_hbm(conv_x),
    )
    shares = [own] + [crossed(own, "head", mask) for mask in range(1, split)]
    fac, eps, inv, table, ids_col, ids_row, x_near = call(
        prep_kernel,
        [spec] * 3 + [hbm],
        [
            shape((rows, 2 * heads), BF16),
            shape((rows, 2 * heads), BF16),
            shape((EDGE, 2 * heads), BF16),
            shape((8, columns), F32),
            shape((rows, 128), F32),
            shape((8, rows), F32),
            shape((rows, columns), BF16),
        ],
        [pltpu.SemaphoreType.DMA],
        "prep",
    )(steps, scale, starts, in_hbm(x_in))
    flag = (lax.axis_index("head") < split // 2).astype(jnp.int32).reshape(1, 1)
    total = sum(SHARES)
    widths = [columns * share // total for share in SHARES]
    lows = [sum(widths[:group]) for group in range(len(widths))]
    state_type = BF16 if turns == 1 else F32
    gain = norm_gain.reshape(1, columns)
    extra = rim_rows(columns, split, widths[0])

    score_shapes = [
        shape((2, CHUNK, CHUNK), BF16),
        shape((rows, DSTATE), BF16),
        shape((CHUNK, DSTATE), BF16),
        shape((DSTATE, CHUNK), BF16),
    ]
    scores, old, carried, ended = call(
        functools.partial(score_kernel, split), [smem] + [spec] * (split + 2), score_shapes, (), "score"
    )(flag, *shares, ids_col, ids_row)

    def fixed(rim):
        shapes = [shape((rows, 2 * DSTATE), BF16), shape((EDGE, columns), BF16)]
        if turns > 1:
            shapes += [shape((2 * DSTATE, 128), BF16), shape((EDGE, columns), BF16)]
        kernel = functools.partial(fix_kernel, split)
        return call(kernel, [smem] + [spec] * (7 + split), shapes, (), "fix")(
            flag, x_near, rim, taps, fac, inv, ids_col, old, *shares
        )

    edges = []
    if turns > 1:
        tail = call(tail_kernel, [spec] * (2 + split), shape((extra, widths[0]), BF16), (), "tail")
        live, edge, *edges = fixed(shifted(tail(x_near, starts, *shares), "ctx", 1))

    def relay(low, width, end):
        if turns == 1:
            return shifted(end, "ctx", 1)
        through = table[5:6, low : low + width]
        turn = lambda _, incoming: shifted(through * incoming + end, "ctx", 1)
        return lax.fori_loop(0, turns, turn, jnp.zeros_like(end)).astype(BF16)

    values, incoming = [], []
    for low, width in zip(lows, widths):
        part = call(
            functools.partial(conv_kernel, low),
            [spec] * 4,
            shape((rows, width), BF16),
            [pltpu.VMEM((rows + 8, 128), F32), pltpu.VMEM((CONV - 1, rows, 128), F32)],
            f"conv{low}",
        )(x_near, taps, fac, ids_col)
        carries = turns == 1 and low == 0
        others = [x_near, starts] if carries else edges
        end = call(
            functools.partial(state_kernel, low, split, carries),
            [smem] + [spec] * (split + 3 + len(others)),
            shape((DSTATE + extra if carries else DSTATE, width), state_type),
            (),
            f"state{low}",
        )(flag, *shares, part, table, ids_row, *others)
        values.append(part)
        incoming.append(relay(low, width, end))
    if turns == 1:
        live, edge = fixed(incoming[0])
    out = None
    for group, (low, width) in enumerate(zip(lows, widths)):
        mixed, decay = call(
            functools.partial(local_kernel, low),
            [spec] * 7,
            [shape((rows, width), F32)] * 2,
            (),
            f"local{low}",
        )(values[group], scores, carried, ended, eps, table, z_in)
        blocks = width // WIDE
        args = [incoming[group], edge, mixed, decay, live, gain]
        in_specs = [spec] * 6
        if group > 0:
            args.append(out)
            in_specs.append(hbm)
        out = call(
            functools.partial(final_kernel, low),
            in_specs,
            shape((rows, columns), BF16),
            [pltpu.VMEM((blocks, rows, WIDE), BF16), pltpu.SemaphoreType.DMA((blocks, 2))],
            f"final{low}",
            hbm,
            {6: 0} if group > 0 else {},
        )(*args)
    return out


def solution(mesh):
    in_specs = (
        P("ctx", "head"),
        P("ctx", "head"),
        P("ctx", "head"),
        P("ctx", "head"),
        P("head"),
        P(None, "head"),
        P(None, "head"),
        P("head"),
        P("ctx"),
    )
    out_specs = P("ctx", "head")
    return jax.shard_map(
        on_device, mesh=mesh, in_specs=in_specs, out_specs=out_specs, check_vma=False
    )
```

```python
import functools

import jax
import jax.numpy as jnp
from jax import lax
from jax.experimental import pallas as pl
from jax.experimental.pallas import tpu as pltpu
from jax.sharding import PartitionSpec as P

HDIM = 64
HDIM_BITS = 6
DSTATE = 128
CONV = 4
CHUNK = 256
WIDE = 256
PIECES = 4
GROUPS = ((0, 1), (2,), (3,))
EDGE = 16
F32 = jnp.float32
BF16 = jnp.bfloat16


def shifted(value, axis, steps):
    count = lax.axis_size(axis)
    pairs = [(source, (source + steps) % count) for source in range(count)]
    return lax.ppermute(value, axis, pairs)


def crossed(value, axis, mask):
    count = lax.axis_size(axis)
    return lax.ppermute(value, axis, [(source, source ^ mask) for source in range(count)])


def iota(shape, dim):
    return lax.broadcasted_iota(jnp.int32, shape, dim)


def mm(a, b):
    return jnp.dot(a, b, preferred_element_type=F32)


def mm_t(a, b):
    return lax.dot_general(a, b, (((1,), (1,)), ((), ())), preferred_element_type=F32)


def parts(value, count, axis=1):
    pieces = []
    for _ in range(count):
        piece = value.astype(BF16)
        pieces.append(piece)
        value = value - piece.astype(F32)
    return jnp.concatenate(pieces, axis=axis)


def spread_matrix(copies, heads, low, width):
    shape = (copies * heads, width)
    head = iota(shape, 0) & (heads - 1)
    return jnp.where(head == (iota(shape, 1) + low) >> HDIM_BITS, 1.0, 0.0).astype(BF16)


def call(kernel, in_specs, outs, scratch, name, out_spec=None, alias=None, limit=12):
    spec = out_spec or pl.BlockSpec(memory_space=pltpu.VMEM)
    return pl.pallas_call(
        kernel,
        out_shape=outs,
        in_specs=in_specs,
        out_specs=[spec] * len(outs) if isinstance(outs, list) else spec,
        scratch_shapes=list(scratch),
        input_output_aliases=alias or {},
        compiler_params=pltpu.CompilerParams(vmem_limit_bytes=limit << 20),
        name=name,
    )


def order_of(split):
    masks = [0]
    mask = split // 2
    while mask:
        masks += [held | mask for held in masks]
        mask //= 2
    return masks


def by_mask(refs, split):
    size = refs[0].shape[0] * 2 // split
    views = []
    for place in range(split):
        ref, row = refs[place * 2 // split], place % (split // 2) * size
        views.append(ref.at[row : row + size, :])
    order = order_of(split)
    return [views[order.index(mask)] for mask in range(split)]


def rim_rows(columns, split, width):
    slots = columns // width + -(-128 * split // width)
    return -(-3 * slots // 16) * 16


def rim_block(x_ref, start_ref, shares, width):
    rows, columns = x_ref.shape
    total = rim_rows(columns, len(shares), width)
    starts = start_ref[:, rows - 128 :].astype(F32)
    last = starts[:, 127:128]
    before = jnp.maximum(last, starts[:, 126:127])
    row = iota((8, 128), 0)
    kept = jnp.where(row == 5, 1.0 - before, jnp.where(row == 6, 1.0 - last, 1.0))
    kept = jnp.where(row >= 5, kept, 0.0)
    kept = jnp.concatenate([kept] * (width // 128), axis=1)
    row = iota((8, width), 0)
    block = jnp.zeros((total, width), F32)
    below = jnp.zeros((total - 8, width), F32)
    slot = 0
    for low in range(0, columns, width):
        piece = x_ref[rows - 8 :, low : low + width].astype(F32) * kept
        piece = jnp.concatenate([piece, below], axis=0)
        block = block + pltpu.roll(piece, (slot - 5) % total, 0)
        slot += 3
    count = width // 128
    for index in range(0, len(shares), count):
        piece = [share[share.shape[0] - 8 :, :128] for share in shares[index : index + count]]
        gap = width - 128 * len(piece)
        piece += [jnp.zeros((8, gap), BF16)] if gap else []
        piece = jnp.concatenate(piece, axis=1).astype(F32)
        piece = jnp.where((row >= 3) & (row < 6), piece, 0.0)
        piece = jnp.concatenate([piece, below], axis=0)
        block = block + pltpu.roll(piece, (slot - 3) % total, 0)
        slot += 3
    return block.astype(BF16)


def tail_kernel(split, x_ref, start_ref, *refs):
    shares = by_mask(refs[:2], split)
    refs[-1][...] = rim_block(x_ref, start_ref, shares, refs[-1].shape[1])


def prep_kernel(dt_ref, scale_ref, start_ref, x_hbm, *refs):
    fac_ref, eps_ref, inv_ref, rows_ref, idc_ref, idr_ref, x_ref, sem = refs
    copy = pltpu.make_async_copy(x_hbm, x_ref, sem)
    copy.start()
    heads = dt_ref.shape[0]
    square = (CHUNK, CHUNK)
    lower = jnp.where(iota(square, 0) >= iota(square, 1), 1.0, 0.0).astype(BF16)
    upper = jnp.where(iota(square, 0) <= iota(square, 1), 1.0, 0.0).astype(BF16)
    mids = []
    offset = jnp.zeros((8, 1), F32)
    for j in range(2):
        span = slice(j * CHUNK, (j + 1) * CHUNK)
        sums = mm_t(lower, parts(dt_ref[:, span], 3, 0))
        sums = sums[:, :heads] + sums[:, heads : 2 * heads] + sums[:, 2 * heads :]
        log_decay = -(sums * scale_ref[...])
        mid = 0.5 * log_decay[CHUNK - 1 : CHUNK, :]
        mids.append(mid)
        fac_ref[span, :] = parts(jnp.exp(mid - log_decay), 2)
        eps_ref[span, :] = parts(jnp.exp(log_decay - mid), 2)
        if j == 0:
            inv_ref[...] = parts(jnp.exp(-log_decay[:EDGE, :]), 2)
        starts = start_ref[:, span].astype(F32).astype(BF16)
        by_row = mm(jnp.broadcast_to(starts, (8, CHUNK)), upper) + offset
        by_col = mm_t(lower, jnp.broadcast_to(starts, (128, CHUNK)))
        idr_ref[:, span] = by_row
        idc_ref[span, :] = by_col + offset[:1, :]
        offset = by_row[:, CHUNK - 1 : CHUNK]
    middle = idr_ref[:1, CHUNK - 1 : CHUNK]
    final = idr_ref[:1, 2 * CHUNK - 1 : 2 * CHUNK]
    keep = jnp.where(middle == final, 1.0, 0.0)
    whole = jnp.where(final == 0.0, 1.0, 0.0)
    first, second = mids
    table = jnp.concatenate(
        [
            jnp.exp(first + second),
            jnp.exp(first + 2.0 * second) * keep,
            jnp.exp(second),
            jnp.exp(first),
            jnp.exp(2.0 * first + second),
            jnp.exp(2.0 * (first + second)) * whole,
            first,
            second,
        ],
        axis=0,
    )
    rows_ref[...] = mm(parts(table, 3), spread_matrix(3, heads, 0, rows_ref.shape[1]))
    copy.wait()


def bc_kernel(*refs):
    sources, (out_ref, *copied), (bc_ref, taps_ref, sems) = refs[:6], refs[6:11], refs[11:]
    width, rows = bc_ref.shape
    start_ref = copied[0]
    copies = [
        pltpu.make_async_copy(source, target, sems.at[index])
        for index, (source, target) in enumerate(zip(sources, [bc_ref, taps_ref, *copied]))
    ]
    for copy in copies:
        copy.start()
    for copy in copies[:3]:
        copy.wait()
    values = jnp.concatenate([jnp.zeros((width, 128), F32), bc_ref[...].astype(F32)], axis=1)
    starts = jnp.broadcast_to(start_ref[...].astype(F32), (8, rows))
    open_ = jnp.concatenate([jnp.ones((8, 128), F32), 1.0 - starts], axis=1)
    taps = jnp.concatenate([taps_ref[...].astype(F32)] * 2, axis=0).T
    total = values[:, 128:] * taps[:, CONV - 1 : CONV]
    kept = open_
    for back in range(1, CONV):
        if back > 1:
            kept = kept * pltpu.roll(open_, back - 1, 1)
        piece = pltpu.roll(values, back, 1)[:, 128:] * kept[:1, 128:]
        total = total + piece * taps[:, CONV - 1 - back : CONV - back]
    out_ref[:width, :] = (total / (1.0 + jnp.exp(-total))).astype(BF16)
    lane = iota((1, 128), 1)
    last = open_[:1, rows:]
    near, far = last[:, 127:128], last[:, 126:127]
    kept = jnp.where(lane == 125, near * far, jnp.where(lane == 126, near, 1.0))
    ends = jnp.where(lane >= 125, kept, 0.0) * values[:, rows:]
    after = jnp.zeros((width, 128), F32)
    for back in range(1, CONV):
        after = after + pltpu.roll(ends, back, 1) * taps[:, CONV - 1 - back : CONV - back]
    table = jnp.where(lane < 3, total[:, :128], pltpu.roll(after, 3, 1))
    table = jnp.where(lane < 6, table, 0.0).T[:8, :]
    high = table.astype(BF16)
    low = (table - high.astype(F32)).astype(BF16)
    gap = [jnp.zeros((8, 64 - width), BF16)] if width < 64 else []
    out_ref[width:, :128] = jnp.concatenate([high, *gap, low, *gap], axis=1)
    out_ref[width:, 128:] = jnp.zeros((8, rows - 128), BF16)
    for copy in copies[3:]:
        copy.wait()


def fix_kernel(split, x_ref, rim_ref, taps_ref, fac_ref, inv_ref, idc_ref, old_ref, *refs):
    shares, (live_ref, xe_ref, *exact) = by_mask(refs[:2], split), refs[2:]
    rows, columns = x_ref.shape
    heads = fac_ref.shape[1] // 2
    width = shares[0].shape[0] - 8
    depth = rim_rows(columns, split, rim_ref.shape[1])
    base = rim_ref.shape[0] - depth

    def rim(low, size, row):
        slot, lane = low // rim_ref.shape[1], low % rim_ref.shape[1]
        block = rim_ref[base:, lane : lane + size].astype(F32)
        return pltpu.roll(block, (row - 3 * slot) % depth, 0)[:8]

    live = idc_ref[:8, :] == 0.0
    row, lane = iota((8, 128), 0), iota((width, 128), 1)
    firsts = []
    for index, share in enumerate(shares):
        own = share[width:, :128].astype(F32)
        total = own + jnp.where(live, rim(columns + index * 128, 128, 0), 0.0)
        total = total + pltpu.roll(total, 64, 1)
        value = total / (1.0 + jnp.exp(-total))
        firsts.append(value[:, :width])
        if exact:
            value = jnp.concatenate([value, jnp.zeros((120, 128), F32)], axis=0).T[:width, :]
            first = jnp.where(lane < 3, value, share[:width, :128].astype(F32))
            exact[0][index * width : (index + 1) * width, :] = first.astype(BF16)
    near = jnp.concatenate(firsts[: split // 2], axis=1)
    far = jnp.concatenate(firsts[split // 2 :], axis=1)
    own = lax.axis_index("head") < split // 2
    b_edge, c_edge = jnp.where(own, near, far), jnp.where(own, far, near)
    b_edge = jnp.where((row < 3) & live, b_edge, 0.0)
    b_edge = jnp.concatenate([b_edge, jnp.zeros((120, DSTATE), F32)], axis=0).astype(BF16)
    old = old_ref[:EDGE, :].astype(F32)
    c_edge = jnp.where(row < 3, jnp.where(live, c_edge, 0.0), old[:8])
    c_edge = jnp.concatenate([c_edge, old[8:]], axis=0).astype(BF16)
    c_all = jnp.concatenate([c_edge, old_ref[EDGE:, :]], axis=0)
    live_ref[:, :DSTATE] = c_all
    ahead = (iota((rows, 128), 0) >= iota((rows, 128), 1)) & (iota((rows, 128), 1) < 3)
    live_ref[:, DSTATE:] = jnp.where(ahead, mm_t(c_all, b_edge), 0.0).astype(BF16)
    ids = jnp.concatenate([jnp.zeros((8, 128), F32), idc_ref[:EDGE, :]], axis=0)
    masks = []
    for back in range(1, CONV):
        same = pltpu.roll(ids, back, 0)[8:] == ids[8:]
        masks.append(jnp.concatenate([jnp.where(same, 1.0, 0.0)] * (WIDE // 128), axis=1))
    for low in range(0, columns, WIDE):
        cols = slice(low, low + WIDE)
        taps = 0.5 * taps_ref[:, cols].astype(F32)
        padded = jnp.concatenate([rim(low, WIDE, 5), x_ref[:EDGE, cols].astype(F32)], axis=0)
        half = padded[8:] * taps[CONV - 1 : CONV, :]
        for back in range(1, CONV):
            piece = pltpu.roll(padded, back, 0)[8:] * masks[back - 1]
            half = half + piece * taps[CONV - 1 - back : CONV - back, :]
        value = half + half * jnp.tanh(half)
        spread = spread_matrix(2, heads, low, WIDE)
        edge = jnp.where(iota(value.shape, 0) < 3, value * mm(inv_ref[...], spread), 0.0)
        xe_ref[:, cols] = edge.astype(BF16)
        if exact:
            exact[1][:, cols] = (value * mm(fac_ref[:EDGE, :], spread)).astype(BF16)


def conv_kernel(low, x_ref, taps_ref, fac_ref, idc_ref, *refs):
    out_ref, ids_ref, mask_ref = refs[-3:]
    if len(refs) > 3:
        out_ref = refs[1]
        refs[2][...] = refs[0][...]
    rows = x_ref.shape[0]
    heads = fac_ref.shape[1] // 2
    ids_ref[:8, :] = jnp.zeros((8, 128), F32)
    ids_ref[8:, :] = idc_ref[...]
    for back in range(1, CONV):
        same = ids_ref[pl.ds(8 - back, rows), :] == idc_ref[...]
        mask_ref[back - 1] = jnp.where(same, 1.0, 0.0)
    for block in range(out_ref.shape[1] // WIDE):
        start = low + block * WIDE
        cols = slice(start, start + WIDE)
        spread = spread_matrix(2, heads, start, WIDE)
        taps = 0.5 * taps_ref[:, cols].astype(F32)
        factor = mm(fac_ref[...], spread)
        size = 128
        for row in range(0, rows, size):
            span = slice(row, row + size)
            here = x_ref[span, cols].astype(F32)
            if row == 0:
                above = jnp.zeros((8, WIDE), F32)
            else:
                above = x_ref[row - 8 : row, cols].astype(F32)
            padded = jnp.concatenate([above, here], axis=0)
            half = here * taps[CONV - 1 : CONV, :]
            for back in range(1, CONV):
                mask = jnp.concatenate([mask_ref[back - 1, span, :]] * (WIDE // 128), axis=1)
                piece = pltpu.roll(padded, back, 0)[8:] * mask
                half = half + piece * taps[CONV - 1 - back : CONV - back, :]
            value = half + half * jnp.tanh(half)
            out_ref[span, block * WIDE : (block + 1) * WIDE] = (value * factor[span]).astype(BF16)


def pick(refs, first=None):
    half = len(refs) // 2
    width = refs[0].shape[0] - 8
    near = jnp.concatenate([ref[:width, :] for ref in refs[:half]], axis=0).astype(F32)
    far = jnp.concatenate([ref[:width, :] for ref in refs[half:]], axis=0).astype(F32)
    if first is not None:
        edge = first[...].astype(F32)
        near = jnp.concatenate([edge[:DSTATE], near[:, 128:]], axis=1)
        far = jnp.concatenate([edge[DSTATE:], far[:, 128:]], axis=1)
    own = lax.axis_index("head") < half
    return jnp.where(own, near, far), jnp.where(own, far, near)


def ending(b_rows, idr_ref, j):
    span = slice(j * CHUNK, (j + 1) * CHUNK)
    end = idr_ref[:1, (j + 1) * CHUNK - 1 : (j + 1) * CHUNK]
    return jnp.where(idr_ref[:1, span] == end, b_rows[:, span], 0.0).astype(BF16)


def state_kernel(low, split, count, carries, *refs):
    xs_refs = refs[2 : 2 + count]
    rows_ref, idr_ref, *edges, end_ref = refs[2 + count :]
    if carries:
        x_ref, start_ref = edges
        edges = []
        end_ref[DSTATE:, :] = rim_block(x_ref, start_ref, by_mask(refs[:2], split), end_ref.shape[1])
    b_rows, _ = pick(by_mask(refs[:2], split), edges[0] if edges else None)
    pieces = [ending(b_rows, idr_ref, j) for j in range(2)]
    each = xs_refs[0].shape[1] // WIDE
    for block in range(each * count):
        xs_ref, part = xs_refs[block // each], slice(block % each * WIDE, (block % each + 1) * WIDE)
        here = slice(block * WIDE, (block + 1) * WIDE)
        cols = slice(low + block * WIDE, low + (block + 1) * WIDE)
        values = xs_ref[:CHUNK, part]
        if edges:
            values = jnp.concatenate([edges[1][:, cols], values[EDGE:]], axis=0)
        first = mm(pieces[0], values)
        second = mm(pieces[1], xs_ref[CHUNK:, part])
        end = first * rows_ref[1:2, cols] + second * rows_ref[2:3, cols]
        end_ref[:DSTATE, here] = end.astype(end_ref.dtype)


def score_kernel(split, *refs):
    idc_ref, idr_ref, g_ref, live_ref, carried_ref, ending_ref = refs[2:]
    b_rows, c_rows = pick(by_mask(refs[:2], split))
    rim = (iota((1, b_rows.shape[1]), 1) < 3) & (idr_ref[:1, :] == 0.0)
    b_rows = jnp.where(rim, 0.0, b_rows)
    ending_ref[...] = ending(b_rows, idr_ref, 0)
    b_rows = b_rows.astype(BF16)
    c_cols = c_rows.T
    for j in range(2):
        span = slice(j * CHUNK, (j + 1) * CHUNK)
        ids = idc_ref[span, :]
        live_ref[span, :] = jnp.where(ids == 0.0, c_cols[span, :], 0.0).astype(BF16)
        scores = mm(c_cols[span, :].astype(BF16), b_rows[:, span])
        square = (CHUNK, CHUNK)
        wide = jnp.concatenate([ids] * (CHUNK // 128), axis=1)
        keep = (iota(square, 0) >= iota(square, 1)) & (wide == idr_ref[:1, span])
        g_ref[j] = jnp.where(keep, scores, 0.0).astype(BF16)
    before = idr_ref[:1, CHUNK - 1 : CHUNK]
    ids = idc_ref[CHUNK:, :]
    carried_ref[...] = jnp.where(ids == before, c_cols[CHUNK:, :], 0.0).astype(BF16)


def local_kernel(low, *refs):
    xs_refs = refs[:-8]
    g_ref, carried_ref, ending_ref, eps_ref, rows_ref, z_ref, y_ref, dec_ref = refs[-8:]
    heads = eps_ref.shape[1] // 2
    each = xs_refs[0].shape[1] // WIDE
    for block in range(each * len(xs_refs)):
        xs_ref, part = xs_refs[block // each], slice(block % each * WIDE, (block % each + 1) * WIDE)
        start = low + block * WIDE
        here = slice(block * WIDE, (block + 1) * WIDE)
        cols = slice(start, start + WIDE)
        spread = spread_matrix(2, heads, start, WIDE)
        values = xs_ref[:CHUNK, part]
        middle = (mm(ending_ref[...], values) * rows_ref[0:1, cols]).astype(BF16)
        for j in range(2):
            span = slice(j * CHUNK, (j + 1) * CHUNK)
            if j == 0:
                y = mm(g_ref[0], values)
            else:
                y = mm(g_ref[1], xs_ref[span, part]) + mm(carried_ref[...], middle)
            half = 0.5 * z_ref[span, cols].astype(F32)
            gate = (half + half * jnp.tanh(half)) * mm(eps_ref[span, :], spread)
            y_ref[span, here] = y * gate
            dec_ref[span, here] = rows_ref[3 + j : 4 + j, cols] * gate


def final_kernel(low, state_ref, edge_ref, y_ref, dec_ref, live_ref, gain_ref, *refs):
    out_ref, buffer, sem = refs[-3:]
    square = (WIDE, WIDE)
    same = iota(square, 0) >> HDIM_BITS == iota(square, 1) >> HDIM_BITS
    mean_matrix = jnp.where(same, 1.0 / HDIM, 0.0).astype(BF16)
    empty = jnp.zeros((DSTATE - EDGE, WIDE), BF16)
    copies = []
    for block in range(y_ref.shape[1] // WIDE):
        here = slice(block * WIDE, (block + 1) * WIDE)
        cols = slice(low + block * WIDE, low + (block + 1) * WIDE)
        gain = gain_ref[:, cols].astype(F32)
        state = jnp.concatenate([state_ref[:DSTATE, here], edge_ref[:, cols], empty], axis=0)
        for j in range(2):
            span = slice(j * CHUNK, (j + 1) * CHUNK)
            mixed = y_ref[span, here] + mm(live_ref[span, :], state) * dec_ref[span, here]
            mean = mm((mixed * mixed).astype(BF16), mean_matrix)
            buffer[block, span, :] = (mixed * lax.rsqrt(mean + 1e-05) * gain).astype(BF16)
            copy = pltpu.make_async_copy(
                buffer.at[block, span], out_ref.at[span, cols], sem.at[block, j]
            )
            copy.start()
            copies.append(copy)
    for copy in copies:
        copy.wait()


def on_device(x_in, z_in, bc_in, dt, decay_scale, conv_x, conv_bc, norm_gain, doc_start):
    rows, columns = x_in.shape
    heads = dt.shape[1]
    bc_width = bc_in.shape[1]
    turns = lax.axis_size("ctx") // 8
    split = lax.axis_size("head")
    starts = doc_start.reshape(1, rows)
    spec = pl.BlockSpec(memory_space=pltpu.VMEM)
    hbm = pl.BlockSpec(memory_space=pltpu.HBM)
    shape = jax.ShapeDtypeStruct
    in_hbm = lambda value: pltpu.with_memory_space_constraint(value, pltpu.HBM)
    own, starts, steps, scale, taps = call(
        bc_kernel,
        [hbm] * 6,
        [
            shape((bc_width + 8, rows), BF16),
            shape((1, rows), jnp.int32),
            shape((heads, rows), F32),
            shape((1, heads), F32),
            shape((CONV, columns), BF16),
        ],
        [
            pltpu.VMEM((bc_width, rows), BF16),
            pltpu.VMEM((CONV, bc_width), BF16),
            pltpu.SemaphoreType.DMA((6,)),
        ],
        "bc",
    )(
        in_hbm(bc_in.T),
        in_hbm(conv_bc),
        in_hbm(starts),
        in_hbm(dt.T),
        in_hbm(decay_scale.reshape(1, heads)),
        in_hbm(conv_x),
    )
    far = crossed(own, "head", split // 2)
    fac, eps, inv, table, ids_col, ids_row, x_near = call(
        prep_kernel,
        [spec] * 3 + [hbm],
        [
            shape((rows, 2 * heads), BF16),
            shape((rows, 2 * heads), BF16),
            shape((EDGE, 2 * heads), BF16),
            shape((8, columns), F32),
            shape((rows, 128), F32),
            shape((8, rows), F32),
            shape((rows, columns), BF16),
        ],
        [pltpu.SemaphoreType.DMA],
        "prep",
    )(steps, scale, starts, in_hbm(x_in))
    width = columns // PIECES
    values = []
    for piece in range(PIECES):
        kept = [own] if piece == 0 else []
        part, *kept = call(
            functools.partial(conv_kernel, piece * width),
            [spec] * (4 + len(kept)),
            [shape((rows, width), BF16)] + [shape(own.shape, BF16)] * len(kept),
            [pltpu.VMEM((rows + 8, 128), F32), pltpu.VMEM((CONV - 1, rows, 128), F32)],
            f"conv{piece}",
        )(x_near, taps, fac, ids_col, *kept)
        values.append(part)
        if piece == 0:
            ours, mask = jnp.concatenate([*kept, far], axis=0), split // 4
    while mask > 1:
        ours = jnp.concatenate([ours, crossed(ours, "head", mask)], axis=0)
        mask //= 2
    shares = [ours, crossed(ours, "head", 1)]
    widths = [width * len(group) for group in GROUPS]
    lows = [width * group[0] for group in GROUPS]
    state_type = BF16 if turns == 1 else F32
    gain = norm_gain.reshape(1, columns)
    extra = rim_rows(columns, split, widths[0])

    score_shapes = [
        shape((2, CHUNK, CHUNK), BF16),
        shape((rows, DSTATE), BF16),
        shape((CHUNK, DSTATE), BF16),
        shape((DSTATE, CHUNK), BF16),
    ]
    scores, old, carried, ended = call(
        functools.partial(score_kernel, split), [spec] * 4, score_shapes, (), "score"
    )(*shares, ids_col, ids_row)

    def fixed(rim):
        shapes = [shape((rows, 2 * DSTATE), BF16), shape((EDGE, columns), BF16)]
        if turns > 1:
            shapes += [shape((2 * DSTATE, 128), BF16), shape((EDGE, columns), BF16)]
        kernel = functools.partial(fix_kernel, split)
        return call(kernel, [spec] * 9, shapes, (), "fix")(
            x_near, rim, taps, fac, inv, ids_col, old, *shares
        )

    edges = []
    if turns > 1:
        kernel = functools.partial(tail_kernel, split)
        tail = call(kernel, [spec] * 4, shape((extra, widths[0]), BF16), (), "tail")
        live, edge, *edges = fixed(shifted(tail(x_near, starts, *shares), "ctx", 1))

    def relay(low, width, end):
        if turns == 1:
            return shifted(end, "ctx", 1)
        through = table[5:6, low : low + width]
        turn = lambda _, incoming: shifted(through * incoming + end, "ctx", 1)
        return lax.fori_loop(0, turns, turn, jnp.zeros_like(end)).astype(BF16)

    incoming = []
    for group, low, width in zip(GROUPS, lows, widths):
        pieces = [values[piece] for piece in group]
        carries = turns == 1 and low == 0
        others = [x_near, starts] if carries else edges
        end = call(
            functools.partial(state_kernel, low, split, len(pieces), carries),
            [spec] * (4 + len(pieces) + len(others)),
            shape((DSTATE + extra if carries else DSTATE, width), state_type),
            (),
            f"state{low}",
        )(*shares, *pieces, table, ids_row, *others)
        incoming.append(relay(low, width, end))
    if turns == 1:
        live, edge = fixed(incoming[0])
    out = None
    for group, (low, width) in enumerate(zip(lows, widths)):
        pieces = [values[piece] for piece in GROUPS[group]]
        mixed, decay = call(
            functools.partial(local_kernel, low),
            [spec] * (6 + len(pieces)),
            [shape((rows, width), F32)] * 2,
            (),
            f"local{low}",
        )(*pieces, scores, carried, ended, eps, table, z_in)
        blocks = width // WIDE
        args = [incoming[group], edge, mixed, decay, live, gain]
        in_specs = [spec] * 6
        if group > 0:
            args.append(out)
            in_specs.append(hbm)
        out = call(
            functools.partial(final_kernel, low),
            in_specs,
            shape((rows, columns), BF16),
            [pltpu.VMEM((blocks, rows, WIDE), BF16), pltpu.SemaphoreType.DMA((blocks, 2))],
            f"final{low}",
            hbm,
            {6: 0} if group > 0 else {},
        )(*args)
    return out


def solution(mesh):
    in_specs = (
        P("ctx", "head"),
        P("ctx", "head"),
        P("ctx", "head"),
        P("ctx", "head"),
        P("head"),
        P(None, "head"),
        P(None, "head"),
        P("head"),
        P("ctx"),
    )
    out_specs = P("ctx", "head")
    return jax.shard_map(
        on_device, mesh=mesh, in_specs=in_specs, out_specs=out_specs, check_vma=False
    )
```

```python
import functools

import jax
import jax.numpy as jnp
from jax import lax
from jax.experimental import pallas as pl
from jax.experimental.pallas import tpu as pltpu
from jax.sharding import PartitionSpec as P

HDIM = 64
HDIM_BITS = 6
DSTATE = 128
CONV = 4
CHUNK = 256
WIDE = 256
GROUPS = ((0, 1), (2,), (3,))
EDGE = 16
F32 = jnp.float32
BF16 = jnp.bfloat16


def shifted(value, axis, steps):
    count = lax.axis_size(axis)
    pairs = [(source, (source + steps) % count) for source in range(count)]
    return lax.ppermute(value, axis, pairs)


def crossed(value, axis, mask):
    count = lax.axis_size(axis)
    return lax.ppermute(value, axis, [(source, source ^ mask) for source in range(count)])


def iota(shape, dim):
    return lax.broadcasted_iota(jnp.int32, shape, dim)


def mm(a, b):
    return jnp.dot(a, b, preferred_element_type=F32)


def mm_t(a, b):
    return lax.dot_general(a, b, (((1,), (1,)), ((), ())), preferred_element_type=F32)


def parts(value, count, axis=1):
    pieces = []
    for _ in range(count):
        piece = value.astype(BF16)
        pieces.append(piece)
        value = value - piece.astype(F32)
    return jnp.concatenate(pieces, axis=axis)


def spread_matrix(copies, heads, low, width):
    shape = (copies * heads, width)
    head = iota(shape, 0) & (heads - 1)
    return jnp.where(head == (iota(shape, 1) + low) >> HDIM_BITS, 1.0, 0.0).astype(BF16)


def call(kernel, in_specs, outs, scratch, name, out_spec=None, alias=None, limit=12):
    spec = out_spec or pl.BlockSpec(memory_space=pltpu.VMEM)
    return pl.pallas_call(
        kernel,
        out_shape=outs,
        in_specs=in_specs,
        out_specs=[spec] * len(outs) if isinstance(outs, list) else spec,
        scratch_shapes=list(scratch),
        input_output_aliases=alias or {},
        compiler_params=pltpu.CompilerParams(vmem_limit_bytes=limit << 20),
        name=name,
    )


def order_of(split):
    masks = [0]
    mask = split // 2
    while mask:
        masks += [held | mask for held in masks]
        mask //= 2
    return masks


def by_mask(refs, split):
    size = refs[0].shape[0] * 2 // split
    views = []
    for place in range(split):
        ref, row = refs[place * 2 // split], place % (split // 2) * size
        views.append(ref.at[row : row + size, :])
    order = order_of(split)
    return [views[order.index(mask)] for mask in range(split)]


def rim_rows(columns, split, width):
    return -(-3 * (columns + 128 * split) // width // 8) * 8


def rim_place(columns, split, width, row, index):
    lane = row * 128 * split + index * 128
    return 3 * columns // width + lane // width, lane % width


def rim_block(x_ref, start_ref, shares, width):
    rows, columns = x_ref.shape
    split = len(shares)
    total = rim_rows(columns, split, width)
    starts = start_ref[:, rows - 128 :].astype(F32)
    last = starts[:, 127:128]
    before = jnp.maximum(last, starts[:, 126:127])
    row = iota((8, 128), 0)
    kept = jnp.where(row == 5, 1.0 - before, jnp.where(row == 6, 1.0 - last, 1.0))
    kept = jnp.where(row >= 5, kept, 0.0)
    kept = jnp.concatenate([kept] * (width // 128), axis=1)

    def placed(piece, shift, left=0):
        right = width - left - piece.shape[1]
        sides = [jnp.zeros((8, left), F32)] if left else []
        sides += [piece] + ([jnp.zeros((8, right), F32)] if right else [])
        piece = jnp.concatenate(sides, axis=1)
        if total > 8:
            piece = jnp.concatenate([piece, jnp.zeros((total - 8, width), F32)], axis=0)
        return pltpu.roll(piece, shift % total, 0) if shift % total else piece

    block = jnp.zeros((total, width), F32)
    for slot, low in enumerate(range(0, columns, width)):
        piece = x_ref[rows - 8 :, low : low + width].astype(F32) * kept
        block = block + placed(piece, 3 * slot - 5)
    count = min(width // 128, split)
    for first in range(0, split, count):
        piece = [share[share.shape[0] - 8 :, :128] for share in shares[first : first + count]]
        piece = jnp.concatenate(piece, axis=1).astype(F32)
        for each in range(3):
            own = jnp.where(iota(piece.shape, 0) == 3 + each, piece, 0.0)
            down, left = rim_place(columns, split, width, each, first)
            block = block + placed(own, down - 3 - each, left)
    return block.astype(BF16)


def tail_kernel(split, x_ref, start_ref, *refs):
    shares = by_mask(refs[:2], split)
    refs[-1][...] = rim_block(x_ref, start_ref, shares, refs[-1].shape[1])


def prep_kernel(dt_ref, scale_ref, start_ref, x_hbm, *refs):
    fac_ref, eps_ref, inv_ref, rows_ref, idc_ref, idr_ref, x_ref, sem = refs
    copy = pltpu.make_async_copy(x_hbm, x_ref, sem)
    copy.start()
    heads = dt_ref.shape[0]
    square = (CHUNK, CHUNK)
    lower = jnp.where(iota(square, 0) >= iota(square, 1), 1.0, 0.0).astype(BF16)
    upper = jnp.where(iota(square, 0) <= iota(square, 1), 1.0, 0.0).astype(BF16)
    mids = []
    offset = jnp.zeros((8, 1), F32)
    for j in range(2):
        span = slice(j * CHUNK, (j + 1) * CHUNK)
        sums = mm_t(lower, parts(dt_ref[:, span], 3, 0))
        sums = sums[:, :heads] + sums[:, heads : 2 * heads] + sums[:, 2 * heads :]
        log_decay = -(sums * scale_ref[...])
        mid = 0.5 * log_decay[CHUNK - 1 : CHUNK, :]
        mids.append(mid)
        fac_ref[span, :] = parts(jnp.exp(mid - log_decay), 2)
        eps_ref[span, :] = parts(jnp.exp(log_decay - mid), 2)
        if j == 0:
            inv_ref[...] = parts(jnp.exp(-log_decay[:EDGE, :]), 2)
        starts = start_ref[:, span].astype(F32).astype(BF16)
        by_row = mm(jnp.broadcast_to(starts, (8, CHUNK)), upper) + offset
        by_col = mm_t(lower, jnp.broadcast_to(starts, (128, CHUNK)))
        idr_ref[:, span] = by_row
        idc_ref[span, :] = by_col + offset[:1, :]
        offset = by_row[:, CHUNK - 1 : CHUNK]
    middle = idr_ref[:1, CHUNK - 1 : CHUNK]
    final = idr_ref[:1, 2 * CHUNK - 1 : 2 * CHUNK]
    keep = jnp.where(middle == final, 1.0, 0.0)
    whole = jnp.where(final == 0.0, 1.0, 0.0)
    first, second = mids
    table = jnp.concatenate(
        [
            jnp.exp(first + second),
            jnp.exp(first + 2.0 * second) * keep,
            jnp.exp(second),
            jnp.exp(first),
            jnp.exp(2.0 * first + second),
            jnp.exp(2.0 * (first + second)) * whole,
            first,
            second,
        ],
        axis=0,
    )
    rows_ref[...] = mm(parts(table, 3), spread_matrix(3, heads, 0, rows_ref.shape[1]))
    copy.wait()


def bc_kernel(*refs):
    sources, (out_ref, *copied), (bc_ref, taps_ref, sems) = refs[:6], refs[6:11], refs[11:]
    width, rows = bc_ref.shape
    start_ref = copied[0]
    copies = [
        pltpu.make_async_copy(source, target, sems.at[index])
        for index, (source, target) in enumerate(zip(sources, [bc_ref, taps_ref, *copied]))
    ]
    for copy in copies:
        copy.start()
    for copy in copies[:3]:
        copy.wait()
    values = jnp.concatenate([jnp.zeros((width, 128), F32), bc_ref[...].astype(F32)], axis=1)
    starts = jnp.broadcast_to(start_ref[...].astype(F32), (8, rows))
    open_ = jnp.concatenate([jnp.ones((8, 128), F32), 1.0 - starts], axis=1)
    taps = jnp.concatenate([taps_ref[...].astype(F32)] * 2, axis=0).T
    total = values[:, 128:] * taps[:, CONV - 1 : CONV]
    kept = open_
    for back in range(1, CONV):
        if back > 1:
            kept = kept * pltpu.roll(open_, back - 1, 1)
        piece = pltpu.roll(values, back, 1)[:, 128:] * kept[:1, 128:]
        total = total + piece * taps[:, CONV - 1 - back : CONV - back]
    half = 0.5 * total
    out_ref[:width, :] = (half + half * jnp.tanh(half)).astype(BF16)
    lane = iota((1, 128), 1)
    last = open_[:1, rows:]
    near, far = last[:, 127:128], last[:, 126:127]
    kept = jnp.where(lane == 125, near * far, jnp.where(lane == 126, near, 1.0))
    ends = jnp.where(lane >= 125, kept, 0.0) * values[:, rows:]
    after = jnp.zeros((width, 128), F32)
    for back in range(1, CONV):
        after = after + pltpu.roll(ends, back, 1) * taps[:, CONV - 1 - back : CONV - back]
    table = jnp.where(lane < 3, total[:, :128], pltpu.roll(after, 3, 1))
    table = jnp.where(lane < 6, table, 0.0).T[:8, :]
    high = table.astype(BF16)
    low = (table - high.astype(F32)).astype(BF16)
    gap = [jnp.zeros((8, 64 - width), BF16)] if width < 64 else []
    out_ref[width:, :128] = jnp.concatenate([high, *gap, low, *gap], axis=1)
    out_ref[width:, 128:] = jnp.zeros((8, rows - 128), BF16)
    for copy in copies[3:]:
        copy.wait()


def fix_kernel(split, x_ref, rim_ref, taps_ref, fac_ref, inv_ref, idc_ref, old_ref, *refs):
    shares, (live_ref, xe_ref, *exact) = by_mask(refs[:2], split), refs[2:]
    rows, columns = x_ref.shape
    heads = fac_ref.shape[1] // 2
    width = shares[0].shape[0] - 8
    depth = rim_rows(columns, split, rim_ref.shape[1])
    base = rim_ref.shape[0] - depth

    def moved(lane, size, shift):
        block = rim_ref[base:, lane : lane + size].astype(F32)
        return (pltpu.roll(block, shift % depth, 0) if shift % depth else block)[:8]

    live = idc_ref[:8, :] == 0.0
    row, lane = iota((8, 128), 0), iota((width, 128), 1)
    firsts = []
    for index, share in enumerate(shares):
        own = share[width:, :128].astype(F32)
        after = jnp.zeros((8, 128), F32)
        for each in range(3):
            down, left = rim_place(columns, split, rim_ref.shape[1], each, index)
            after = jnp.where(row == each, moved(left, 128, each - down), after)
        total = own + jnp.where(live, after, 0.0)
        total = total + pltpu.roll(total, 64, 1)
        value = total / (1.0 + jnp.exp(-total))
        firsts.append(value[:, :width])
        if exact:
            value = jnp.concatenate([value, jnp.zeros((120, 128), F32)], axis=0).T[:width, :]
            first = jnp.where(lane < 3, value, share[:width, :128].astype(F32))
            exact[0][index * width : (index + 1) * width, :] = first.astype(BF16)
    near = jnp.concatenate(firsts[: split // 2], axis=1)
    far = jnp.concatenate(firsts[split // 2 :], axis=1)
    own = lax.axis_index("head") < split // 2
    b_edge, c_edge = jnp.where(own, near, far), jnp.where(own, far, near)
    b_edge = jnp.where((row < 3) & live, b_edge, 0.0)
    b_edge = jnp.concatenate([b_edge, jnp.zeros((120, DSTATE), F32)], axis=0).astype(BF16)
    old = old_ref[:EDGE, :].astype(F32)
    c_edge = jnp.where(row < 3, jnp.where(live, c_edge, 0.0), old[:8])
    c_edge = jnp.concatenate([c_edge, old[8:]], axis=0).astype(BF16)
    c_all = jnp.concatenate([c_edge, old_ref[EDGE:, :]], axis=0)
    live_ref[:, :DSTATE] = c_all
    ahead = (iota((rows, 128), 0) >= iota((rows, 128), 1)) & (iota((rows, 128), 1) < 3)
    live_ref[:, DSTATE:] = jnp.where(ahead, mm_t(c_all, b_edge), 0.0).astype(BF16)
    ids = jnp.concatenate([jnp.zeros((8, 128), F32), idc_ref[:EDGE, :]], axis=0)
    masks = []
    for back in range(1, CONV):
        same = pltpu.roll(ids, back, 0)[8:] == ids[8:]
        masks.append(jnp.concatenate([jnp.where(same, 1.0, 0.0)] * (WIDE // 128), axis=1))
    for low in range(0, columns, WIDE):
        cols = slice(low, low + WIDE)
        taps = 0.5 * taps_ref[:, cols].astype(F32)
        slot, left = low // rim_ref.shape[1], low % rim_ref.shape[1]
        above = moved(left, WIDE, 5 - 3 * slot)
        padded = jnp.concatenate([above, x_ref[:EDGE, cols].astype(F32)], axis=0)
        half = padded[8:] * taps[CONV - 1 : CONV, :]
        for back in range(1, CONV):
            piece = pltpu.roll(padded, back, 0)[8:] * masks[back - 1]
            half = half + piece * taps[CONV - 1 - back : CONV - back, :]
        value = half + half * jnp.tanh(half)
        spread = spread_matrix(2, heads, low, WIDE)
        edge = jnp.where(iota(value.shape, 0) < 3, value * mm(inv_ref[...], spread), 0.0)
        xe_ref[:, cols] = edge.astype(BF16)
        if exact:
            exact[1][:, cols] = (value * mm(fac_ref[:EDGE, :], spread)).astype(BF16)


def conv_kernel(low, x_ref, taps_ref, fac_ref, idc_ref, *refs):
    out_ref, ids_ref, mask_ref = refs[-3:]
    if len(refs) > 3:
        out_ref = refs[1]
        refs[2][...] = refs[0][...]
    rows = x_ref.shape[0]
    heads = fac_ref.shape[1] // 2
    ids_ref[:8, :] = jnp.zeros((8, 128), F32)
    ids_ref[8:, :] = idc_ref[...]
    for back in range(1, CONV):
        same = ids_ref[pl.ds(8 - back, rows), :] == idc_ref[...]
        mask_ref[back - 1] = jnp.where(same, 1.0, 0.0)
    for block in range(out_ref.shape[1] // WIDE):
        start = low + block * WIDE
        cols = slice(start, start + WIDE)
        spread = spread_matrix(2, heads, start, WIDE)
        taps = 0.5 * taps_ref[:, cols].astype(F32)
        factor = mm(fac_ref[...], spread)
        size = 128
        for row in range(0, rows, size):
            span = slice(row, row + size)
            here = x_ref[span, cols].astype(F32)
            if row == 0:
                above = jnp.zeros((8, WIDE), F32)
            else:
                above = x_ref[row - 8 : row, cols].astype(F32)
            padded = jnp.concatenate([above, here], axis=0)
            half = here * taps[CONV - 1 : CONV, :]
            for back in range(1, CONV):
                mask = jnp.concatenate([mask_ref[back - 1, span, :]] * (WIDE // 128), axis=1)
                piece = pltpu.roll(padded, back, 0)[8:] * mask
                half = half + piece * taps[CONV - 1 - back : CONV - back, :]
            value = half + half * jnp.tanh(half)
            out_ref[span, block * WIDE : (block + 1) * WIDE] = (value * factor[span]).astype(BF16)


def pick(refs, first=None):
    half = len(refs) // 2
    width = refs[0].shape[0] - 8
    near = jnp.concatenate([ref[:width, :] for ref in refs[:half]], axis=0).astype(F32)
    far = jnp.concatenate([ref[:width, :] for ref in refs[half:]], axis=0).astype(F32)
    if first is not None:
        edge = first[...].astype(F32)
        near = jnp.concatenate([edge[:DSTATE], near[:, 128:]], axis=1)
        far = jnp.concatenate([edge[DSTATE:], far[:, 128:]], axis=1)
    own = lax.axis_index("head") < half
    return jnp.where(own, near, far), jnp.where(own, far, near)


def ending(b_rows, idr_ref, j):
    span = slice(j * CHUNK, (j + 1) * CHUNK)
    end = idr_ref[:1, (j + 1) * CHUNK - 1 : (j + 1) * CHUNK]
    return jnp.where(idr_ref[:1, span] == end, b_rows[:, span], 0.0).astype(BF16)


def state_kernel(low, split, count, carries, *refs):
    xs_refs = refs[2 : 2 + count]
    rows_ref, idr_ref, *edges, end_ref = refs[2 + count :]
    if carries:
        x_ref, start_ref = edges
        edges = []
        end_ref[DSTATE:, :] = rim_block(x_ref, start_ref, by_mask(refs[:2], split), end_ref.shape[1])
    b_rows, _ = pick(by_mask(refs[:2], split), edges[0] if edges else None)
    pieces = [ending(b_rows, idr_ref, j) for j in range(2)]
    each = xs_refs[0].shape[1] // WIDE
    for block in range(each * count):
        xs_ref, part = xs_refs[block // each], slice(block % each * WIDE, (block % each + 1) * WIDE)
        here = slice(block * WIDE, (block + 1) * WIDE)
        cols = slice(low + block * WIDE, low + (block + 1) * WIDE)
        values = xs_ref[:CHUNK, part]
        if edges:
            values = jnp.concatenate([edges[1][:, cols], values[EDGE:]], axis=0)
        first = mm(pieces[0], values)
        second = mm(pieces[1], xs_ref[CHUNK:, part])
        end = first * rows_ref[1:2, cols] + second * rows_ref[2:3, cols]
        end_ref[:DSTATE, here] = end.astype(end_ref.dtype)


def score_kernel(split, *refs):
    idc_ref, idr_ref, g_ref, live_ref, carried_ref, ending_ref = refs[2:]
    b_rows, c_rows = pick(by_mask(refs[:2], split))
    rim = (iota((1, b_rows.shape[1]), 1) < 3) & (idr_ref[:1, :] == 0.0)
    b_rows = jnp.where(rim, 0.0, b_rows)
    ending_ref[...] = ending(b_rows, idr_ref, 0)
    b_rows = b_rows.astype(BF16)
    c_cols = c_rows.T
    for j in range(2):
        span = slice(j * CHUNK, (j + 1) * CHUNK)
        ids = idc_ref[span, :]
        live_ref[span, :] = jnp.where(ids == 0.0, c_cols[span, :], 0.0).astype(BF16)
        scores = mm(c_cols[span, :].astype(BF16), b_rows[:, span])
        square = (CHUNK, CHUNK)
        wide = jnp.concatenate([ids] * (CHUNK // 128), axis=1)
        keep = (iota(square, 0) >= iota(square, 1)) & (wide == idr_ref[:1, span])
        g_ref[j] = jnp.where(keep, scores, 0.0).astype(BF16)
    before = idr_ref[:1, CHUNK - 1 : CHUNK]
    ids = idc_ref[CHUNK:, :]
    carried_ref[...] = jnp.where(ids == before, c_cols[CHUNK:, :], 0.0).astype(BF16)


def local_kernel(low, *refs):
    xs_refs = refs[:-8]
    g_ref, carried_ref, ending_ref, eps_ref, rows_ref, z_ref, y_ref, dec_ref = refs[-8:]
    heads = eps_ref.shape[1] // 2
    each = xs_refs[0].shape[1] // WIDE
    for block in range(each * len(xs_refs)):
        xs_ref, part = xs_refs[block // each], slice(block % each * WIDE, (block % each + 1) * WIDE)
        start = low + block * WIDE
        here = slice(block * WIDE, (block + 1) * WIDE)
        cols = slice(start, start + WIDE)
        spread = spread_matrix(2, heads, start, WIDE)
        values = xs_ref[:CHUNK, part]
        middle = (mm(ending_ref[...], values) * rows_ref[0:1, cols]).astype(BF16)
        for j in range(2):
            span = slice(j * CHUNK, (j + 1) * CHUNK)
            if j == 0:
                y = mm(g_ref[0], values)
            else:
                y = mm(g_ref[1], xs_ref[span, part]) + mm(carried_ref[...], middle)
            half = 0.5 * z_ref[span, cols].astype(F32)
            gate = (half + half * jnp.tanh(half)) * mm(eps_ref[span, :], spread)
            y_ref[span, here] = y * gate
            dec_ref[span, here] = rows_ref[3 + j : 4 + j, cols] * gate


def final_kernel(low, state_ref, edge_ref, y_ref, dec_ref, live_ref, gain_ref, *refs):
    out_ref, buffer, sem = refs[-3:]
    square = (WIDE, WIDE)
    same = iota(square, 0) >> HDIM_BITS == iota(square, 1) >> HDIM_BITS
    mean_matrix = jnp.where(same, 1.0 / HDIM, 0.0).astype(BF16)
    empty = jnp.zeros((DSTATE - EDGE, WIDE), BF16)
    copies = []
    for block in range(y_ref.shape[1] // WIDE):
        here = slice(block * WIDE, (block + 1) * WIDE)
        cols = slice(low + block * WIDE, low + (block + 1) * WIDE)
        gain = gain_ref[:, cols].astype(F32)
        state = jnp.concatenate([state_ref[:DSTATE, here], edge_ref[:, cols], empty], axis=0)
        for j in range(2):
            span = slice(j * CHUNK, (j + 1) * CHUNK)
            mixed = y_ref[span, here] + mm(live_ref[span, :], state) * dec_ref[span, here]
            mean = mm((mixed * mixed).astype(BF16), mean_matrix)
            buffer[block, span, :] = (mixed * lax.rsqrt(mean + 1e-05) * gain).astype(BF16)
            copy = pltpu.make_async_copy(
                buffer.at[block, span], out_ref.at[span, cols], sem.at[block, j]
            )
            copy.start()
            copies.append(copy)
    for copy in copies:
        copy.wait()


def on_device(x_in, z_in, bc_in, dt, decay_scale, conv_x, conv_bc, norm_gain, doc_start):
    rows, columns = x_in.shape
    heads = dt.shape[1]
    bc_width = bc_in.shape[1]
    turns = lax.axis_size("ctx") // 8
    split = lax.axis_size("head")
    starts = doc_start.reshape(1, rows)
    spec = pl.BlockSpec(memory_space=pltpu.VMEM)
    hbm = pl.BlockSpec(memory_space=pltpu.HBM)
    shape = jax.ShapeDtypeStruct
    in_hbm = lambda value: pltpu.with_memory_space_constraint(value, pltpu.HBM)
    own, starts, steps, scale, taps = call(
        bc_kernel,
        [hbm] * 6,
        [
            shape((bc_width + 8, rows), BF16),
            shape((1, rows), jnp.int32),
            shape((heads, rows), F32),
            shape((1, heads), F32),
            shape((CONV, columns), BF16),
        ],
        [
            pltpu.VMEM((bc_width, rows), BF16),
            pltpu.VMEM((CONV, bc_width), BF16),
            pltpu.SemaphoreType.DMA((6,)),
        ],
        "bc",
    )(
        in_hbm(bc_in.T),
        in_hbm(conv_bc),
        in_hbm(starts),
        in_hbm(dt.T),
        in_hbm(decay_scale.reshape(1, heads)),
        in_hbm(conv_x),
    )
    far = crossed(own, "head", split // 2)
    fac, eps, inv, table, ids_col, ids_row, x_near = call(
        prep_kernel,
        [spec] * 3 + [hbm],
        [
            shape((rows, 2 * heads), BF16),
            shape((rows, 2 * heads), BF16),
            shape((EDGE, 2 * heads), BF16),
            shape((8, columns), F32),
            shape((rows, 128), F32),
            shape((8, rows), F32),
            shape((rows, columns), BF16),
        ],
        [pltpu.SemaphoreType.DMA],
        "prep",
    )(steps, scale, starts, in_hbm(x_in))
    units = columns // WIDE
    sizes = [units // 4] * 4
    sizes = [WIDE * size for size in sizes]
    places = [sum(sizes[:piece]) for piece in range(len(sizes))]
    values = []
    for piece, (place, width) in enumerate(zip(places, sizes)):
        kept = [own] if piece == 0 else []
        part, *kept = call(
            functools.partial(conv_kernel, place),
            [spec] * (4 + len(kept)),
            [shape((rows, width), BF16)] + [shape(own.shape, BF16)] * len(kept),
            [pltpu.VMEM((rows + 8, 128), F32), pltpu.VMEM((CONV - 1, rows, 128), F32)],
            f"conv{piece}",
        )(x_near, taps, fac, ids_col, *kept)
        values.append(part)
        if piece == 0:
            ours, mask = jnp.concatenate([*kept, far], axis=0), split // 4
    while mask > 1:
        ours = jnp.concatenate([ours, crossed(ours, "head", mask)], axis=0)
        mask //= 2
    shares = [ours, crossed(ours, "head", 1)]
    widths = [sum(sizes[piece] for piece in group) for group in GROUPS]
    lows = [places[group[0]] for group in GROUPS]
    state_type = BF16 if turns == 1 else F32
    gain = norm_gain.reshape(1, columns)
    extra = rim_rows(columns, split, widths[0])

    score_shapes = [
        shape((2, CHUNK, CHUNK), BF16),
        shape((rows, DSTATE), BF16),
        shape((CHUNK, DSTATE), BF16),
        shape((DSTATE, CHUNK), BF16),
    ]
    scores, old, carried, ended = call(
        functools.partial(score_kernel, split), [spec] * 4, score_shapes, (), "score"
    )(*shares, ids_col, ids_row)

    def fixed(rim):
        shapes = [shape((rows, 2 * DSTATE), BF16), shape((EDGE, columns), BF16)]
        if turns > 1:
            shapes += [shape((2 * DSTATE, 128), BF16), shape((EDGE, columns), BF16)]
        kernel = functools.partial(fix_kernel, split)
        return call(kernel, [spec] * 9, shapes, (), "fix")(
            x_near, rim, taps, fac, inv, ids_col, old, *shares
        )

    edges = []
    if turns > 1:
        kernel = functools.partial(tail_kernel, split)
        tail = call(kernel, [spec] * 4, shape((extra, widths[0]), BF16), (), "tail")
        live, edge, *edges = fixed(shifted(tail(x_near, starts, *shares), "ctx", 1))

    def relay(low, width, end):
        if turns == 1:
            return shifted(end, "ctx", 1)
        through = table[5:6, low : low + width]
        turn = lambda _, incoming: shifted(through * incoming + end, "ctx", 1)
        return lax.fori_loop(0, turns, turn, jnp.zeros_like(end)).astype(BF16)

    incoming = []
    for group, low, width in zip(GROUPS, lows, widths):
        pieces = [values[piece] for piece in group]
        carries = turns == 1 and low == 0
        others = [x_near, starts] if carries else edges
        end = call(
            functools.partial(state_kernel, low, split, len(pieces), carries),
            [spec] * (4 + len(pieces) + len(others)),
            shape((DSTATE + extra if carries else DSTATE, width), state_type),
            (),
            f"state{low}",
        )(*shares, *pieces, table, ids_row, *others)
        incoming.append(relay(low, width, end))
    if turns == 1:
        live, edge = fixed(incoming[0])
    out = None
    for group, (low, width) in enumerate(zip(lows, widths)):
        pieces = [values[piece] for piece in GROUPS[group]]
        mixed, decay = call(
            functools.partial(local_kernel, low),
            [spec] * (6 + len(pieces)),
            [shape((rows, width), F32)] * 2,
            (),
            f"local{low}",
        )(*pieces, scores, carried, ended, eps, table, z_in)
        blocks = width // WIDE
        args = [incoming[group], edge, mixed, decay, live, gain]
        in_specs = [spec] * 6
        if group > 0:
            args.append(out)
            in_specs.append(hbm)
        out = call(
            functools.partial(final_kernel, low),
            in_specs,
            shape((rows, columns), BF16),
            [pltpu.VMEM((blocks, rows, WIDE), BF16), pltpu.SemaphoreType.DMA((blocks, 2))],
            f"final{low}",
            hbm,
            {6: 0} if group > 0 else {},
        )(*args)
    return out


def solution(mesh):
    in_specs = (
        P("ctx", "head"),
        P("ctx", "head"),
        P("ctx", "head"),
        P("ctx", "head"),
        P("head"),
        P(None, "head"),
        P(None, "head"),
        P("head"),
        P("ctx"),
    )
    out_specs = P("ctx", "head")
    return jax.shard_map(
        on_device, mesh=mesh, in_specs=in_specs, out_specs=out_specs, check_vma=False
    )
```

```python
import functools

import jax
import jax.numpy as jnp
from jax import lax
from jax.experimental import pallas as pl
from jax.experimental.pallas import tpu as pltpu
from jax.sharding import PartitionSpec as P

HDIM = 64
HDIM_BITS = 6
DSTATE = 128
CONV = 4
CHUNK = 256
WIDE = 256
GROUPS = ((0, 1), (2,), (3,))
EDGE = 16
F32 = jnp.float32
BF16 = jnp.bfloat16


def shifted(value, axis, steps):
    count = lax.axis_size(axis)
    pairs = [(source, (source + steps) % count) for source in range(count)]
    return lax.ppermute(value, axis, pairs)


def crossed(value, axis, mask):
    count = lax.axis_size(axis)
    return lax.ppermute(value, axis, [(source, source ^ mask) for source in range(count)])


def iota(shape, dim):
    return lax.broadcasted_iota(jnp.int32, shape, dim)


def mm(a, b):
    return jnp.dot(a, b, preferred_element_type=F32)


def mm_t(a, b):
    return lax.dot_general(a, b, (((1,), (1,)), ((), ())), preferred_element_type=F32)


def parts(value, count, axis=1):
    pieces = []
    for _ in range(count):
        piece = value.astype(BF16)
        pieces.append(piece)
        value = value - piece.astype(F32)
    return jnp.concatenate(pieces, axis=axis)


def spread_matrix(copies, heads, low, width):
    shape = (copies * heads, width)
    head = iota(shape, 0) & (heads - 1)
    return jnp.where(head == (iota(shape, 1) + low) >> HDIM_BITS, 1.0, 0.0).astype(BF16)


def call(kernel, in_specs, outs, scratch, name, out_spec=None, alias=None, limit=12):
    spec = out_spec or pl.BlockSpec(memory_space=pltpu.VMEM)
    return pl.pallas_call(
        kernel,
        out_shape=outs,
        in_specs=in_specs,
        out_specs=[spec] * len(outs) if isinstance(outs, list) else spec,
        scratch_shapes=list(scratch),
        input_output_aliases=alias or {},
        compiler_params=pltpu.CompilerParams(vmem_limit_bytes=limit << 20),
        name=name,
    )


def order_of(split):
    masks = [0]
    mask = split // 2
    while mask:
        masks += [held | mask for held in masks]
        mask //= 2
    return masks


def by_mask(refs, split):
    size = refs[0].shape[0] * 2 // split
    views = []
    for place in range(split):
        ref, row = refs[place * 2 // split], place % (split // 2) * size
        views.append(ref.at[row : row + size, :])
    order = order_of(split)
    return [views[order.index(mask)] for mask in range(split)]


def rim_rows(columns, split, width):
    return -(-3 * (columns + 128 * split) // width // 8) * 8


def rim_place(columns, split, width, row, index):
    lane = row * 128 * split + index * 128
    return 3 * columns // width + lane // width, lane % width


def rim_block(x_ref, start_ref, shares, width):
    rows, columns = x_ref.shape
    split = len(shares)
    total = rim_rows(columns, split, width)
    starts = start_ref[:, rows - 128 :].astype(F32)
    last = starts[:, 127:128]
    before = jnp.maximum(last, starts[:, 126:127])
    row = iota((8, 128), 0)
    kept = jnp.where(row == 5, 1.0 - before, jnp.where(row == 6, 1.0 - last, 1.0))
    kept = jnp.where(row >= 5, kept, 0.0)
    kept = jnp.concatenate([kept] * (width // 128), axis=1)

    def placed(piece, shift, left=0):
        right = width - left - piece.shape[1]
        sides = [jnp.zeros((8, left), F32)] if left else []
        sides += [piece] + ([jnp.zeros((8, right), F32)] if right else [])
        piece = jnp.concatenate(sides, axis=1)
        if total > 8:
            piece = jnp.concatenate([piece, jnp.zeros((total - 8, width), F32)], axis=0)
        return pltpu.roll(piece, shift % total, 0) if shift % total else piece

    block = jnp.zeros((total, width), F32)
    for slot, low in enumerate(range(0, columns, width)):
        piece = x_ref[rows - 8 :, low : low + width].astype(F32) * kept
        block = block + placed(piece, 3 * slot - 5)
    count = min(width // 128, split)
    for first in range(0, split, count):
        piece = [share[share.shape[0] - 8 :, :128] for share in shares[first : first + count]]
        piece = jnp.concatenate(piece, axis=1).astype(F32)
        for each in range(3):
            own = jnp.where(iota(piece.shape, 0) == 3 + each, piece, 0.0)
            down, left = rim_place(columns, split, width, each, first)
            block = block + placed(own, down - 3 - each, left)
    return block.astype(BF16)


def tail_kernel(split, x_ref, start_ref, *refs):
    shares = by_mask(refs[:2], split)
    refs[-1][...] = rim_block(x_ref, start_ref, shares, refs[-1].shape[1])


def prep_kernel(dt_ref, scale_ref, start_ref, x_hbm, *refs):
    fac_ref, eps_ref, inv_ref, rows_ref, idc_ref, idr_ref, x_ref, sem = refs
    copy = pltpu.make_async_copy(x_hbm, x_ref, sem)
    copy.start()
    heads = dt_ref.shape[0]
    square = (CHUNK, CHUNK)
    lower = jnp.where(iota(square, 0) >= iota(square, 1), 1.0, 0.0).astype(BF16)
    upper = jnp.where(iota(square, 0) <= iota(square, 1), 1.0, 0.0).astype(BF16)
    mids = []
    offset = jnp.zeros((8, 1), F32)
    for j in range(2):
        span = slice(j * CHUNK, (j + 1) * CHUNK)
        sums = mm_t(lower, parts(dt_ref[:, span], 3, 0))
        sums = sums[:, :heads] + sums[:, heads : 2 * heads] + sums[:, 2 * heads :]
        log_decay = -(sums * scale_ref[...])
        mid = 0.5 * log_decay[CHUNK - 1 : CHUNK, :]
        mids.append(mid)
        fac_ref[span, :] = parts(jnp.exp(mid - log_decay), 2)
        eps_ref[span, :] = parts(jnp.exp(log_decay - mid), 2)
        if j == 0:
            inv_ref[...] = parts(jnp.exp(-log_decay[:EDGE, :]), 2)
        starts = start_ref[:, span].astype(F32).astype(BF16)
        by_row = mm(jnp.broadcast_to(starts, (8, CHUNK)), upper) + offset
        by_col = mm_t(lower, jnp.broadcast_to(starts, (128, CHUNK)))
        idr_ref[:, span] = by_row
        idc_ref[span, :] = by_col + offset[:1, :]
        offset = by_row[:, CHUNK - 1 : CHUNK]
    middle = idr_ref[:1, CHUNK - 1 : CHUNK]
    final = idr_ref[:1, 2 * CHUNK - 1 : 2 * CHUNK]
    keep = jnp.where(middle == final, 1.0, 0.0)
    whole = jnp.where(final == 0.0, 1.0, 0.0)
    first, second = mids
    table = jnp.concatenate(
        [
            jnp.exp(first),
            jnp.exp(second),
            jnp.exp(2.0 * first),
            jnp.exp(2.0 * second) * keep,
            jnp.exp(2.0 * (first + second)) * whole,
            first,
            second,
            second,
        ],
        axis=0,
    )
    rows_ref[...] = mm(parts(table, 3), spread_matrix(3, heads, 0, rows_ref.shape[1]))
    copy.wait()


def bc_kernel(*refs):
    sources, (out_ref, *copied), (bc_ref, taps_ref, sems) = refs[:6], refs[6:11], refs[11:]
    width, rows = bc_ref.shape
    start_ref = copied[0]
    copies = [
        pltpu.make_async_copy(source, target, sems.at[index])
        for index, (source, target) in enumerate(zip(sources, [bc_ref, taps_ref, *copied]))
    ]
    for copy in copies:
        copy.start()
    for copy in copies[:3]:
        copy.wait()
    values = jnp.concatenate([jnp.zeros((width, 128), F32), bc_ref[...].astype(F32)], axis=1)
    starts = jnp.broadcast_to(start_ref[...].astype(F32), (8, rows))
    open_ = jnp.concatenate([jnp.ones((8, 128), F32), 1.0 - starts], axis=1)
    taps = jnp.concatenate([taps_ref[...].astype(F32)] * 2, axis=0).T
    total = values[:, 128:] * taps[:, CONV - 1 : CONV]
    kept = open_
    for back in range(1, CONV):
        if back > 1:
            kept = kept * pltpu.roll(open_, back - 1, 1)
        piece = pltpu.roll(values, back, 1)[:, 128:] * kept[:1, 128:]
        total = total + piece * taps[:, CONV - 1 - back : CONV - back]
    half = 0.5 * total
    out_ref[:width, :] = (half + half * jnp.tanh(half)).astype(BF16)
    lane = iota((1, 128), 1)
    last = open_[:1, rows:]
    near, far = last[:, 127:128], last[:, 126:127]
    kept = jnp.where(lane == 125, near * far, jnp.where(lane == 126, near, 1.0))
    ends = jnp.where(lane >= 125, kept, 0.0) * values[:, rows:]
    after = jnp.zeros((width, 128), F32)
    for back in range(1, CONV):
        after = after + pltpu.roll(ends, back, 1) * taps[:, CONV - 1 - back : CONV - back]
    table = jnp.where(lane < 3, total[:, :128], pltpu.roll(after, 3, 1))
    table = jnp.where(lane < 6, table, 0.0).T[:8, :]
    high = table.astype(BF16)
    low = (table - high.astype(F32)).astype(BF16)
    gap = [jnp.zeros((8, 64 - width), BF16)] if width < 64 else []
    out_ref[width:, :128] = jnp.concatenate([high, *gap, low, *gap], axis=1)
    out_ref[width:, 128:] = jnp.zeros((8, rows - 128), BF16)
    for copy in copies[3:]:
        copy.wait()


def fix_kernel(split, x_ref, rim_ref, taps_ref, fac_ref, inv_ref, idc_ref, old_ref, *refs):
    shares, (live_ref, xe_ref, *exact) = by_mask(refs[:2], split), refs[2:]
    rows, columns = x_ref.shape
    heads = fac_ref.shape[1] // 2
    width = shares[0].shape[0] - 8
    depth = rim_rows(columns, split, rim_ref.shape[1])
    base = rim_ref.shape[0] - depth

    def moved(lane, size, shift):
        block = rim_ref[base:, lane : lane + size].astype(F32)
        return (pltpu.roll(block, shift % depth, 0) if shift % depth else block)[:8]

    live = idc_ref[:8, :] == 0.0
    row, lane = iota((8, 128), 0), iota((width, 128), 1)
    firsts = []
    for index, share in enumerate(shares):
        own = share[width:, :128].astype(F32)
        after = jnp.zeros((8, 128), F32)
        for each in range(3):
            down, left = rim_place(columns, split, rim_ref.shape[1], each, index)
            after = jnp.where(row == each, moved(left, 128, each - down), after)
        total = own + jnp.where(live, after, 0.0)
        total = total + pltpu.roll(total, 64, 1)
        value = total / (1.0 + jnp.exp(-total))
        firsts.append(value[:, :width])
        if exact:
            value = jnp.concatenate([value, jnp.zeros((120, 128), F32)], axis=0).T[:width, :]
            first = jnp.where(lane < 3, value, share[:width, :128].astype(F32))
            exact[0][index * width : (index + 1) * width, :] = first.astype(BF16)
    near = jnp.concatenate(firsts[: split // 2], axis=1)
    far = jnp.concatenate(firsts[split // 2 :], axis=1)
    own = lax.axis_index("head") < split // 2
    b_edge, c_edge = jnp.where(own, near, far), jnp.where(own, far, near)
    b_edge = jnp.where((row < 3) & live, b_edge, 0.0)
    b_edge = jnp.concatenate([b_edge, jnp.zeros((120, DSTATE), F32)], axis=0).astype(BF16)
    old = old_ref[:EDGE, :].astype(F32)
    c_edge = jnp.where(row < 3, jnp.where(live, c_edge, 0.0), old[:8])
    c_edge = jnp.concatenate([c_edge, old[8:]], axis=0).astype(BF16)
    c_all = jnp.concatenate([c_edge, old_ref[EDGE:, :]], axis=0)
    live_ref[:, :DSTATE] = c_all
    ahead = (iota((rows, 128), 0) >= iota((rows, 128), 1)) & (iota((rows, 128), 1) < 3)
    live_ref[:, DSTATE:] = jnp.where(ahead, mm_t(c_all, b_edge), 0.0).astype(BF16)
    ids = jnp.concatenate([jnp.zeros((8, 128), F32), idc_ref[:EDGE, :]], axis=0)
    masks = []
    for back in range(1, CONV):
        same = pltpu.roll(ids, back, 0)[8:] == ids[8:]
        masks.append(jnp.concatenate([jnp.where(same, 1.0, 0.0)] * (WIDE // 128), axis=1))
    for low in range(0, columns, WIDE):
        cols = slice(low, low + WIDE)
        taps = 0.5 * taps_ref[:, cols].astype(F32)
        slot, left = low // rim_ref.shape[1], low % rim_ref.shape[1]
        above = moved(left, WIDE, 5 - 3 * slot)
        padded = jnp.concatenate([above, x_ref[:EDGE, cols].astype(F32)], axis=0)
        half = padded[8:] * taps[CONV - 1 : CONV, :]
        for back in range(1, CONV):
            piece = pltpu.roll(padded, back, 0)[8:] * masks[back - 1]
            half = half + piece * taps[CONV - 1 - back : CONV - back, :]
        value = half + half * jnp.tanh(half)
        spread = spread_matrix(2, heads, low, WIDE)
        edge = jnp.where(iota(value.shape, 0) < 3, value * mm(inv_ref[...], spread), 0.0)
        xe_ref[:, cols] = edge.astype(BF16)
        if exact:
            exact[1][:, cols] = (value * mm(fac_ref[:EDGE, :], spread)).astype(BF16)


def conv_kernel(low, x_ref, taps_ref, fac_ref, idc_ref, *refs):
    out_ref, ids_ref, mask_ref = refs[-3:]
    if len(refs) > 3:
        out_ref = refs[1]
        refs[2][...] = refs[0][...]
    rows = x_ref.shape[0]
    heads = fac_ref.shape[1] // 2
    ids_ref[:8, :] = jnp.zeros((8, 128), F32)
    ids_ref[8:, :] = idc_ref[...]
    for back in range(1, CONV):
        same = ids_ref[pl.ds(8 - back, rows), :] == idc_ref[...]
        mask_ref[back - 1] = jnp.where(same, 1.0, 0.0)
    for block in range(out_ref.shape[1] // WIDE):
        start = low + block * WIDE
        cols = slice(start, start + WIDE)
        spread = spread_matrix(2, heads, start, WIDE)
        taps = 0.5 * taps_ref[:, cols].astype(F32)
        factor = mm(fac_ref[...], spread)
        size = 128
        for row in range(0, rows, size):
            span = slice(row, row + size)
            here = x_ref[span, cols].astype(F32)
            if row == 0:
                above = jnp.zeros((8, WIDE), F32)
            else:
                above = x_ref[row - 8 : row, cols].astype(F32)
            padded = jnp.concatenate([above, here], axis=0)
            half = here * taps[CONV - 1 : CONV, :]
            for back in range(1, CONV):
                mask = jnp.concatenate([mask_ref[back - 1, span, :]] * (WIDE // 128), axis=1)
                piece = pltpu.roll(padded, back, 0)[8:] * mask
                half = half + piece * taps[CONV - 1 - back : CONV - back, :]
            value = half + half * jnp.tanh(half)
            out_ref[span, block * WIDE : (block + 1) * WIDE] = (value * factor[span]).astype(BF16)


def pick(refs, first=None):
    half = len(refs) // 2
    width = refs[0].shape[0] - 8
    near = jnp.concatenate([ref[:width, :] for ref in refs[:half]], axis=0).astype(F32)
    far = jnp.concatenate([ref[:width, :] for ref in refs[half:]], axis=0).astype(F32)
    if first is not None:
        edge = first[...].astype(F32)
        near = jnp.concatenate([edge[:DSTATE], near[:, 128:]], axis=1)
        far = jnp.concatenate([edge[DSTATE:], far[:, 128:]], axis=1)
    own = lax.axis_index("head") < half
    return jnp.where(own, near, far), jnp.where(own, far, near)


def ending(b_rows, idr_ref, j):
    span = slice(j * CHUNK, (j + 1) * CHUNK)
    end = idr_ref[:1, (j + 1) * CHUNK - 1 : (j + 1) * CHUNK]
    return jnp.where(idr_ref[:1, span] == end, b_rows[:, span], 0.0).astype(BF16)


def state_kernel(low, split, count, carries, *refs):
    xs_refs = refs[2 : 2 + count]
    rows_ref, idr_ref, *edges, end_ref = refs[2 + count :]
    if carries:
        x_ref, start_ref = edges
        edges = []
        end_ref[DSTATE:, :] = rim_block(x_ref, start_ref, by_mask(refs[:2], split), end_ref.shape[1])
    b_rows, _ = pick(by_mask(refs[:2], split), edges[0] if edges else None)
    pieces = [ending(b_rows, idr_ref, j) for j in range(2)]
    each = xs_refs[0].shape[1] // WIDE
    for block in range(each * count):
        xs_ref, part = xs_refs[block // each], slice(block % each * WIDE, (block % each + 1) * WIDE)
        here = slice(block * WIDE, (block + 1) * WIDE)
        cols = slice(low + block * WIDE, low + (block + 1) * WIDE)
        values = xs_ref[:CHUNK, part]
        if edges:
            values = jnp.concatenate([edges[1][:, cols], values[EDGE:]], axis=0)
        first = mm(pieces[0], values)
        second = mm(pieces[1], xs_ref[CHUNK:, part])
        first = first * rows_ref[0:1, cols] * rows_ref[3:4, cols]
        end = first + second * rows_ref[1:2, cols]
        end_ref[:DSTATE, here] = end.astype(end_ref.dtype)


def score_kernel(split, *refs):
    idc_ref, idr_ref, g_ref, live_ref, carried_ref, ending_ref = refs[2:]
    b_rows, c_rows = pick(by_mask(refs[:2], split))
    rim = (iota((1, b_rows.shape[1]), 1) < 3) & (idr_ref[:1, :] == 0.0)
    b_rows = jnp.where(rim, 0.0, b_rows)
    ending_ref[...] = ending(b_rows, idr_ref, 0)
    b_rows = b_rows.astype(BF16)
    c_cols = c_rows.T
    for j in range(2):
        span = slice(j * CHUNK, (j + 1) * CHUNK)
        ids = idc_ref[span, :]
        live_ref[span, :] = jnp.where(ids == 0.0, c_cols[span, :], 0.0).astype(BF16)
        scores = mm(c_cols[span, :].astype(BF16), b_rows[:, span])
        square = (CHUNK, CHUNK)
        wide = jnp.concatenate([ids] * (CHUNK // 128), axis=1)
        keep = (iota(square, 0) >= iota(square, 1)) & (wide == idr_ref[:1, span])
        g_ref[j] = jnp.where(keep, scores, 0.0).astype(BF16)
    before = idr_ref[:1, CHUNK - 1 : CHUNK]
    ids = idc_ref[CHUNK:, :]
    carried_ref[...] = jnp.where(ids == before, c_cols[CHUNK:, :], 0.0).astype(BF16)


def local_kernel(low, *refs):
    xs_refs = refs[:-8]
    g_ref, carried_ref, ending_ref, eps_ref, rows_ref, z_ref, y_ref, dec_ref = refs[-8:]
    heads = eps_ref.shape[1] // 2
    each = xs_refs[0].shape[1] // WIDE
    for block in range(each * len(xs_refs)):
        xs_ref, part = xs_refs[block // each], slice(block % each * WIDE, (block % each + 1) * WIDE)
        start = low + block * WIDE
        here = slice(block * WIDE, (block + 1) * WIDE)
        cols = slice(start, start + WIDE)
        spread = spread_matrix(2, heads, start, WIDE)
        values = xs_ref[:CHUNK, part]
        middle = mm(ending_ref[...], values) * rows_ref[0:1, cols]
        middle = (middle * rows_ref[1:2, cols]).astype(BF16)
        for j in range(2):
            span = slice(j * CHUNK, (j + 1) * CHUNK)
            if j == 0:
                y = mm(g_ref[0], values)
            else:
                y = mm(g_ref[1], xs_ref[span, part]) + mm(carried_ref[...], middle)
            half = 0.5 * z_ref[span, cols].astype(F32)
            gate = (half + half * jnp.tanh(half)) * mm(eps_ref[span, :], spread)
            y_ref[span, here] = y * gate
            decay = gate * rows_ref[j : j + 1, cols]
            dec_ref[span, here] = decay * rows_ref[2:3, cols] if j else decay


def final_kernel(low, state_ref, edge_ref, y_ref, dec_ref, live_ref, gain_ref, *refs):
    out_ref, buffer, sem = refs[-3:]
    square = (WIDE, WIDE)
    same = iota(square, 0) >> HDIM_BITS == iota(square, 1) >> HDIM_BITS
    mean_matrix = jnp.where(same, 1.0 / HDIM, 0.0).astype(BF16)
    empty = jnp.zeros((DSTATE - EDGE, WIDE), BF16)
    copies = []
    for block in range(y_ref.shape[1] // WIDE):
        here = slice(block * WIDE, (block + 1) * WIDE)
        cols = slice(low + block * WIDE, low + (block + 1) * WIDE)
        gain = gain_ref[:, cols].astype(F32)
        state = jnp.concatenate([state_ref[:DSTATE, here], edge_ref[:, cols], empty], axis=0)
        for j in range(2):
            span = slice(j * CHUNK, (j + 1) * CHUNK)
            mixed = y_ref[span, here] + mm(live_ref[span, :], state) * dec_ref[span, here]
            mean = mm((mixed * mixed).astype(BF16), mean_matrix)
            buffer[block, span, :] = (mixed * lax.rsqrt(mean + 1e-05) * gain).astype(BF16)
            copy = pltpu.make_async_copy(
                buffer.at[block, span], out_ref.at[span, cols], sem.at[block, j]
            )
            copy.start()
            copies.append(copy)
    for copy in copies:
        copy.wait()


def on_device(x_in, z_in, bc_in, dt, decay_scale, conv_x, conv_bc, norm_gain, doc_start):
    rows, columns = x_in.shape
    heads = dt.shape[1]
    bc_width = bc_in.shape[1]
    turns = lax.axis_size("ctx") // 8
    split = lax.axis_size("head")
    starts = doc_start.reshape(1, rows)
    spec = pl.BlockSpec(memory_space=pltpu.VMEM)
    hbm = pl.BlockSpec(memory_space=pltpu.HBM)
    shape = jax.ShapeDtypeStruct
    in_hbm = lambda value: pltpu.with_memory_space_constraint(value, pltpu.HBM)
    own, starts, steps, scale, taps = call(
        bc_kernel,
        [hbm] * 6,
        [
            shape((bc_width + 8, rows), BF16),
            shape((1, rows), jnp.int32),
            shape((heads, rows), F32),
            shape((1, heads), F32),
            shape((CONV, columns), BF16),
        ],
        [
            pltpu.VMEM((bc_width, rows), BF16),
            pltpu.VMEM((CONV, bc_width), BF16),
            pltpu.SemaphoreType.DMA((6,)),
        ],
        "bc",
    )(
        in_hbm(bc_in.T),
        in_hbm(conv_bc),
        in_hbm(starts),
        in_hbm(dt.T),
        in_hbm(decay_scale.reshape(1, heads)),
        in_hbm(conv_x),
    )
    far = crossed(own, "head", split // 2)
    fac, eps, inv, table, ids_col, ids_row, x_near = call(
        prep_kernel,
        [spec] * 3 + [hbm],
        [
            shape((rows, 2 * heads), BF16),
            shape((rows, 2 * heads), BF16),
            shape((EDGE, 2 * heads), BF16),
            shape((8, columns), F32),
            shape((rows, 128), F32),
            shape((8, rows), F32),
            shape((rows, columns), BF16),
        ],
        [pltpu.SemaphoreType.DMA],
        "prep",
    )(steps, scale, starts, in_hbm(x_in))
    units = columns // WIDE
    sizes = [units // 4] * 4
    sizes = [WIDE * size for size in sizes]
    places = [sum(sizes[:piece]) for piece in range(len(sizes))]
    values = []
    for piece, (place, width) in enumerate(zip(places, sizes)):
        kept = [own] if piece == 0 else []
        part, *kept = call(
            functools.partial(conv_kernel, place),
            [spec] * (4 + len(kept)),
            [shape((rows, width), BF16)] + [shape(own.shape, BF16)] * len(kept),
            [pltpu.VMEM((rows + 8, 128), F32), pltpu.VMEM((CONV - 1, rows, 128), F32)],
            f"conv{piece}",
        )(x_near, taps, fac, ids_col, *kept)
        values.append(part)
        if piece == 0:
            ours, mask = jnp.concatenate([*kept, far], axis=0), split // 4
    while mask > 1:
        ours = jnp.concatenate([ours, crossed(ours, "head", mask)], axis=0)
        mask //= 2
    shares = [ours, crossed(ours, "head", 1)]
    widths = [sum(sizes[piece] for piece in group) for group in GROUPS]
    lows = [places[group[0]] for group in GROUPS]
    state_type = BF16 if turns == 1 else F32
    gain = norm_gain.reshape(1, columns)
    extra = rim_rows(columns, split, widths[0])

    score_shapes = [
        shape((2, CHUNK, CHUNK), BF16),
        shape((rows, DSTATE), BF16),
        shape((CHUNK, DSTATE), BF16),
        shape((DSTATE, CHUNK), BF16),
    ]
    scores, old, carried, ended = call(
        functools.partial(score_kernel, split), [spec] * 4, score_shapes, (), "score"
    )(*shares, ids_col, ids_row)

    def fixed(rim):
        shapes = [shape((rows, 2 * DSTATE), BF16), shape((EDGE, columns), BF16)]
        if turns > 1:
            shapes += [shape((2 * DSTATE, 128), BF16), shape((EDGE, columns), BF16)]
        kernel = functools.partial(fix_kernel, split)
        return call(kernel, [spec] * 9, shapes, (), "fix")(
            x_near, rim, taps, fac, inv, ids_col, old, *shares
        )

    edges = []
    if turns > 1:
        kernel = functools.partial(tail_kernel, split)
        tail = call(kernel, [spec] * 4, shape((extra, widths[0]), BF16), (), "tail")
        live, edge, *edges = fixed(shifted(tail(x_near, starts, *shares), "ctx", 1))

    def relay(low, width, end):
        if turns == 1:
            return shifted(end, "ctx", 1)
        through = table[4:5, low : low + width]
        turn = lambda _, incoming: shifted(through * incoming + end, "ctx", 1)
        return lax.fori_loop(0, turns, turn, jnp.zeros_like(end)).astype(BF16)

    incoming = []
    for group, low, width in zip(GROUPS, lows, widths):
        pieces = [values[piece] for piece in group]
        carries = turns == 1 and low == 0
        others = [x_near, starts] if carries else edges
        end = call(
            functools.partial(state_kernel, low, split, len(pieces), carries),
            [spec] * (4 + len(pieces) + len(others)),
            shape((DSTATE + extra if carries else DSTATE, width), state_type),
            (),
            f"state{low}",
        )(*shares, *pieces, table, ids_row, *others)
        incoming.append(relay(low, width, end))
    if turns == 1:
        live, edge = fixed(incoming[0])
    out = None
    for group, (low, width) in enumerate(zip(lows, widths)):
        pieces = [values[piece] for piece in GROUPS[group]]
        mixed, decay = call(
            functools.partial(local_kernel, low),
            [spec] * (6 + len(pieces)),
            [shape((rows, width), F32)] * 2,
            (),
            f"local{low}",
        )(*pieces, scores, carried, ended, eps, table, z_in)
        blocks = width // WIDE
        args = [incoming[group], edge, mixed, decay, live, gain]
        in_specs = [spec] * 6
        if group > 0:
            args.append(out)
            in_specs.append(hbm)
        out = call(
            functools.partial(final_kernel, low),
            in_specs,
            shape((rows, columns), BF16),
            [pltpu.VMEM((blocks, rows, WIDE), BF16), pltpu.SemaphoreType.DMA((blocks, 2))],
            f"final{low}",
            hbm,
            {6: 0} if group > 0 else {},
        )(*args)
    return out


def solution(mesh):
    in_specs = (
        P("ctx", "head"),
        P("ctx", "head"),
        P("ctx", "head"),
        P("ctx", "head"),
        P("head"),
        P(None, "head"),
        P(None, "head"),
        P("head"),
        P("ctx"),
    )
    out_specs = P("ctx", "head")
    return jax.shard_map(
        on_device, mesh=mesh, in_specs=in_specs, out_specs=out_specs, check_vma=False
    )
```

```python
import functools

import jax
import jax.numpy as jnp
from jax import lax
from jax.experimental import pallas as pl
from jax.experimental.pallas import tpu as pltpu
from jax.sharding import PartitionSpec as P

HDIM = 64
HDIM_BITS = 6
DSTATE = 128
CONV = 4
CHUNK = 256
WIDE = 256
GROUPS = ((0, 1), (2,), (3,))
EDGE = 16
F32 = jnp.float32
BF16 = jnp.bfloat16


def shifted(value, axis, steps):
    count = lax.axis_size(axis)
    pairs = [(source, (source + steps) % count) for source in range(count)]
    return lax.ppermute(value, axis, pairs)


def crossed(value, axis, mask):
    count = lax.axis_size(axis)
    return lax.ppermute(value, axis, [(source, source ^ mask) for source in range(count)])


def iota(shape, dim):
    return lax.broadcasted_iota(jnp.int32, shape, dim)


def mm(a, b):
    return jnp.dot(a, b, preferred_element_type=F32)


def mm_t(a, b):
    return lax.dot_general(a, b, (((1,), (1,)), ((), ())), preferred_element_type=F32)


def parts(value, count, axis=1):
    pieces = []
    for _ in range(count):
        piece = value.astype(BF16)
        pieces.append(piece)
        value = value - piece.astype(F32)
    return jnp.concatenate(pieces, axis=axis)


def spread_matrix(copies, heads, low, width):
    shape = (copies * heads, width)
    head = iota(shape, 0) & (heads - 1)
    return jnp.where(head == (iota(shape, 1) + low) >> HDIM_BITS, 1.0, 0.0).astype(BF16)


def call(kernel, in_specs, outs, scratch, name, out_spec=None, alias=None, limit=12):
    spec = out_spec or pl.BlockSpec(memory_space=pltpu.VMEM)
    return pl.pallas_call(
        kernel,
        out_shape=outs,
        in_specs=in_specs,
        out_specs=[spec] * len(outs) if isinstance(outs, list) else spec,
        scratch_shapes=list(scratch),
        input_output_aliases=alias or {},
        compiler_params=pltpu.CompilerParams(vmem_limit_bytes=limit << 20),
        name=name,
    )


def order_of(split):
    masks = [0]
    mask = split // 2
    while mask:
        masks += [held | mask for held in masks]
        mask //= 2
    return masks


def by_mask(refs, split):
    size = refs[0].shape[0] * 2 // split
    views = []
    for place in range(split):
        ref, row = refs[place * 2 // split], place % (split // 2) * size
        views.append(ref.at[row : row + size, :])
    order = order_of(split)
    return [views[order.index(mask)] for mask in range(split)]


def rim_rows(columns, split, width):
    return -(-3 * (columns + 128 * split) // width // 8) * 8


def rim_place(columns, split, width, row, index):
    lane = row * 128 * split + index * 128
    return 3 * columns // width + lane // width, lane % width


def rim_block(x_ref, start_ref, shares, width):
    rows, columns = x_ref.shape
    split = len(shares)
    total = rim_rows(columns, split, width)
    starts = start_ref[:, rows - 128 :].astype(F32)
    last = starts[:, 127:128]
    before = jnp.maximum(last, starts[:, 126:127])
    row = iota((8, 128), 0)
    kept = jnp.where(row == 5, 1.0 - before, jnp.where(row == 6, 1.0 - last, 1.0))
    kept = jnp.where(row >= 5, kept, 0.0)
    kept = jnp.concatenate([kept] * (width // 128), axis=1)

    def placed(piece, shift, left=0):
        right = width - left - piece.shape[1]
        sides = [jnp.zeros((8, left), F32)] if left else []
        sides += [piece] + ([jnp.zeros((8, right), F32)] if right else [])
        piece = jnp.concatenate(sides, axis=1)
        if total > 8:
            piece = jnp.concatenate([piece, jnp.zeros((total - 8, width), F32)], axis=0)
        return pltpu.roll(piece, shift % total, 0) if shift % total else piece

    block = jnp.zeros((total, width), F32)
    for slot, low in enumerate(range(0, columns, width)):
        piece = x_ref[rows - 8 :, low : low + width].astype(F32) * kept
        block = block + placed(piece, 3 * slot - 5)
    count = min(width // 128, split)
    for first in range(0, split, count):
        piece = [share[share.shape[0] - 8 :, :128] for share in shares[first : first + count]]
        piece = jnp.concatenate(piece, axis=1).astype(F32)
        for each in range(3):
            own = jnp.where(iota(piece.shape, 0) == 3 + each, piece, 0.0)
            down, left = rim_place(columns, split, width, each, first)
            block = block + placed(own, down - 3 - each, left)
    return block.astype(BF16)


def tail_kernel(split, x_ref, start_ref, *refs):
    shares = by_mask(refs[:2], split)
    refs[-1][...] = rim_block(x_ref, start_ref, shares, refs[-1].shape[1])


def prep_kernel(dt_ref, scale_ref, start_ref, x_hbm, *refs):
    fac_ref, eps_ref, inv_ref, rows_ref, idc_ref, idr_ref, x_ref, sem = refs
    copy = pltpu.make_async_copy(x_hbm, x_ref, sem)
    copy.start()
    heads = dt_ref.shape[0]
    square = (CHUNK, CHUNK)
    lower = jnp.where(iota(square, 0) >= iota(square, 1), 1.0, 0.0).astype(BF16)
    upper = jnp.where(iota(square, 0) <= iota(square, 1), 1.0, 0.0).astype(BF16)
    mids = []
    offset = jnp.zeros((8, 1), F32)
    for j in range(2):
        span = slice(j * CHUNK, (j + 1) * CHUNK)
        sums = mm_t(lower, parts(dt_ref[:, span], 3, 0))
        sums = sums[:, :heads] + sums[:, heads : 2 * heads] + sums[:, 2 * heads :]
        log_decay = -(sums * scale_ref[...])
        mid = 0.5 * log_decay[CHUNK - 1 : CHUNK, :]
        mids.append(mid)
        fac_ref[span, :] = parts(jnp.exp(mid - log_decay), 2)
        eps_ref[span, :] = parts(jnp.exp(log_decay - mid), 2)
        if j == 0:
            inv_ref[...] = parts(jnp.exp(-log_decay[:EDGE, :]), 2)
        starts = start_ref[:, span].astype(F32).astype(BF16)
        by_row = mm(jnp.broadcast_to(starts, (8, CHUNK)), upper) + offset
        by_col = mm_t(lower, jnp.broadcast_to(starts, (128, CHUNK)))
        idr_ref[:, span] = by_row
        idc_ref[span, :] = by_col + offset[:1, :]
        offset = by_row[:, CHUNK - 1 : CHUNK]
    middle = idr_ref[:1, CHUNK - 1 : CHUNK]
    final = idr_ref[:1, 2 * CHUNK - 1 : 2 * CHUNK]
    keep = jnp.where(middle == final, 1.0, 0.0)
    whole = jnp.where(final == 0.0, 1.0, 0.0)
    first, second = mids
    table = jnp.concatenate(
        [
            jnp.exp(first),
            jnp.exp(second),
            jnp.exp(2.0 * first),
            jnp.exp(2.0 * second) * keep,
            jnp.exp(2.0 * (first + second)) * whole,
            first,
            second,
            second,
        ],
        axis=0,
    )
    rows_ref[...] = mm(parts(table, 3), spread_matrix(3, heads, 0, rows_ref.shape[1]))
    copy.wait()


def bc_kernel(*refs):
    sources, (out_ref, *copied), (bc_ref, taps_ref, sems) = refs[:6], refs[6:11], refs[11:]
    width, rows = bc_ref.shape
    start_ref = copied[0]
    copies = [
        pltpu.make_async_copy(source, target, sems.at[index])
        for index, (source, target) in enumerate(zip(sources, [bc_ref, taps_ref, *copied]))
    ]
    for copy in copies:
        copy.start()
    copies[1].wait()
    copies[2].wait()
    starts = jnp.broadcast_to(start_ref[...].astype(F32), (8, rows))
    open_ = jnp.concatenate([jnp.ones((8, 128), F32), 1.0 - starts], axis=1)
    taps = jnp.concatenate([taps_ref[...].astype(F32)] * 2, axis=0).T
    copies[0].wait()
    values = jnp.concatenate([jnp.zeros((width, 128), F32), bc_ref[...].astype(F32)], axis=1)
    total = values[:, 128:] * taps[:, CONV - 1 : CONV]
    kept = open_
    for back in range(1, CONV):
        if back > 1:
            kept = kept * pltpu.roll(open_, back - 1, 1)
        piece = pltpu.roll(values, back, 1)[:, 128:] * kept[:1, 128:]
        total = total + piece * taps[:, CONV - 1 - back : CONV - back]
    half = 0.5 * total
    out_ref[:width, :] = (half + half * jnp.tanh(half)).astype(BF16)
    lane = iota((1, 128), 1)
    last = open_[:1, rows:]
    near, far = last[:, 127:128], last[:, 126:127]
    kept = jnp.where(lane == 125, near * far, jnp.where(lane == 126, near, 1.0))
    ends = jnp.where(lane >= 125, kept, 0.0) * values[:, rows:]
    after = jnp.zeros((width, 128), F32)
    for back in range(1, CONV):
        after = after + pltpu.roll(ends, back, 1) * taps[:, CONV - 1 - back : CONV - back]
    table = jnp.where(lane < 3, total[:, :128], pltpu.roll(after, 3, 1))
    table = jnp.where(lane < 6, table, 0.0).T[:8, :]
    high = table.astype(BF16)
    low = (table - high.astype(F32)).astype(BF16)
    gap = [jnp.zeros((8, 64 - width), BF16)] if width < 64 else []
    out_ref[width:, :128] = jnp.concatenate([high, *gap, low, *gap], axis=1)
    out_ref[width:, 128:] = jnp.zeros((8, rows - 128), BF16)
    for copy in copies[3:]:
        copy.wait()


def fix_kernel(split, x_ref, rim_ref, taps_ref, fac_ref, inv_ref, idc_ref, old_ref, *refs):
    shares, (live_ref, xe_ref, *exact) = by_mask(refs[:2], split), refs[2:]
    rows, columns = x_ref.shape
    heads = fac_ref.shape[1] // 2
    width = shares[0].shape[0] - 8
    depth = rim_rows(columns, split, rim_ref.shape[1])
    base = rim_ref.shape[0] - depth

    def moved(lane, size, shift):
        block = rim_ref[base:, lane : lane + size].astype(F32)
        return (pltpu.roll(block, shift % depth, 0) if shift % depth else block)[:8]

    live = idc_ref[:8, :] == 0.0
    row, lane = iota((8, 128), 0), iota((width, 128), 1)
    firsts = []
    for index, share in enumerate(shares):
        own = share[width:, :128].astype(F32)
        after = jnp.zeros((8, 128), F32)
        for each in range(3):
            down, left = rim_place(columns, split, rim_ref.shape[1], each, index)
            after = jnp.where(row == each, moved(left, 128, each - down), after)
        total = own + jnp.where(live, after, 0.0)
        total = total + pltpu.roll(total, 64, 1)
        value = total / (1.0 + jnp.exp(-total))
        firsts.append(value[:, :width])
        if exact:
            value = jnp.concatenate([value, jnp.zeros((120, 128), F32)], axis=0).T[:width, :]
            first = jnp.where(lane < 3, value, share[:width, :128].astype(F32))
            exact[0][index * width : (index + 1) * width, :] = first.astype(BF16)
    near = jnp.concatenate(firsts[: split // 2], axis=1)
    far = jnp.concatenate(firsts[split // 2 :], axis=1)
    own = lax.axis_index("head") < split // 2
    b_edge, c_edge = jnp.where(own, near, far), jnp.where(own, far, near)
    b_edge = jnp.where((row < 3) & live, b_edge, 0.0)
    b_edge = jnp.concatenate([b_edge, jnp.zeros((120, DSTATE), F32)], axis=0).astype(BF16)
    old = old_ref[:EDGE, :].astype(F32)
    c_edge = jnp.where(row < 3, jnp.where(live, c_edge, 0.0), old[:8])
    c_edge = jnp.concatenate([c_edge, old[8:]], axis=0).astype(BF16)
    c_all = jnp.concatenate([c_edge, old_ref[EDGE:, :]], axis=0)
    live_ref[:, :DSTATE] = c_all
    ahead = (iota((rows, 128), 0) >= iota((rows, 128), 1)) & (iota((rows, 128), 1) < 3)
    live_ref[:, DSTATE:] = jnp.where(ahead, mm_t(c_all, b_edge), 0.0).astype(BF16)
    ids = jnp.concatenate([jnp.zeros((8, 128), F32), idc_ref[:EDGE, :]], axis=0)
    masks = []
    for back in range(1, CONV):
        same = pltpu.roll(ids, back, 0)[8:] == ids[8:]
        masks.append(jnp.concatenate([jnp.where(same, 1.0, 0.0)] * (WIDE // 128), axis=1))
    for low in range(0, columns, WIDE):
        cols = slice(low, low + WIDE)
        taps = 0.5 * taps_ref[:, cols].astype(F32)
        slot, left = low // rim_ref.shape[1], low % rim_ref.shape[1]
        above = moved(left, WIDE, 5 - 3 * slot)
        padded = jnp.concatenate([above, x_ref[:EDGE, cols].astype(F32)], axis=0)
        half = padded[8:] * taps[CONV - 1 : CONV, :]
        for back in range(1, CONV):
            piece = pltpu.roll(padded, back, 0)[8:] * masks[back - 1]
            half = half + piece * taps[CONV - 1 - back : CONV - back, :]
        value = half + half * jnp.tanh(half)
        spread = spread_matrix(2, heads, low, WIDE)
        edge = jnp.where(iota(value.shape, 0) < 3, value * mm(inv_ref[...], spread), 0.0)
        xe_ref[:, cols] = edge.astype(BF16)
        if exact:
            exact[1][:, cols] = (value * mm(fac_ref[:EDGE, :], spread)).astype(BF16)


def conv_kernel(low, x_ref, taps_ref, fac_ref, idc_ref, *refs):
    out_ref, ids_ref, mask_ref = refs[-3:]
    if len(refs) > 3:
        out_ref = refs[1]
        refs[2][...] = refs[0][...]
    rows = x_ref.shape[0]
    heads = fac_ref.shape[1] // 2
    ids_ref[:8, :] = jnp.zeros((8, 128), F32)
    ids_ref[8:, :] = idc_ref[...]
    for back in range(1, CONV):
        same = ids_ref[pl.ds(8 - back, rows), :] == idc_ref[...]
        mask_ref[back - 1] = jnp.where(same, 1.0, 0.0)
    for block in range(out_ref.shape[1] // WIDE):
        start = low + block * WIDE
        cols = slice(start, start + WIDE)
        spread = spread_matrix(2, heads, start, WIDE)
        taps = 0.5 * taps_ref[:, cols].astype(F32)
        factor = mm(fac_ref[...], spread)
        size = 128
        for row in range(0, rows, size):
            span = slice(row, row + size)
            here = x_ref[span, cols].astype(F32)
            if row == 0:
                above = jnp.zeros((8, WIDE), F32)
            else:
                above = x_ref[row - 8 : row, cols].astype(F32)
            padded = jnp.concatenate([above, here], axis=0)
            half = here * taps[CONV - 1 : CONV, :]
            for back in range(1, CONV):
                mask = jnp.concatenate([mask_ref[back - 1, span, :]] * (WIDE // 128), axis=1)
                piece = pltpu.roll(padded, back, 0)[8:] * mask
                half = half + piece * taps[CONV - 1 - back : CONV - back, :]
            value = half + half * jnp.tanh(half)
            out_ref[span, block * WIDE : (block + 1) * WIDE] = (value * factor[span]).astype(BF16)


def pick(refs, first=None):
    half = len(refs) // 2
    width = refs[0].shape[0] - 8
    near = jnp.concatenate([ref[:width, :] for ref in refs[:half]], axis=0).astype(F32)
    far = jnp.concatenate([ref[:width, :] for ref in refs[half:]], axis=0).astype(F32)
    if first is not None:
        edge = first[...].astype(F32)
        near = jnp.concatenate([edge[:DSTATE], near[:, 128:]], axis=1)
        far = jnp.concatenate([edge[DSTATE:], far[:, 128:]], axis=1)
    own = lax.axis_index("head") < half
    return jnp.where(own, near, far), jnp.where(own, far, near)


def ending(b_rows, idr_ref, j):
    span = slice(j * CHUNK, (j + 1) * CHUNK)
    end = idr_ref[:1, (j + 1) * CHUNK - 1 : (j + 1) * CHUNK]
    return jnp.where(idr_ref[:1, span] == end, b_rows[:, span], 0.0).astype(BF16)


def state_kernel(low, split, count, carries, *refs):
    xs_refs = refs[2 : 2 + count]
    rows_ref, idr_ref, *edges, end_ref = refs[2 + count :]
    if carries:
        x_ref, start_ref = edges
        edges = []
        end_ref[DSTATE:, :] = rim_block(x_ref, start_ref, by_mask(refs[:2], split), end_ref.shape[1])
    b_rows, _ = pick(by_mask(refs[:2], split), edges[0] if edges else None)
    pieces = [ending(b_rows, idr_ref, j) for j in range(2)]
    each = xs_refs[0].shape[1] // WIDE
    for block in range(each * count):
        xs_ref, part = xs_refs[block // each], slice(block % each * WIDE, (block % each + 1) * WIDE)
        here = slice(block * WIDE, (block + 1) * WIDE)
        cols = slice(low + block * WIDE, low + (block + 1) * WIDE)
        values = xs_ref[:CHUNK, part]
        if edges:
            values = jnp.concatenate([edges[1][:, cols], values[EDGE:]], axis=0)
        first = mm(pieces[0], values)
        second = mm(pieces[1], xs_ref[CHUNK:, part])
        first = first * rows_ref[0:1, cols] * rows_ref[3:4, cols]
        end = first + second * rows_ref[1:2, cols]
        end_ref[:DSTATE, here] = end.astype(end_ref.dtype)


def score_kernel(split, *refs):
    idc_ref, idr_ref, g_ref, live_ref, carried_ref, ending_ref = refs[2:]
    b_rows, c_rows = pick(by_mask(refs[:2], split))
    rim = (iota((1, b_rows.shape[1]), 1) < 3) & (idr_ref[:1, :] == 0.0)
    b_rows = jnp.where(rim, 0.0, b_rows)
    ending_ref[...] = ending(b_rows, idr_ref, 0)
    b_rows = b_rows.astype(BF16)
    c_cols = c_rows.T
    for j in range(2):
        span = slice(j * CHUNK, (j + 1) * CHUNK)
        ids = idc_ref[span, :]
        live_ref[span, :] = jnp.where(ids == 0.0, c_cols[span, :], 0.0).astype(BF16)
        scores = mm(c_cols[span, :].astype(BF16), b_rows[:, span])
        square = (CHUNK, CHUNK)
        wide = jnp.concatenate([ids] * (CHUNK // 128), axis=1)
        keep = (iota(square, 0) >= iota(square, 1)) & (wide == idr_ref[:1, span])
        g_ref[j] = jnp.where(keep, scores, 0.0).astype(BF16)
    before = idr_ref[:1, CHUNK - 1 : CHUNK]
    ids = idc_ref[CHUNK:, :]
    carried_ref[...] = jnp.where(ids == before, c_cols[CHUNK:, :], 0.0).astype(BF16)


def local_kernel(low, *refs):
    xs_refs = refs[:-8]
    g_ref, carried_ref, ending_ref, eps_ref, rows_ref, z_ref, y_ref, dec_ref = refs[-8:]
    heads = eps_ref.shape[1] // 2
    each = xs_refs[0].shape[1] // WIDE
    for block in range(each * len(xs_refs)):
        xs_ref, part = xs_refs[block // each], slice(block % each * WIDE, (block % each + 1) * WIDE)
        start = low + block * WIDE
        here = slice(block * WIDE, (block + 1) * WIDE)
        cols = slice(start, start + WIDE)
        spread = spread_matrix(2, heads, start, WIDE)
        values = xs_ref[:CHUNK, part]
        middle = mm(ending_ref[...], values) * rows_ref[0:1, cols]
        middle = (middle * rows_ref[1:2, cols]).astype(BF16)
        for j in range(2):
            span = slice(j * CHUNK, (j + 1) * CHUNK)
            if j == 0:
                y = mm(g_ref[0], values)
            else:
                y = mm(g_ref[1], xs_ref[span, part]) + mm(carried_ref[...], middle)
            half = 0.5 * z_ref[span, cols].astype(F32)
            gate = (half + half * jnp.tanh(half)) * mm(eps_ref[span, :], spread)
            y_ref[span, here] = y * gate
            decay = gate * rows_ref[j : j + 1, cols]
            dec_ref[span, here] = decay * rows_ref[2:3, cols] if j else decay


def final_kernel(low, state_ref, edge_ref, y_ref, dec_ref, live_ref, gain_ref, *refs):
    out_ref, buffer, sem = refs[-3:]
    square = (WIDE, WIDE)
    same = iota(square, 0) >> HDIM_BITS == iota(square, 1) >> HDIM_BITS
    mean_matrix = jnp.where(same, 1.0 / HDIM, 0.0).astype(BF16)
    empty = jnp.zeros((DSTATE - EDGE, WIDE), BF16)
    copies = []
    for block in range(y_ref.shape[1] // WIDE):
        here = slice(block * WIDE, (block + 1) * WIDE)
        cols = slice(low + block * WIDE, low + (block + 1) * WIDE)
        gain = gain_ref[:, cols].astype(F32)
        state = jnp.concatenate([state_ref[:DSTATE, here], edge_ref[:, cols], empty], axis=0)
        for j in range(2):
            span = slice(j * CHUNK, (j + 1) * CHUNK)
            mixed = y_ref[span, here] + mm(live_ref[span, :], state) * dec_ref[span, here]
            mean = mm((mixed * mixed).astype(BF16), mean_matrix)
            buffer[block, span, :] = (mixed * lax.rsqrt(mean + 1e-05) * gain).astype(BF16)
            copy = pltpu.make_async_copy(
                buffer.at[block, span], out_ref.at[span, cols], sem.at[block, j]
            )
            copy.start()
            copies.append(copy)
    for copy in copies:
        copy.wait()


def on_device(x_in, z_in, bc_in, dt, decay_scale, conv_x, conv_bc, norm_gain, doc_start):
    rows, columns = x_in.shape
    heads = dt.shape[1]
    bc_width = bc_in.shape[1]
    turns = lax.axis_size("ctx") // 8
    split = lax.axis_size("head")
    starts = doc_start.reshape(1, rows)
    spec = pl.BlockSpec(memory_space=pltpu.VMEM)
    hbm = pl.BlockSpec(memory_space=pltpu.HBM)
    shape = jax.ShapeDtypeStruct
    in_hbm = lambda value: pltpu.with_memory_space_constraint(value, pltpu.HBM)
    own, starts, steps, scale, taps = call(
        bc_kernel,
        [hbm] * 6,
        [
            shape((bc_width + 8, rows), BF16),
            shape((1, rows), jnp.int32),
            shape((heads, rows), F32),
            shape((1, heads), F32),
            shape((CONV, columns), BF16),
        ],
        [
            pltpu.VMEM((bc_width, rows), BF16),
            pltpu.VMEM((CONV, bc_width), BF16),
            pltpu.SemaphoreType.DMA((6,)),
        ],
        "bc",
    )(
        in_hbm(bc_in.T),
        in_hbm(conv_bc),
        in_hbm(starts),
        in_hbm(dt.T),
        in_hbm(decay_scale.reshape(1, heads)),
        in_hbm(conv_x),
    )
    far = crossed(own, "head", split // 2)
    fac, eps, inv, table, ids_col, ids_row, x_near = call(
        prep_kernel,
        [spec] * 3 + [hbm],
        [
            shape((rows, 2 * heads), BF16),
            shape((rows, 2 * heads), BF16),
            shape((EDGE, 2 * heads), BF16),
            shape((8, columns), F32),
            shape((rows, 128), F32),
            shape((8, rows), F32),
            shape((rows, columns), BF16),
        ],
        [pltpu.SemaphoreType.DMA],
        "prep",
    )(steps, scale, starts, in_hbm(x_in))
    units = columns // WIDE
    sizes = [units // 4] * 4
    sizes = [WIDE * size for size in sizes]
    places = [sum(sizes[:piece]) for piece in range(len(sizes))]
    values = []
    for piece, (place, width) in enumerate(zip(places, sizes)):
        kept = [own] if piece == 0 else []
        part, *kept = call(
            functools.partial(conv_kernel, place),
            [spec] * (4 + len(kept)),
            [shape((rows, width), BF16)] + [shape(own.shape, BF16)] * len(kept),
            [pltpu.VMEM((rows + 8, 128), F32), pltpu.VMEM((CONV - 1, rows, 128), F32)],
            f"conv{piece}",
        )(x_near, taps, fac, ids_col, *kept)
        values.append(part)
        if piece == 0:
            ours, mask = jnp.concatenate([*kept, far], axis=0), split // 4
    while mask > 1:
        ours = jnp.concatenate([ours, crossed(ours, "head", mask)], axis=0)
        mask //= 2
    shares = [ours, crossed(ours, "head", 1)]
    widths = [sum(sizes[piece] for piece in group) for group in GROUPS]
    lows = [places[group[0]] for group in GROUPS]
    state_type = BF16 if turns == 1 else F32
    gain = norm_gain.reshape(1, columns)
    extra = rim_rows(columns, split, widths[0])

    score_shapes = [
        shape((2, CHUNK, CHUNK), BF16),
        shape((rows, DSTATE), BF16),
        shape((CHUNK, DSTATE), BF16),
        shape((DSTATE, CHUNK), BF16),
    ]
    scores, old, carried, ended = call(
        functools.partial(score_kernel, split), [spec] * 4, score_shapes, (), "score"
    )(*shares, ids_col, ids_row)

    def fixed(rim):
        shapes = [shape((rows, 2 * DSTATE), BF16), shape((EDGE, columns), BF16)]
        if turns > 1:
            shapes += [shape((2 * DSTATE, 128), BF16), shape((EDGE, columns), BF16)]
        kernel = functools.partial(fix_kernel, split)
        return call(kernel, [spec] * 9, shapes, (), "fix")(
            x_near, rim, taps, fac, inv, ids_col, old, *shares
        )

    edges = []
    if turns > 1:
        kernel = functools.partial(tail_kernel, split)
        tail = call(kernel, [spec] * 4, shape((extra, widths[0]), BF16), (), "tail")
        live, edge, *edges = fixed(shifted(tail(x_near, starts, *shares), "ctx", 1))

    def relay(low, width, end):
        if turns == 1:
            return shifted(end, "ctx", 1)
        through = table[4:5, low : low + width]
        turn = lambda _, incoming: shifted(through * incoming + end, "ctx", 1)
        return lax.fori_loop(0, turns, turn, jnp.zeros_like(end)).astype(BF16)

    incoming = []
    for group, low, width in zip(GROUPS, lows, widths):
        pieces = [values[piece] for piece in group]
        carries = turns == 1 and low == 0
        others = [x_near, starts] if carries else edges
        end = call(
            functools.partial(state_kernel, low, split, len(pieces), carries),
            [spec] * (4 + len(pieces) + len(others)),
            shape((DSTATE + extra if carries else DSTATE, width), state_type),
            (),
            f"state{low}",
        )(*shares, *pieces, table, ids_row, *others)
        incoming.append(relay(low, width, end))
    if turns == 1:
        live, edge = fixed(incoming[0])
    out = None
    for group, (low, width) in enumerate(zip(lows, widths)):
        pieces = [values[piece] for piece in GROUPS[group]]
        mixed, decay = call(
            functools.partial(local_kernel, low),
            [spec] * (6 + len(pieces)),
            [shape((rows, width), F32)] * 2,
            (),
            f"local{low}",
        )(*pieces, scores, carried, ended, eps, table, z_in)
        blocks = width // WIDE
        args = [incoming[group], edge, mixed, decay, live, gain]
        in_specs = [spec] * 6
        if group > 0:
            args.append(out)
            in_specs.append(hbm)
        out = call(
            functools.partial(final_kernel, low),
            in_specs,
            shape((rows, columns), BF16),
            [pltpu.VMEM((blocks, rows, WIDE), BF16), pltpu.SemaphoreType.DMA((blocks, 2))],
            f"final{low}",
            hbm,
            {6: 0} if group > 0 else {},
        )(*args)
    return out


def solution(mesh):
    in_specs = (
        P("ctx", "head"),
        P("ctx", "head"),
        P("ctx", "head"),
        P("ctx", "head"),
        P("head"),
        P(None, "head"),
        P(None, "head"),
        P("head"),
        P("ctx"),
    )
    out_specs = P("ctx", "head")
    return jax.shard_map(
        on_device, mesh=mesh, in_specs=in_specs, out_specs=out_specs, check_vma=False
    )
```
